32 devices in a mesh: dp: 8 (over z, y), mp: 4 (over x, core).
Axes of the slice: x: 2, y: 2, z: 4, core: 2. Of those that a mesh axis runs over, the one named last changes fastest.
Arguments:
- doc_tokens: bfloat16 [16, 1024, 768], P('dp', 'mp'), may hold values from -6 to 6
- query_tokens: bfloat16 [64, 32, 768], P(('dp', 'mp')), may hold values from -6 to 6
- doc_segments: int32 [16, 1024], P('dp'), may hold values from 0 to 3, never falling along the last dimension, each value on 1 to 512 neighbouring positions
- query_keep: int32 [64, 32], replicated, may hold values from 0 to 1, as said below
- retrieved: int32 [64, 32, 64], P(None, None, 'dp'), may hold values 0 or 1
- positives: int32 [64], replicated, may hold values from 0 to 63
- attn_gain: bfloat16 [768], replicated, may hold values from 0.5 to 1.5
- query_weight: bfloat16 [768, 768], P(None, 'mp'), may hold values from -0.02734375 to 0.02734375
- key_weight: bfloat16 [768, 768], P(None, 'mp'), may hold values from -0.21875 to 0.21875
- value_weight: bfloat16 [768, 768], P(None, 'mp'), may hold values from -0.21875 to 0.21875
- output_weight: bfloat16 [768, 768], P('mp'), may hold values from -0.625 to 0.625
- position_bias: bfloat16 [32, 12], P(None, 'mp'), may hold values from -4 to 4
- ffn_gain: bfloat16 [768], replicated, may hold values from 0.5 to 1.5
- gate_weight: bfloat16 [768, 2048], P(None, 'mp'), may hold values from -0.21875 to 0.21875
- up_weight: bfloat16 [768, 2048], P(None, 'mp'), may hold values from -0.21875 to 0.21875
- down_weight: bfloat16 [2048, 768], P('mp'), may hold values from -0.125 to 0.125
- final_gain: bfloat16 [768], replicated, may hold values from 0.5 to 1.5
- proj_weight: bfloat16 [768, 128], replicated, may hold values from -0.21875 to 0.21875
Outputs:
- loss_value: float32 [], replicated
- found_share: float32 [], replicated
- doc_grad: float32 [16, 1024, 768], P('dp', 'mp')
- query_grad: float32 [64, 32, 768], P(('dp', 'mp'))
- attn_gain_grad: float32 [768], replicated
- query_weight_grad: float32 [768, 768], P(None, 'mp')
- key_weight_grad: float32 [768, 768], P(None, 'mp')
- value_weight_grad: float32 [768, 768], P(None, 'mp')
- output_weight_grad: float32 [768, 768], P('mp')
- position_bias_grad: float32 [32, 12], P(None, 'mp')
- ffn_gain_grad: float32 [768], replicated
- switch_matrix_derivative: float32 [768, 2048], P(None, 'mp')
- up_weight_grad: float32 [768, 2048], P(None, 'mp')
- down_weight_grad: float32 [2048, 768], P('mp')
- final_gain_grad: float32 [768], replicated
- proj_weight_grad: float32 [768, 128], replicated
The draws below stay inside these ranges and needn't reach their ends.
Inputs may be any that keep to these rules, and one draw needn't show every extreme that they name: `doc_segments`: each row holds 4 documents, numbered in order and never falling. `query_keep`: each query keeps a prefix of its tokens, at least 8 of them.
All inputs are finite; a program needn't handle non-finite values. No bound on the sum of `retrieved` on one device may be relied on, other than what follows from the above.
Results may differ from the reference program's by a relative error of at most 0.035.
Values may be sent and summed in bfloat16 or wider, within the bound.
No kernel may reach another device: no remote copies, remote signals or barrier semaphores. Data moves between devices by JAX's collectives and lax.ppermute only.
A program may use at most 192 MiB of HBM per device.

```python
import math
from functools import partial
import jax
import jax.numpy as jnp
import numpy as np
from jax import lax

D = 768
HEADS = 12
HEAD = 64
FF = 2048
BUCKETS = 32
EMB = 128
LEN = 1024
DOCS_ROW = 4
QLEN = 32
DOC_ROWS = 16
QUERIES = 64
DOCS = 64


def draw_query_keep(key, part):
    lengths = jax.random.randint(key, (QUERIES, 1), QLEN // 4, QLEN + 1)
    return (jnp.arange(QLEN)[None, :] < lengths).astype(jnp.int32)


def set_ends(drawn, rng, smallest, top_value):
    place = [jax.random.randint(jax.random.fold_in(rng, axis), (), 0, length) for axis, length in enumerate(drawn.shape)]
    main_axis = drawn.shape.index(max(drawn.shape))
    beside = place[:main_axis] + [(place[main_axis] + 1) % drawn.shape[main_axis]] + place[main_axis + 1:]
    return drawn.at[tuple(place)].set(smallest).at[tuple(beside)].set(top_value)


def levels(key, shape, pieces, low, top_value):
    def one(position, blocks):
        steps = jax.random.uniform(jax.random.fold_in(jax.random.fold_in(key, 6), position), (blocks,), jnp.float32, low / len(pieces), top_value / len(pieces))
        return jnp.repeat(jnp.exp(steps), shape[position] // blocks).reshape((-1,) + (1,) * (len(shape) - position - 1))

    level = one(*pieces[0])
    for cut in pieces[1:]:
        level = level * one(*cut)
    return level


def length_profile(count, total, reach, lean):
    loads = [(1 << 20) // math.isqrt(rank ** lean) + 1 for rank in range(2, count + 1)]
    surplus, given = total - reach - (count - 1), [1] * (count - 1)
    while surplus > 0:
        candidates = [i for i in range(count - 1) if given[i] < reach]
        mass, budget = sum([loads[i] for i in candidates]), surplus
        for i in candidates:
            extra = min(reach - given[i], max(1, budget * loads[i] // mass), surplus)
            given[i] = given[i] + extra
            surplus = surplus - extra
    return np.array([reach] + given)


def ragged_sizes(rng, count, total, limit, lean):
    if count == 2:
        one = jax.random.randint(rng, (), max(1, total - limit), min(limit, total - 1) + 1)
        return jnp.stack([one, total - one])
    sizes = jnp.asarray(length_profile(count, total, limit, lean), jnp.int32)
    pairs = (count - 1) // 2
    giver, taker = sizes[1:1 + 2 * pairs:2], sizes[2:2 + 2 * pairs:2]
    slack = jnp.minimum(giver - 1, limit - taker)
    shifted = jax.random.randint(jax.random.fold_in(rng, 1), (pairs,), 0, 1 << 20) % (slack + 1)
    sizes = sizes.at[1:1 + 2 * pairs:2].set(giver - shifted).at[2:2 + 2 * pairs:2].set(taker + shifted)
    return sizes[jax.random.permutation(jax.random.fold_in(rng, 2), count)]


def centred(stream_key, dims, spread, bound, cuts=(), held_as=jnp.bfloat16):
    loudness = levels(stream_key, dims, cuts, -0.22, 0.18) if cuts else 1.0
    result = jax.random.normal(stream_key, dims, jnp.float32) * spread * loudness
    return jnp.minimum(jnp.maximum(result, -bound), bound).astype(held_as)


def setup_inputs(seed: int = 0) -> dict:
    key_list = jax.random.split(jax.random.key(seed), 19)
    doc_tokens = centred(key_list[0], (DOC_ROWS, LEN, D), 1.0, 6.0, ((0, 8), (1, 4)))
    query_tokens = centred(key_list[1], (QUERIES, QLEN, D), 1.0, 6.0, ((0, 32),))
    doc_segments = jax.vmap(lambda own: jnp.searchsorted(jnp.cumsum(ragged_sizes(own, DOCS_ROW, LEN, LEN // 2, 1)), jnp.arange(LEN), side="right"))(jax.random.split(key_list[2], DOC_ROWS)).reshape((DOC_ROWS, LEN)).astype(jnp.int32)
    query_keep = draw_query_keep(jax.random.fold_in(key_list[18], 71), 0)
    retrieved = set_ends((jax.random.randint(key_list[4], (QUERIES, QLEN, DOCS), 0, 8) < 1).astype(jnp.int32), jax.random.fold_in(key_list[4], 1), 0, 1)
    positives = set_ends(jax.random.randint(key_list[5], (QUERIES,), 0, DOCS), jax.random.fold_in(key_list[5], 1), 0, DOCS - 1).astype(jnp.int32)
    attn_gain = jnp.clip(1.0 + 0.1 * jax.random.normal(key_list[6], (D,), jnp.float32), 0.5, 1.5).astype(jnp.bfloat16)
    query_weight = centred(key_list[7], (D, D), (D * HEAD) ** -0.5, 0.02734375, ((1, 4),))
    key_weight = centred(key_list[8], (D, D), D ** -0.5, 0.21875, ((1, 4),))
    value_weight = centred(key_list[9], (D, D), D ** -0.5, 0.21875, ((1, 4),))
    output_weight = centred(key_list[10], (D, D), (D // 8) ** -0.5, 0.625, ((0, 4),))
    position_bias = centred(key_list[11], (BUCKETS, HEADS), 1.0, 4.0, ((1, 4),))
    ffn_gain = jnp.clip(1.0 + 0.1 * jax.random.normal(key_list[12], (D,), jnp.float32), 0.5, 1.5).astype(jnp.bfloat16)
    gate_weight = centred(key_list[13], (D, FF), D ** -0.5, 0.21875, ((1, 4),))
    up_weight = centred(key_list[14], (D, FF), D ** -0.5, 0.21875, ((1, 4),))
    down_weight = centred(key_list[15], (FF, D), FF ** -0.5, 0.125, ((0, 4),))
    final_gain = jnp.clip(1.0 + 0.1 * jax.random.normal(key_list[16], (D,), jnp.float32), 0.5, 1.5).astype(jnp.bfloat16)
    proj_weight = centred(key_list[17], (D, EMB), D ** -0.5, 0.21875)
    return {"doc_tokens": doc_tokens, "query_tokens": query_tokens, "doc_segments": doc_segments, "query_keep": query_keep, "retrieved": retrieved, "positives": positives, "attn_gain": attn_gain, "query_weight": query_weight, "key_weight": key_weight, "value_weight": value_weight, "output_weight": output_weight, "position_bias": position_bias, "ffn_gain": ffn_gain, "gate_weight": gate_weight, "up_weight": up_weight, "down_weight": down_weight, "final_gain": final_gain, "proj_weight": proj_weight}


epsilon = 1e-06
sharpness = 16.0
smoothing_divisor = 0.05
masked_score = -1e+30

@jax.custom_vjp
def low(v):
    return lax.optimization_barrier(v.astype(jnp.bfloat16)).astype(jnp.float32)

@jax.custom_vjp
def low_back(v):
    return v

def low_keep(v):
    return (low(v), None)

def low_pass(kept, grad):
    return (grad,)

def back_keep(v):
    return (v, None)

def back_low(kept, grad):
    return (low(grad),)
low.defvjp(low_keep, low_pass)
low_back.defvjp(back_keep, back_low)

def bucket_table(length, buckets):
    offsets = np.arange(-(length - 1), length)
    half_count = buckets // 2
    exact_count = half_count // 2
    distance = np.abs(offsets)
    scaled = np.log(np.maximum(distance, 1) / exact_count) / np.log(128.0 / exact_count) * (half_count - exact_count)
    far_bucket = np.minimum(exact_count + np.floor(np.maximum(scaled, 0.0)), half_count - 1)
    bucket = np.where(distance < exact_count, distance, far_bucket) + np.where(offsets > 0, half_count, 0)
    return bucket.astype(np.int32)

def bias_rows(bias_table, bucket_ids, row_start, row_count, length):
    by_offset = jnp.transpose(jnp.take(bias_table, jnp.asarray(bucket_ids), axis=0))
    columns = jnp.arange(length).astype(jnp.int32)
    row_ids = (row_start + jnp.arange(row_count).astype(jnp.int32)).astype(jnp.int32)
    offset_index = (columns[None, :] - row_ids[:, None] + (length - 1)).astype(jnp.int32)
    return jnp.take(by_offset, offset_index, axis=1)

def matmul_high(left_side, right_side):
    return jnp.dot(left_side, right_side, precision=lax.Precision.HIGHEST)

def rms_normed(values, gain_values):
    return values * lax.rsqrt(lax.optimization_barrier(jnp.mean(values * values, axis=-1, keepdims=True)) + epsilon) * gain_values

def encoder_layer(tokens, segments, keep_mask, bucket_ids, params):
    attn_gain, query_weight, key_weight, value_weight, output_weight, position_bias, ffn_gain, gate_weight, up_weight, down_weight, final_gain, proj_weight = params
    seq_len = tokens.shape[0]
    head_count = position_bias.shape[1]
    head_size = query_weight.shape[1] // head_count
    normed_attn = low(rms_normed(tokens, attn_gain))
    search_requests = low(low_back(matmul_high(normed_attn, query_weight))).reshape(seq_len, head_count, head_size)
    key_heads = low(low_back(matmul_high(normed_attn, key_weight))).reshape(seq_len, head_count, head_size)
    value_heads = low(low_back(matmul_high(normed_attn, value_weight))).reshape(seq_len, head_count, head_size)
    block_rows = min(512, seq_len)

    def attend_block(row_start):
        block_queries = lax.dynamic_slice_in_dim(search_requests, row_start, block_rows, 0)
        block_segments = lax.dynamic_slice_in_dim(segments, row_start, block_rows, 0)
        pairing_ratings = jnp.einsum('ihd,jhd->hij', block_queries, key_heads, precision=lax.Precision.HIGHEST)
        pairing_ratings = low_back(pairing_ratings + bias_rows(position_bias, bucket_ids, row_start, block_rows, seq_len))
        allowed = (block_segments[:, None] == segments[None, :]) & (keep_mask[None, :] > 0)
        pairing_ratings = jnp.where(allowed[None], pairing_ratings, masked_score)
        largest = lax.optimization_barrier(jnp.max(pairing_ratings, axis=-1, keepdims=True))
        powered_scores = jnp.exp(pairing_ratings - largest)
        weights = low(powered_scores / lax.optimization_barrier(jnp.sum(powered_scores, axis=-1, keepdims=True)))
        return jnp.einsum('hij,jhd->ihd', weights, value_heads, precision=lax.Precision.HIGHEST)
    starts = (jnp.arange(seq_len // block_rows) * block_rows).astype(jnp.int32)
    attended = lax.map(jax.checkpoint(attend_block), starts).reshape(seq_len, head_count * head_size)
    context = low(low_back(attended))
    mid_values = tokens + low_back(matmul_high(context, output_weight))
    normed_ffn = low(rms_normed(mid_values, ffn_gain))
    gate_values = low_back(matmul_high(normed_ffn, gate_weight))
    up_values = low_back(matmul_high(normed_ffn, up_weight))
    hidden = low(jax.nn.gelu(gate_values, approximate=True) * up_values)
    layer_out = mid_values + low_back(matmul_high(hidden, down_weight))
    final_normed = low(rms_normed(layer_out, final_gain))
    projected = low_back(matmul_high(final_normed, proj_weight))
    return low(projected * lax.rsqrt(lax.optimization_barrier(jnp.sum(projected * projected, axis=-1, keepdims=True)) + epsilon))

def document_sums(query_vectors, row_args):
    doc_vectors, row_segments = row_args
    inner_products = low_back(matmul_high(query_vectors, jnp.transpose(doc_vectors)))
    member = (row_segments[:, None] == jnp.arange(DOCS_ROW).astype(jnp.int32)[None, :]).astype(jnp.float32)
    return matmul_high(jnp.exp(sharpness * (inner_products - 1.0)), member)

def reference(doc_tokens, query_tokens, doc_segments, query_keep, retrieved, positives, attn_gain, query_weight, key_weight, value_weight, output_weight, position_bias, ffn_gain, gate_weight, up_weight, down_weight, final_gain, proj_weight):
    params = tuple((weight.astype(jnp.float32) for weight in (attn_gain, query_weight, key_weight, value_weight, output_weight, position_bias, ffn_gain, gate_weight, up_weight, down_weight, final_gain, proj_weight)))
    group_size = math.gcd(QUERIES, 128)
    group_span = group_size * QLEN
    doc_table = bucket_table(LEN, BUCKETS)
    query_table = bucket_table(group_span, BUCKETS)
    query_segments = (jnp.arange(group_span) // QLEN).astype(jnp.int32)
    doc_keep = jnp.ones((LEN,), jnp.int32)
    group_keep = query_keep.reshape(QUERIES // group_size, group_span)
    chosen = (query_keep[:, :, None] * retrieved).astype(jnp.float32)
    counts = lax.optimization_barrier(jnp.sum(chosen, axis=1))
    selected_mask = jnp.arange(DOCS).astype(jnp.int32)[None, :] == positives[:, None]

    def total_loss(doc_values, query_values, weights):

        def doc_row(row_args):
            return encoder_layer(row_args[0], row_args[1], doc_keep, doc_table, weights)

        def query_group(group_args):
            return encoder_layer(group_args[0], query_segments, group_args[1], query_table, weights)
        doc_vectors = lax.map(jax.checkpoint(doc_row), (doc_values, doc_segments))
        query_vectors = lax.map(jax.checkpoint(query_group), (query_values.reshape(QUERIES // group_size, group_span, D), group_keep))
        query_vectors = query_vectors.reshape(QUERIES * QLEN, EMB)
        token_sums = lax.map(jax.checkpoint(partial(document_sums, query_vectors)), (doc_vectors, doc_segments))
        smooth = 1.0 + jnp.log(token_sums) / sharpness
        smooth = jnp.transpose(smooth, (1, 0, 2)).reshape(QUERIES, QLEN, DOCS)
        pairing_ratings = lax.optimization_barrier(jnp.sum(chosen * smooth, axis=1)) / jnp.maximum(counts, 1.0)
        rating_energies = pairing_ratings / smoothing_divisor
        largest = lax.optimization_barrier(jnp.max(rating_energies, axis=1, keepdims=True))
        log_total = largest[:, 0] + jnp.log(lax.optimization_barrier(jnp.sum(jnp.exp(rating_energies - largest), axis=1)))
        picked = lax.optimization_barrier(jnp.sum(jnp.where(selected_mask, rating_energies, 0.0), axis=1))
        return jnp.sum(log_total - picked)
    loss_sum, pullback = jax.vjp(total_loss, doc_tokens.astype(jnp.float32), query_tokens.astype(jnp.float32), params)
    doc_grad, query_grad, weight_grads = pullback(jnp.ones_like(loss_sum))
    found_rows = lax.optimization_barrier(jnp.sum(jnp.where(selected_mask, counts, 0.0), axis=1)) > 0.5
    found_share = jnp.mean(found_rows.astype(jnp.float32))
    return (loss_sum / QUERIES, found_share, doc_grad, query_grad, weight_grads[0], weight_grads[1], weight_grads[2], weight_grads[3], weight_grads[4], weight_grads[5], weight_grads[6], weight_grads[7], weight_grads[8], weight_grads[9], weight_grads[10], weight_grads[11])
```

```python
from functools import partial

import jax
import jax.numpy as jnp
import numpy as np
from jax import lax
from jax.experimental import pallas as pl
from jax.experimental.pallas import tpu as pltpu
from jax.sharding import PartitionSpec as P

epsilon = 1e-06
sharpness = 16.0
smoothing_divisor = 0.05
masked_score = -1e30
BLOCK = 128
PAIR = 2 * BLOCK
bf16 = jnp.bfloat16
f32 = jnp.float32


def bucket_starts(buckets):
    half = buckets // 2
    exact = half // 2
    distance = np.arange(0, 2048)
    scaled = (
        np.log(np.maximum(distance, 1) / exact) / np.log(128.0 / exact) * (half - exact)
    )
    far = np.minimum(exact + np.floor(np.maximum(scaled, 0.0)), half - 1)
    bucket = np.where(distance < exact, distance, far)
    return [int(np.argmax(bucket >= b)) for b in range(half)]


def dot_nn(a, b):
    return lax.dot_general(a, b, (((1,), (0,)), ((), ())), preferred_element_type=f32)


def dot_nt(a, b):
    return lax.dot_general(a, b, (((1,), (1,)), ((), ())), preferred_element_type=f32)


def dot_tn(a, b):
    return lax.dot_general(a, b, (((0,), (0,)), ((), ())), preferred_element_type=f32)


def dot_exact(a, b):
    return lax.dot_general(
        a, b, (((1,), (0,)), ((), ())), precision=lax.Precision.HIGHEST, preferred_element_type=f32
    )


def params(limit_mib=40):
    return pltpu.CompilerParams(vmem_limit_bytes=limit_mib << 20)


def bias_kernel(starts, heads, tab_ref, t_ref, tt_ref):
    half = len(starts)
    sub = lax.broadcasted_iota(jnp.int32, (BLOCK, BLOCK), 0)
    lane = lax.broadcasted_iota(jnp.int32, (BLOCK, BLOCK), 1)
    for ref, base in ((t_ref, lane - sub), (tt_ref, sub - lane)):
        for d in (-1, 0, 1):
            offset = base + BLOCK * d
            n = jnp.abs(offset)
            for h in range(heads):
                low = high = None
                if d <= 0:
                    low = jnp.full((BLOCK, BLOCK), tab_ref[0, h], f32)
                    for b in range(1, half):
                        low = jnp.where(n >= starts[b], tab_ref[b, h], low)
                if d >= 0:
                    high = jnp.full((BLOCK, BLOCK), tab_ref[half, h], f32)
                    for b in range(1, half):
                        high = jnp.where(n >= starts[b], tab_ref[half + b, h], high)
                if d < 0:
                    tile = low
                elif d > 0:
                    tile = high
                else:
                    tile = jnp.where(offset > 0, high, low)
                ref[h, d + 2] = tile
        for h in range(heads):
            ref[h, 0] = jnp.full((BLOCK, BLOCK), tab_ref[half - 1, h], f32)
            ref[h, 4] = jnp.full((BLOCK, BLOCK), tab_ref[2 * half - 1, h], f32)


def bias_tiles(table):
    buckets, heads = table.shape
    starts = bucket_starts(buckets)
    shape = jax.ShapeDtypeStruct((heads, 5, BLOCK, BLOCK), f32)
    return pl.pallas_call(
        partial(bias_kernel, starts, heads),
        in_specs=[pl.BlockSpec(memory_space=pltpu.SMEM)],
        out_shape=(shape, shape),
        compiler_params=params(),
        name="bias_tiles",
    )(table)


def clipped(d):
    return jnp.minimum(jnp.maximum(d, -2), 2) + 2


def attend_kernel(heads, size, lo_ref, cnt_ref, qkv_ref, segq_ref, segk_ref, t_ref, ctx_ref, lse_ref, k_s, v_s, s_s):
    b = pl.program_id(0)
    inner = heads * size

    @pl.when(b == 0)
    def _():
        for h in range(heads):
            k_s[h] = qkv_ref[:, inner + h * size : inner + (h + 1) * size]
            v_s[h] = qkv_ref[:, 2 * inner + h * size : 2 * inner + (h + 1) * size]

    rows = pl.multiple_of(b * BLOCK, BLOCK)
    block = qkv_ref[pl.ds(rows, BLOCK), :inner]
    queries = [block[:, h * size : (h + 1) * size] for h in range(heads)]
    seg_col = segq_ref[...]
    lo = lo_ref[b]
    cnt = cnt_ref[b]

    def first(i, tops):
        at = lo + 2 * i
        start = pl.multiple_of(at * BLOCK, BLOCK)
        allowed = seg_col == segk_ref[:, pl.ds(start, PAIR)]
        i0 = clipped(at - b)
        i1 = clipped(at + 1 - b)
        out = []
        for h in range(heads):
            s = dot_nt(queries[h], k_s[h, pl.ds(start, PAIR), :])
            s0 = jnp.where(allowed[:, :BLOCK], s[:, :BLOCK] + t_ref[h, i0], masked_score)
            s1 = jnp.where(allowed[:, BLOCK:], s[:, BLOCK:] + t_ref[h, i1], masked_score)
            s_s[h, i, :, :BLOCK] = s0
            s_s[h, i, :, BLOCK:] = s1
            out.append(jnp.maximum(tops[h], jnp.maximum(s0, s1)))
        return tuple(out)

    tops = lax.fori_loop(
        0, cnt, first, tuple(jnp.full((BLOCK, BLOCK), masked_score, f32) for _ in range(heads))
    )
    largest = [
        jnp.broadcast_to(jnp.max(top, axis=1, keepdims=True), (BLOCK, BLOCK)) for top in tops
    ]

    def second(i, carry):
        at = lo + 2 * i
        start = pl.multiple_of(at * BLOCK, BLOCK)
        sums, accs = carry
        new_sums, new_accs = [], []
        for h in range(heads):
            p0 = jnp.exp(s_s[h, i, :, :BLOCK] - largest[h])
            p1 = jnp.exp(s_s[h, i, :, BLOCK:] - largest[h])
            new_sums.append(sums[h] + (p0 + p1))
            p = jnp.concatenate([p0.astype(bf16), p1.astype(bf16)], axis=1)
            new_accs.append(accs[h] + dot_nn(p, v_s[h, pl.ds(start, PAIR), :]))
        return (tuple(new_sums), tuple(new_accs))

    sums, accs = lax.fori_loop(
        0,
        cnt,
        second,
        (
            tuple(jnp.zeros((BLOCK, BLOCK), f32) for _ in range(heads)),
            tuple(jnp.zeros((BLOCK, size), f32) for _ in range(heads)),
        ),
    )
    outs = []
    for h in range(heads):
        total = jnp.sum(sums[h], axis=1, keepdims=True)
        outs.append((accs[h] / total).astype(bf16))
        lse = largest[h] + jnp.log(jnp.broadcast_to(total, (BLOCK, BLOCK)))
        lse_ref[h : h + 1, :] = jnp.transpose(lse)[0:1, :]
    ctx_ref[...] = jnp.concatenate(outs, axis=1)


def attend(qkv, ranges, segs, tiles):
    lo, cnt = ranges
    segq_col, segq_row, segk_col, segk_row = segs
    total, wide = qkv.shape
    heads = tiles.shape[0]
    inner = wide // 3
    size = inner // heads
    blocks = total // BLOCK
    flops = 4 * total * total * inner // 2
    return pl.pallas_call(
        partial(attend_kernel, heads, size),
        grid_spec=pltpu.PrefetchScalarGridSpec(
            num_scalar_prefetch=2,
            grid=(blocks,),
            in_specs=[
                pl.BlockSpec((total, wide), lambda b, *_: (0, 0)),
                pl.BlockSpec((BLOCK, 1), lambda b, *_: (b, 0)),
                pl.BlockSpec((1, total), lambda b, *_: (0, 0)),
                pl.BlockSpec((heads, 5, BLOCK, BLOCK), lambda b, *_: (0, 0, 0, 0)),
            ],
            out_specs=[
                pl.BlockSpec((BLOCK, inner), lambda b, *_: (b, 0)),
                pl.BlockSpec((8, BLOCK), lambda b, *_: (0, b)),
            ],
            scratch_shapes=[
                pltpu.VMEM((heads, total, size), bf16),
                pltpu.VMEM((heads, total, size), bf16),
                pltpu.VMEM((heads, blocks // 2 + 1, BLOCK, PAIR), f32),
            ],
        ),
        out_shape=(
            jax.ShapeDtypeStruct((total, inner), bf16),
            jax.ShapeDtypeStruct((8, total), f32),
        ),
        compiler_params=params(),
        cost_estimate=pl.CostEstimate(
            flops=flops, transcendentals=total * total * heads // 2, bytes_accessed=4 << 20
        ),
        name="attend",
    )(lo, cnt, qkv, segq_col, segk_row, tiles)


def attend_back_kernel(
    starts,
    heads,
    size,
    lo_ref,
    cnt_ref,
    qkv_ref,
    do_ref,
    ctx_ref,
    lse_ref,
    segk_ref,
    segq_ref,
    tt_ref,
    grad_ref,
    bias_ref,
    q_s,
    do_s,
    dq_s,
    delta_s,
    d_s,
):
    b = pl.program_id(0)
    inner = heads * size
    total = qkv_ref.shape[0]
    half = len(starts)

    @pl.when(b == 0)
    def _():
        prod = do_ref[...].astype(f32) * ctx_ref[...].astype(f32)
        high = prod.astype(bf16)
        low = (prod - high.astype(f32)).astype(bf16)
        row = lax.broadcasted_iota(jnp.int32, (8, inner), 0)
        col = lax.broadcasted_iota(jnp.int32, (8, inner), 1)
        pick = ((col >= row * size) & (col < (row + 1) * size)).astype(f32).astype(bf16)
        delta_s[...] = dot_nt(pick, high) + dot_nt(pick, low)
        for h in range(heads):
            q_s[h] = qkv_ref[:, h * size : (h + 1) * size]
            do_s[h] = do_ref[:, h * size : (h + 1) * size]
        dq_s[...] = jnp.zeros(dq_s.shape, f32)
        d_s[...] = jnp.zeros(d_s.shape, f32)

    rows = pl.multiple_of(b * BLOCK, BLOCK)
    block = qkv_ref[pl.ds(rows, BLOCK), :]
    keys = [block[:, inner + h * size : inner + (h + 1) * size] for h in range(heads)]
    values = [block[:, 2 * inner + h * size : 2 * inner + (h + 1) * size] for h in range(heads)]
    seg_col = segk_ref[...]
    lo = lo_ref[b]
    cnt = cnt_ref[b]

    def step(i, carry):
        dks, dvs = carry
        at = lo + 2 * i
        start = pl.multiple_of(at * BLOCK, BLOCK)
        allowed = seg_col == segq_ref[:, pl.ds(start, PAIR)]
        i0 = clipped(b - at)
        i1 = clipped(b - at - 1)
        new_k, new_v = [], []
        for h in range(heads):
            q = q_s[h, pl.ds(start, PAIR), :]
            do = do_s[h, pl.ds(start, PAIR), :]
            s = dot_nt(keys[h], q)
            dp = dot_nt(values[h], do)
            bias = jnp.concatenate([tt_ref[h, i0], tt_ref[h, i1]], axis=1)
            lse = lse_ref[h : h + 1, pl.ds(start, PAIR)]
            delta = delta_s[h : h + 1, pl.ds(start, PAIR)]
            p = jnp.where(allowed, jnp.exp(s + bias - lse), 0.0)
            ds = p * (dp - delta)
            d_s[h, i0] += ds[:, :BLOCK]
            d_s[h, i1] += ds[:, BLOCK:]
            ds16 = ds.astype(bf16)
            new_v.append(dvs[h] + dot_nn(p.astype(bf16), do))
            new_k.append(dks[h] + dot_nn(ds16, q))
            dq_s[h, pl.ds(start, PAIR), :] += dot_tn(ds16, keys[h])
        return (tuple(new_k), tuple(new_v))

    zero = tuple(jnp.zeros((BLOCK, size), f32) for _ in range(heads))
    dks, dvs = lax.fori_loop(0, cnt, step, (zero, zero))
    grad_ref[pl.ds(rows, BLOCK), inner : 2 * inner] = jnp.concatenate(dks, axis=1).astype(bf16)
    grad_ref[pl.ds(rows, BLOCK), 2 * inner :] = jnp.concatenate(dvs, axis=1).astype(bf16)

    @pl.when(b == pl.num_programs(0) - 1)
    def _():
        grad_ref[:, :inner] = jnp.concatenate([dq_s[h] for h in range(heads)], axis=1).astype(bf16)
        sub = lax.broadcasted_iota(jnp.int32, (BLOCK, BLOCK), 0)
        lane = lax.broadcasted_iota(jnp.int32, (BLOCK, BLOCK), 1)
        ids = {}
        for d in (-1, 0, 1):
            offset = sub - lane + BLOCK * d
            n = jnp.abs(offset)
            bucket = jnp.zeros((BLOCK, BLOCK), jnp.int32)
            for e in range(1, half):
                bucket = jnp.where(n >= starts[e], e, bucket)
            ids[d] = jnp.where(offset > 0, bucket + half, bucket)
        for h in range(heads):
            for e in range(2 * half):
                parts = []
                for d in (-1, 0, 1):
                    if (d < 0 and e >= half) or (d > 0 and e < half):
                        continue
                    parts.append(jnp.where(ids[d] == e, d_s[h, d + 2], 0.0))
                if e == half - 1:
                    parts.append(d_s[h, 0])
                if e == 2 * half - 1:
                    parts.append(d_s[h, 4])
                whole = parts[0]
                for part in parts[1:]:
                    whole = whole + part
                bias_ref[h, e : e + 1, :] = jnp.sum(whole, axis=0, keepdims=True)


def attend_back(qkv, context_grad, context, lse, ranges, segs, tiles, buckets):
    lo, cnt = ranges
    segq_col, segq_row, segk_col, segk_row = segs
    total, wide = qkv.shape
    heads = tiles.shape[0]
    inner = wide // 3
    size = inner // heads
    blocks = total // BLOCK
    starts = bucket_starts(buckets)
    whole = lambda b, *_: (0, 0)
    return pl.pallas_call(
        partial(attend_back_kernel, starts, heads, size),
        grid_spec=pltpu.PrefetchScalarGridSpec(
            num_scalar_prefetch=2,
            grid=(blocks,),
            in_specs=[
                pl.BlockSpec((total, wide), whole),
                pl.BlockSpec((total, inner), whole),
                pl.BlockSpec((total, inner), whole),
                pl.BlockSpec((8, total), whole),
                pl.BlockSpec((BLOCK, 1), lambda b, *_: (b, 0)),
                pl.BlockSpec((1, total), whole),
                pl.BlockSpec((heads, 5, BLOCK, BLOCK), lambda b, *_: (0, 0, 0, 0)),
            ],
            out_specs=[
                pl.BlockSpec((total, wide), whole),
                pl.BlockSpec((heads, buckets, BLOCK), lambda b, *_: (0, 0, 0)),
            ],
            scratch_shapes=[
                pltpu.VMEM((heads, total, size), bf16),
                pltpu.VMEM((heads, total, size), bf16),
                pltpu.VMEM((heads, total, size), f32),
                pltpu.VMEM((8, total), f32),
                pltpu.VMEM((heads, 5, BLOCK, BLOCK), f32),
            ],
        ),
        out_shape=(
            jax.ShapeDtypeStruct((total, wide), bf16),
            jax.ShapeDtypeStruct((heads, buckets, BLOCK), f32),
        ),
        compiler_params=params(),
        cost_estimate=pl.CostEstimate(
            flops=10 * total * total * inner // 2,
            transcendentals=total * total * heads // 2,
            bytes_accessed=6 << 20,
        ),
        name="attend_back",
    )(lo, cnt, qkv, context_grad, context, lse, segk_col, segq_row, tiles)


def pool_matrix(shape, axis, me, query_len, query_local):
    token = lax.broadcasted_iota(jnp.int32, shape, axis)
    query = lax.broadcasted_iota(jnp.int32, shape, 1 - axis)
    span = query_len * query_local
    holder = jnp.bitwise_xor(token // span, me)
    return (holder * query_local + token % span // query_len == query).astype(f32)


def score_kernel(query_len, query_local, docs, first_ref, emb_ref, qe_ref, seg_ref, chosen_ref, pos_ref, sums_ref, logit_ref, stat_ref, acc_s):
    b = pl.program_id(0)
    count = qe_ref.shape[0]

    @pl.when(b == 0)
    def _():
        acc_s[...] = jnp.zeros(acc_s.shape, f32)

    near = jnp.exp(sharpness * (dot_nt(emb_ref[...], qe_ref[...]) - 1.0))
    seg = seg_ref[...]
    for d in range(docs):
        acc_s[d : d + 1, :] += jnp.sum(jnp.where(seg == d, near, 0.0), axis=0, keepdims=True)

    @pl.when(b == pl.num_programs(0) - 1)
    def _():
        sums = acc_s[:docs, :]
        sums_ref[...] = acc_s[...]
        chosen = chosen_ref[:docs, :]
        smooth = 1.0 + jnp.log(sums) / sharpness
        pool = pool_matrix((count, pos_ref.shape[1]), 0, first_ref[1], query_len, query_local)
        picked = dot_exact(chosen * smooth, pool)
        counts = dot_exact(chosen, pool)
        logits = picked / jnp.maximum(counts, 1.0) / smoothing_divisor
        top = jnp.max(logits, axis=0, keepdims=True)
        spread = jnp.sum(jnp.exp(logits - top), axis=0, keepdims=True)
        doc = lax.broadcasted_iota(jnp.int32, logits.shape, 0) + first_ref[0]
        mine = doc == pos_ref[0:1, :]
        stat_ref[0:1, :] = top
        stat_ref[1:2, :] = spread
        stat_ref[2:3, :] = jnp.sum(jnp.where(mine, logits, 0.0), axis=0, keepdims=True)
        stat_ref[3:4, :] = jnp.sum(jnp.where(mine, counts, 0.0), axis=0, keepdims=True)
        stat_ref[4:8, :] = jnp.zeros((4, pos_ref.shape[1]), f32)
        logit_ref[0:docs, :] = logits
        logit_ref[docs : 2 * docs, :] = counts


def score(first, emb, query_emb, seg_col, chosen, positives, query_len, query_local, docs):
    count, width = query_emb.shape
    lanes = positives.shape[1]
    length = emb.shape[0]
    blocks = length // BLOCK
    whole = lambda b, *_: (0, 0)
    return pl.pallas_call(
        partial(score_kernel, query_len, query_local, docs),
        grid_spec=pltpu.PrefetchScalarGridSpec(
            num_scalar_prefetch=1,
            grid=(blocks,),
            in_specs=[
                pl.BlockSpec((BLOCK, width), lambda b, *_: (b, 0)),
                pl.BlockSpec((count, width), whole),
                pl.BlockSpec((BLOCK, 1), lambda b, *_: (b, 0)),
                pl.BlockSpec((8, count), whole),
                pl.BlockSpec((8, lanes), whole),
            ],
            out_specs=[
                pl.BlockSpec((8, count), whole),
                pl.BlockSpec((8, lanes), whole),
                pl.BlockSpec((8, lanes), whole),
            ],
            scratch_shapes=[pltpu.VMEM((8, count), f32)],
        ),
        out_shape=(
            jax.ShapeDtypeStruct((8, count), f32),
            jax.ShapeDtypeStruct((8, lanes), f32),
            jax.ShapeDtypeStruct((8, lanes), f32),
        ),
        compiler_params=params(),
        name="score",
    )(first, emb, query_emb, seg_col, chosen, positives)


def score_back_kernel(query_len, query_local, docs, first_ref, emb_ref, qe_ref, seg_ref, chosen_ref, pos_ref, sums_ref, logit_ref, stat_ref, demb_ref, dqe_ref, grad_s, dq_s):
    b = pl.program_id(0)
    count = qe_ref.shape[0]

    @pl.when(b == 0)
    def _():
        logits = logit_ref[0:docs, :]
        counts = logit_ref[docs : 2 * docs, :]
        doc = lax.broadcasted_iota(jnp.int32, logits.shape, 0) + first_ref[0]
        mine = (doc == pos_ref[0:1, :]).astype(f32)
        share = jnp.exp(logits - stat_ref[0:1, :]) / stat_ref[1:2, :]
        grad = (share - mine) / smoothing_divisor / jnp.maximum(counts, 1.0)
        spread = pool_matrix((logits.shape[1], count), 1, first_ref[1], query_len, query_local)
        grad_s[0:docs, :] = dot_exact(grad, spread) * chosen_ref[:docs, :] / sums_ref[:docs, :]
        dq_s[...] = jnp.zeros(dq_s.shape, f32)

    emb = emb_ref[...]
    near = jnp.exp(sharpness * (dot_nt(emb, qe_ref[...]) - 1.0))
    seg = seg_ref[...]
    weight = jnp.broadcast_to(grad_s[0:1, :], near.shape)
    for d in range(1, docs):
        weight = jnp.where(seg == d, grad_s[d : d + 1, :], weight)
    grad = (near * weight).astype(bf16)
    demb_ref[...] = dot_nn(grad, qe_ref[...])
    dq_s[...] += dot_tn(emb, grad)

    @pl.when(b == pl.num_programs(0) - 1)
    def _():
        dqe_ref[...] = jnp.transpose(dq_s[...]).astype(bf16)


def score_back(first, emb, query_emb, seg_col, chosen, positives, sums, logits, stats, query_len, query_local, docs):
    count, width = query_emb.shape
    lanes = positives.shape[1]
    length = emb.shape[0]
    blocks = length // BLOCK
    whole = lambda b, *_: (0, 0)
    return pl.pallas_call(
        partial(score_back_kernel, query_len, query_local, docs),
        grid_spec=pltpu.PrefetchScalarGridSpec(
            num_scalar_prefetch=1,
            grid=(blocks,),
            in_specs=[
                pl.BlockSpec((BLOCK, width), lambda b, *_: (b, 0)),
                pl.BlockSpec((count, width), whole),
                pl.BlockSpec((BLOCK, 1), lambda b, *_: (b, 0)),
                pl.BlockSpec((8, count), whole),
                pl.BlockSpec((8, lanes), whole),
                pl.BlockSpec((8, count), whole),
                pl.BlockSpec((8, lanes), whole),
                pl.BlockSpec((8, lanes), whole),
            ],
            out_specs=[
                pl.BlockSpec((BLOCK, width), lambda b, *_: (b, 0)),
                pl.BlockSpec((count, width), whole),
            ],
            scratch_shapes=[pltpu.VMEM((8, count), f32), pltpu.VMEM((width, count), f32)],
        ),
        out_shape=(
            jax.ShapeDtypeStruct((length, width), f32),
            jax.ShapeDtypeStruct((count, width), bf16),
        ),
        compiler_params=params(),
        name="score_back",
    )(first, emb, query_emb, seg_col, chosen, positives, sums, logits, stats)


def rms_scale(values):
    return lax.rsqrt(jnp.mean(values * values, axis=-1, keepdims=True) + epsilon)


def rms_back(values, scale_values, gain_values, gradient):
    weighted = gradient * gain_values
    average = jnp.mean(weighted * values, axis=-1, keepdims=True)
    input_grad = (
        scale_values * weighted - values * (scale_values * scale_values * scale_values) * average
    )
    gain_grad = jnp.sum(gradient * values * scale_values, axis=0)
    return (input_grad, gain_grad)


def gated_unit(gate_values, up_values):
    return jax.nn.gelu(gate_values, approximate=True) * up_values


def swapped(bit, mine, theirs, axis=0):
    first = jnp.where(bit == 0, mine, theirs)
    second = jnp.where(bit == 0, theirs, mine)
    return jnp.concatenate([first, second], axis=axis)


def part(values, index, parts, axis=0):
    size = values.shape[axis] // parts
    return lax.dynamic_slice_in_dim(values, index * size, size, axis)


def shards(
    doc_tokens,
    query_tokens,
    doc_segments,
    query_keep,
    retrieved,
    positives,
    attn_gain,
    query_weight,
    key_weight,
    value_weight,
    output_weight,
    position_bias,
    ffn_gain,
    gate_weight,
    up_weight,
    down_weight,
    final_gain,
    proj_weight,
):
    groups = lax.axis_size("dp")
    tensor_size = lax.axis_size("mp")
    bits = groups.bit_length() - 1
    dp = lax.axis_index("dp")
    mp = lax.axis_index("mp")
    x = mp // 2
    core = mp % 2
    row_count, shard_len, width = doc_tokens.shape
    length = shard_len * tensor_size
    query_local, query_len, _ = query_tokens.shape
    chip_queries = query_local * 2
    buckets = position_bias.shape[0]
    hidden_local = gate_weight.shape[1]
    doc_local = retrieved.shape[2]
    docs_row = doc_local // row_count
    query_total = query_keep.shape[0]
    vector_width = proj_weight.shape[1]
    inner = query_weight.shape[1]

    def over(axis, size, mask):
        pairs = [(i, i ^ mask) for i in range(size)]
        return lambda values: lax.ppermute(values, axis, pairs)

    to_x = over("mp", tensor_size, 2)
    to_core = over("mp", tensor_size, 1)
    to_dp = [over("dp", groups, 1 << b) for b in range(bits)]
    dp_bit = [(dp >> b) & 1 for b in range(bits)]

    kept_rows = lax.dynamic_index_in_dim(doc_tokens, x, 0, keepdims=False)
    sent_rows = lax.dynamic_index_in_dim(doc_tokens, 1 - x, 0, keepdims=False)
    far_rows = to_x(sent_rows)
    near_rows = to_core(kept_rows)
    far_core_rows = to_core(far_rows)
    flat_queries = query_tokens.reshape(query_local * query_len, width)
    near_queries = to_core(flat_queries)

    def from_x(weight):
        if bits == 0:
            return to_x(weight)
        got = to_x(part(weight, dp_bit[0], 2))
        return swapped(dp_bit[0], got, to_dp[0](got))

    own_qkv = jnp.concatenate([query_weight, key_weight, value_weight], axis=1)
    far_qkv = from_x(own_qkv)
    far_output = from_x(output_weight)
    own_gate_up = jnp.concatenate([gate_weight, up_weight], axis=1)
    far_gate_up = from_x(own_gate_up)
    far_down = from_x(down_weight)
    far_bias = to_x(position_bias)
    qkv_weights = (own_qkv, far_qkv)
    output_weights = (output_weight, far_output)
    gate_up_weights = (own_gate_up, far_gate_up)
    down_weights = (down_weight, far_down)
    tiles = [bias_tiles(table.astype(f32)) for table in (position_bias, far_bias)]

    row_segments = lax.dynamic_index_in_dim(doc_segments, x, 0, keepdims=False)
    chip_keep = lax.dynamic_slice_in_dim(
        query_keep, (dp * tensor_size + x * 2) * query_local, chip_queries, 0
    ).reshape(-1)
    query_ids = jnp.arange(chip_queries * query_len, dtype=jnp.int32) // query_len + docs_row
    seg_q = jnp.concatenate([row_segments, query_ids])
    seg_k = jnp.concatenate([row_segments, jnp.where(chip_keep > 0, query_ids, -1)])
    segs = (seg_q[:, None], seg_q[None, :], seg_k[:, None], seg_k[None, :])
    blocked = row_segments.reshape(-1, BLOCK)
    low = jnp.sum((row_segments[None, :] < blocked[:, :1]).astype(jnp.int32), axis=1)
    high = jnp.sum((row_segments[None, :] <= blocked[:, -1:]).astype(jnp.int32), axis=1)
    low_block = low // BLOCK
    high_block = (high + BLOCK - 1) // BLOCK
    doc_blocks = length // BLOCK
    query_blocks = chip_queries * query_len // BLOCK
    lo = jnp.concatenate([low_block, jnp.full((query_blocks,), doc_blocks - 1, jnp.int32)])
    cnt = jnp.concatenate(
        [(high_block - low_block + 1) // 2, jnp.full((query_blocks,), 1, jnp.int32)]
    )
    ranges = (lo, cnt)

    order = [("dp", b) for b in reversed(range(bits))] + [("x", 0)]
    blocks = groups * 2

    def my_queries(values, moved=True):
        lead = values.shape[0]
        split = values.reshape(lead, blocks, 2, -1)
        mine = lax.dynamic_index_in_dim(split, core, 2, keepdims=False)
        mine = mine.reshape((lead,) + (2,) * (bits + 1) + (-1,))
        for s, (axis, b) in enumerate(order if moved else []):
            bit = x if axis == "x" else dp_bit[b]
            mine = jnp.where(bit == 0, mine, jnp.flip(mine, 1 + s))
        mine = jnp.transpose(mine, (0,) + tuple(range(bits + 1, 0, -1)) + (bits + 2,))
        return mine.reshape(lead, -1)

    row_retrieved = lax.dynamic_slice_in_dim(retrieved, x * docs_row, docs_row, 2)
    chosen = (query_keep[:, :, None] * row_retrieved).reshape(query_total * query_len, docs_row)
    chosen = my_queries(jnp.transpose(chosen.astype(f32)))
    chosen = jnp.pad(chosen, ((0, 8 - docs_row), (0, 0)))
    my_positives = my_queries(positives.reshape(1, -1), moved=False)
    half_queries = my_positives.shape[1]
    query_lanes = -(-half_queries // BLOCK) * BLOCK
    pos_rows = jnp.pad(my_positives, ((0, 7), (0, query_lanes - half_queries)), constant_values=-1)

    near_first = jnp.where(core == 0, kept_rows, near_rows)
    near_second = jnp.where(core == 0, near_rows, kept_rows)
    far_first = jnp.where(core == 0, far_rows, far_core_rows)
    far_second = jnp.where(core == 0, far_core_rows, far_rows)
    tokens = jnp.concatenate(
        [
            jnp.where(x == 0, near_first, far_first),
            jnp.where(x == 0, near_second, far_second),
            jnp.where(x == 0, far_first, near_first),
            jnp.where(x == 0, far_second, near_second),
            jnp.where(core == 0, flat_queries, near_queries),
            jnp.where(core == 0, near_queries, flat_queries),
        ],
        axis=0,
    )
    inputs = tokens.astype(f32)
    gain_attn = attn_gain.astype(f32)
    gain_ffn = ffn_gain.astype(f32)
    gain_final = final_gain.astype(f32)
    scale_attn = rms_scale(inputs)
    normed_attn = (inputs * scale_attn * gain_attn).astype(bf16)
    heads = [dot_nn(normed_attn, w).astype(bf16) for w in qkv_weights]
    attended = [attend(h, ranges, segs, t[0]) for h, t in zip(heads, tiles)]
    contexts = [a[0] for a in attended]
    logs = [a[1] for a in attended]
    attn_part = sum(dot_nn(c, w) for c, w in zip(contexts, output_weights)).astype(bf16)
    mid = inputs + (attn_part.astype(f32) + to_core(attn_part).astype(f32))
    scale_ffn = rms_scale(mid)
    normed_ffn = (mid * scale_ffn * gain_ffn).astype(bf16)
    hiddens, pulls = [], []
    for w in gate_up_weights:
        gate_up = dot_nn(normed_ffn, w)
        hidden, pull = jax.vjp(gated_unit, gate_up[:, :hidden_local], gate_up[:, hidden_local:])
        hiddens.append(hidden.astype(bf16))
        pulls.append(pull)
    ffn_part = sum(dot_nn(h, w) for h, w in zip(hiddens, down_weights)).astype(bf16)
    layer_out = mid + (ffn_part.astype(f32) + to_core(ffn_part).astype(f32))
    scale_final = rms_scale(layer_out)
    final_normed = (layer_out * scale_final * gain_final).astype(bf16)
    projected = dot_nn(final_normed, proj_weight)
    proj_scale = lax.rsqrt(jnp.sum(projected * projected, axis=-1, keepdims=True) + epsilon)
    unit_vectors = projected * proj_scale
    embedded = unit_vectors.astype(bf16)

    doc_embedded = embedded[:length]
    query_emb = part(embedded[length:], core, 2)
    for axis, b in order:
        moved = to_x(query_emb) if axis == "x" else to_dp[b](query_emb)
        query_emb = jnp.concatenate([query_emb, moved], axis=0)
    place = sum((x if axis == "x" else dp_bit[b]) << s for s, (axis, b) in enumerate(order))
    first_doc = jnp.stack([dp * doc_local + x * docs_row, place])
    seg_col = row_segments[:, None]
    sums, logits, stats = score(
        first_doc, doc_embedded, query_emb, seg_col, chosen, pos_rows, query_len, query_local, docs_row
    )
    for move in [to_x] + to_dp:
        moved = move(stats)
        top = jnp.maximum(stats[0:1], moved[0:1])
        total = stats[1:2] * jnp.exp(stats[0:1] - top) + moved[1:2] * jnp.exp(moved[0:1] - top)
        stats = jnp.concatenate([top, total, stats[2:] + moved[2:]], axis=0)
    valid = jnp.arange(query_lanes) < half_queries
    loss_sum = jnp.sum(jnp.where(valid, stats[0] + jnp.log(stats[1]) - stats[2], 0.0))
    found_sum = jnp.sum(jnp.where(valid & (stats[3] > 0.5), 1.0, 0.0))
    ends = jnp.broadcast_to(jnp.stack([loss_sum, found_sum])[:, None], (2, BLOCK))
    ends = (ends + to_core(ends)) / query_total
    loss_value = ends[0, 0]
    found_share = ends[1, 0]

    demb, dqe = score_back(
        first_doc,
        doc_embedded,
        query_emb,
        seg_col,
        chosen,
        pos_rows,
        sums,
        logits,
        stats,
        query_len,
        query_local,
        docs_row,
    )
    demb16 = demb.astype(bf16)
    doc_vector_grad = demb16.astype(f32) + to_core(demb16).astype(f32)
    for axis, b in reversed(order):
        half = dqe.shape[0] // 2
        moved = to_x(dqe[half:]) if axis == "x" else to_dp[b](dqe[half:])
        dqe = (dqe[:half].astype(f32) + moved.astype(f32)).astype(bf16)
    query_vector_grad = swapped(core, dqe, to_core(dqe)).astype(f32)
    embedded_grad = jnp.concatenate([doc_vector_grad, query_vector_grad], axis=0)

    def reduced(own, far, first=False):
        own16 = own.astype(bf16)
        acc = own16.astype(f32) + to_x(far.astype(bf16)).astype(f32)
        for b in range(bits - 1):
            acc = acc.astype(bf16)
            acc = part(acc, dp_bit[b], 2).astype(f32) + to_dp[b](
                part(acc, 1 - dp_bit[b], 2)
            ).astype(f32)
        acc = acc.astype(bf16)
        acc = (acc.astype(f32) + to_dp[bits - 1](acc).astype(f32)).astype(bf16)
        for b in reversed(range(bits - 1)):
            acc = swapped(dp_bit[b], acc, to_dp[b](acc))
        return acc.astype(f32)

    projected_grad = (
        proj_scale
        * (
            embedded_grad
            - unit_vectors * jnp.sum(embedded_grad * unit_vectors, axis=-1, keepdims=True)
        )
    ).astype(bf16)
    proj_part = part(dot_tn(final_normed, projected_grad), core, 2).astype(bf16)
    for move in [to_x] + to_dp:
        proj_part = (proj_part.astype(f32) + move(proj_part).astype(f32)).astype(bf16)
    proj_weight_grad = swapped(core, proj_part, to_core(proj_part)).astype(f32)
    final_grad = dot_nt(projected_grad, proj_weight)
    layer_out_grad, final_gain_part = rms_back(layer_out, scale_final, gain_final, final_grad)
    ffn_out_grad = layer_out_grad.astype(bf16)
    down_grads = [dot_tn(h, ffn_out_grad) for h in hiddens]
    down_weight_grad = reduced(*down_grads)
    gate_up_grads = []
    for w, pull in zip(down_weights, pulls):
        gate_grad, up_grad = pull(dot_nt(ffn_out_grad, w))
        gate_up_grads.append(jnp.concatenate([gate_grad, up_grad], axis=1).astype(bf16))
    gate_up_weight_grad = reduced(*[dot_tn(normed_ffn, g) for g in gate_up_grads])
    nf_part = sum(dot_nt(g, w) for g, w in zip(gate_up_grads, gate_up_weights)).astype(bf16)
    normed_ffn_grad = nf_part.astype(f32) + to_core(nf_part).astype(f32)
    back_ffn, ffn_gain_part = rms_back(mid, scale_ffn, gain_ffn, normed_ffn_grad)
    mid_grad = layer_out_grad + back_ffn
    attn_out_grad = mid_grad.astype(bf16)
    output_weight_grad = reduced(*[dot_tn(c, attn_out_grad) for c in contexts])
    heads_grads, bias_grads = [], []
    for k in range(2):
        context_grad = dot_nt(attn_out_grad, output_weights[k]).astype(bf16)
        heads_grad, bias_grad = attend_back(
            heads[k], context_grad, contexts[k], logs[k], ranges, segs, tiles[k][1], buckets
        )
        heads_grads.append(heads_grad)
        bias_grads.append(jnp.sum(bias_grad, axis=-1))
    projection_grad = reduced(*[dot_tn(normed_attn, g) for g in heads_grads])
    na_part = sum(dot_nt(g, w) for g, w in zip(heads_grads, qkv_weights))
    attn_gain_part = jnp.sum(na_part * inputs * scale_attn, axis=0)

    def my_tokens(values, which):
        doc_mine = jnp.concatenate(
            [
                lax.dynamic_slice_in_dim(values, which * shard_len, shard_len, 0),
                lax.dynamic_slice_in_dim(values, (which + 2) * shard_len, shard_len, 0),
                lax.dynamic_slice_in_dim(
                    values, length + which * query_local * query_len, query_local * query_len, 0
                ),
            ],
            axis=0,
        )
        return doc_mine

    na_half = my_tokens(na_part.astype(bf16), core).astype(f32) + to_core(
        my_tokens(na_part.astype(bf16), 1 - core)
    ).astype(f32)
    inputs_half = my_tokens(inputs, core)
    scale_half = my_tokens(scale_attn, core)
    weighted = na_half * gain_attn
    average = jnp.mean(weighted * inputs_half, axis=-1, keepdims=True)
    input_grad = (
        my_tokens(mid_grad, core)
        + scale_half * weighted
        - inputs_half * (scale_half * scale_half * scale_half) * average
    )
    first_half = input_grad[:shard_len]
    second_half = input_grad[shard_len : 2 * shard_len]
    stay = jnp.where(x == 0, first_half, second_half)
    leave = jnp.where(x == 0, second_half, first_half).astype(bf16)
    back = to_x(leave).astype(f32)
    doc_grad = jnp.stack([jnp.where(x == 0, stay, back), jnp.where(x == 0, back, stay)], axis=0)
    query_grad = input_grad[2 * shard_len :].reshape(query_local, query_len, width)

    lanes = BLOCK
    gains = jnp.concatenate(
        [
            (0.5 * final_gain_part).reshape(-1, lanes),
            (0.5 * ffn_gain_part).reshape(-1, lanes),
            attn_gain_part.reshape(-1, lanes),
        ],
        axis=0,
    )
    gain_rows = gains.shape[0]
    bias_rows = [jnp.pad(g, ((0, 0), (0, lanes - buckets))) for g in bias_grads]
    packet = jnp.concatenate([gains, bias_rows[0]], axis=0) + to_x(
        jnp.concatenate([gains, bias_rows[1]], axis=0)
    )
    for move in to_dp:
        packet = packet + move(packet)
    position_bias_grad = jnp.transpose(packet[gain_rows:, :buckets])
    gains = packet[:gain_rows]
    gains = (gains + to_core(gains)).reshape(3, width)

    return (
        loss_value,
        found_share,
        doc_grad,
        query_grad,
        gains[2],
        projection_grad[:, :inner],
        projection_grad[:, inner : 2 * inner],
        projection_grad[:, 2 * inner :],
        output_weight_grad,
        position_bias_grad,
        gains[1],
        gate_up_weight_grad[:, :hidden_local],
        gate_up_weight_grad[:, hidden_local:],
        down_weight_grad,
        gains[0],
        proj_weight_grad,
    )


def solution(mesh):
    placed = (
        P("dp", "mp", None),
        P(("dp", "mp"), None, None),
        P("dp", None),
        P(),
        P(None, None, "dp"),
        P(),
        P(),
        P(None, "mp"),
        P(None, "mp"),
        P(None, "mp"),
        P("mp", None),
        P(None, "mp"),
        P(),
        P(None, "mp"),
        P(None, "mp"),
        P("mp", None),
        P(),
        P(),
    )
    return jax.shard_map(
        shards,
        mesh=mesh,
        in_specs=placed,
        out_specs=(
            P(),
            P(),
            P("dp", "mp", None),
            P(("dp", "mp"), None, None),
            P(),
            P(None, "mp"),
            P(None, "mp"),
            P(None, "mp"),
            P("mp", None),
            P(None, "mp"),
            P(),
            P(None, "mp"),
            P(None, "mp"),
            P("mp", None),
            P(),
            P(),
        ),
        check_vma=False,
    )
```

```python
from functools import partial

import jax
import jax.numpy as jnp
import numpy as np
from jax import lax
from jax.experimental import pallas as pl
from jax.experimental.pallas import tpu as pltpu
from jax.sharding import PartitionSpec as P

epsilon = 1e-06
sharpness = 16.0
smoothing_divisor = 0.05
masked_score = -1e30
BLOCK = 128
PAIR = 2 * BLOCK
bf16 = jnp.bfloat16
f32 = jnp.float32


def bucket_starts(buckets):
    half = buckets // 2
    exact = half // 2
    distance = np.arange(0, 2048)
    scaled = (
        np.log(np.maximum(distance, 1) / exact) / np.log(128.0 / exact) * (half - exact)
    )
    far = np.minimum(exact + np.floor(np.maximum(scaled, 0.0)), half - 1)
    bucket = np.where(distance < exact, distance, far)
    return [int(np.argmax(bucket >= b)) for b in range(half)]


def dot_nn(a, b):
    return lax.dot_general(a, b, (((1,), (0,)), ((), ())), preferred_element_type=f32)


def dot_nt(a, b):
    return lax.dot_general(a, b, (((1,), (1,)), ((), ())), preferred_element_type=f32)


def dot_tn(a, b):
    return lax.dot_general(a, b, (((0,), (0,)), ((), ())), preferred_element_type=f32)


def dot_exact(a, b):
    return lax.dot_general(
        a, b, (((1,), (0,)), ((), ())), precision=lax.Precision.HIGHEST, preferred_element_type=f32
    )


def params(limit_mib=40):
    return pltpu.CompilerParams(vmem_limit_bytes=limit_mib << 20)


def cost(micros):
    return pl.CostEstimate(flops=int(micros * 3e9), transcendentals=0, bytes_accessed=1 << 10)


def bias_kernel(starts, heads, tab_ref, t_ref, tt_ref):
    half = len(starts)
    sub = lax.broadcasted_iota(jnp.int32, (BLOCK, BLOCK), 0)
    lane = lax.broadcasted_iota(jnp.int32, (BLOCK, BLOCK), 1)
    for ref, base in ((t_ref, lane - sub), (tt_ref, sub - lane)):
        for d in (-1, 0, 1):
            offset = base + BLOCK * d
            n = jnp.abs(offset)
            for h in range(heads):
                low = high = None
                if d <= 0:
                    low = jnp.full((BLOCK, BLOCK), tab_ref[0, h], f32)
                    for b in range(1, half):
                        low = jnp.where(n >= starts[b], tab_ref[b, h], low)
                if d >= 0:
                    high = jnp.full((BLOCK, BLOCK), tab_ref[half, h], f32)
                    for b in range(1, half):
                        high = jnp.where(n >= starts[b], tab_ref[half + b, h], high)
                if d < 0:
                    tile = low
                elif d > 0:
                    tile = high
                else:
                    tile = jnp.where(offset > 0, high, low)
                ref[h, d + 2] = tile
        for h in range(heads):
            ref[h, 0] = jnp.full((BLOCK, BLOCK), tab_ref[half - 1, h], f32)
            ref[h, 4] = jnp.full((BLOCK, BLOCK), tab_ref[2 * half - 1, h], f32)


def bias_tiles(table):
    buckets, heads = table.shape
    starts = bucket_starts(buckets)
    shape = jax.ShapeDtypeStruct((heads, 5, BLOCK, BLOCK), f32)
    return pl.pallas_call(
        partial(bias_kernel, starts, heads),
        in_specs=[pl.BlockSpec(memory_space=pltpu.SMEM)],
        out_shape=(shape, shape),
        compiler_params=params(6),
        cost_estimate=cost(2),
        name="bias_tiles",
    )(table)


def clipped(d):
    return jnp.minimum(jnp.maximum(d, -2), 2) + 2


def attend_kernel(heads, size, most, lo_ref, cnt_ref, qkv_ref, segq_ref, segk_ref, t_ref, ctx_ref, lse_ref, k_s, v_s):
    b = pl.program_id(0)
    inner = heads * size
    last = pl.num_programs(0) - 1

    @pl.when(b == 0)
    def _():
        for h in range(heads):
            k_s[h] = qkv_ref[:, inner + h * size : inner + (h + 1) * size]
            v_s[h] = qkv_ref[:, 2 * inner + h * size : 2 * inner + (h + 1) * size]

    def window(first, count, lo, pairs):
        rows = pl.ds(pl.multiple_of(first * BLOCK, BLOCK), count * BLOCK)
        block = qkv_ref[rows, :inner]
        seg_col = segq_ref[rows, :]
        spans = [pl.ds(pl.multiple_of((lo + 2 * i) * BLOCK, BLOCK), PAIR) for i in range(pairs)]
        allowed = [seg_col == segk_ref[:, span] for span in spans]
        outs, logs = [], []
        for h in range(heads):
            query = block[:, h * size : (h + 1) * size]
            scores = []
            for i, span in enumerate(spans):
                s = dot_nt(query, k_s[h, span, :])
                bias = jnp.concatenate(
                    [
                        jnp.concatenate(
                            [t_ref[h, clipped(lo + 2 * i + c - first - r)] for c in range(2)], axis=1
                        )
                        for r in range(count)
                    ],
                    axis=0,
                )
                scores.append(jnp.where(allowed[i], s + bias, masked_score))
            top = scores[0]
            for s in scores[1:]:
                top = jnp.maximum(top, s)
            largest = jnp.max(top, axis=1, keepdims=True)
            total = acc = None
            for i, span in enumerate(spans):
                p = jnp.exp(scores[i] - largest)
                total = p if total is None else total + p
                more = dot_nn(p.astype(bf16), v_s[h, span, :])
                acc = more if acc is None else acc + more
            total = jnp.sum(total, axis=1, keepdims=True)
            outs.append((acc / total).astype(bf16))
            lse = jnp.broadcast_to(largest + jnp.log(total), (count * BLOCK, BLOCK))
            lse_ref[h : h + 1, rows] = jnp.transpose(lse)[0:1, :]
        ctx_ref[rows, :] = jnp.concatenate(outs, axis=1)

    for pairs in range(1, most + 1):
        pl.when((b < last) & (cnt_ref[b] == pairs))(partial(window, 2 * b, 2, lo_ref[b], pairs))
    pl.when(b == last)(partial(window, 2 * b, 1, lo_ref[b], 1))


def attend(qkv, ranges, segs, tiles):
    lo, cnt = ranges
    segq_col, segq_row, segk_col, segk_row = segs
    total, wide = qkv.shape
    heads = tiles.shape[0]
    inner = wide // 3
    size = inner // heads
    steps = lo.shape[0]
    whole = lambda b, *_: (0, 0)
    return pl.pallas_call(
        partial(attend_kernel, heads, size, steps - 1),
        grid_spec=pltpu.PrefetchScalarGridSpec(
            num_scalar_prefetch=2,
            grid=(steps,),
            in_specs=[
                pl.BlockSpec((total, wide), whole, pipeline_mode=pl.Buffered(1)),
                pl.BlockSpec((total, 1), whole, pipeline_mode=pl.Buffered(1)),
                pl.BlockSpec((1, total), whole, pipeline_mode=pl.Buffered(1)),
                pl.BlockSpec((heads, 5, BLOCK, BLOCK), lambda b, *_: (0, 0, 0, 0), pipeline_mode=pl.Buffered(1)),
            ],
            out_specs=[
                pl.BlockSpec((total, inner), whole),
                pl.BlockSpec((8, total), whole),
            ],
            scratch_shapes=[
                pltpu.VMEM((heads, total, size), bf16),
                pltpu.VMEM((heads, total, size), bf16),
            ],
        ),
        out_shape=(
            jax.ShapeDtypeStruct((total, inner), bf16),
            jax.ShapeDtypeStruct((8, total), f32),
        ),
        compiler_params=params(12),
        cost_estimate=cost(9),
        name="attend",
    )(lo, cnt, qkv, segq_col, segk_row, tiles)


def attend_back_kernel(
    starts,
    heads,
    size,
    most,
    lo_ref,
    cnt_ref,
    qkv_ref,
    do_ref,
    ctx_ref,
    lse_ref,
    segk_ref,
    segq_ref,
    tt_ref,
    grad_ref,
    bias_ref,
    q_s,
    do_s,
    dq_s,
    delta_s,
    d_s,
):
    b = pl.program_id(0)
    last = pl.num_programs(0) - 1
    inner = heads * size
    half = len(starts)

    @pl.when(b == 0)
    def _():
        prod = do_ref[...].astype(f32) * ctx_ref[...].astype(f32)
        high = prod.astype(bf16)
        low = (prod - high.astype(f32)).astype(bf16)
        row = lax.broadcasted_iota(jnp.int32, (8, inner), 0)
        col = lax.broadcasted_iota(jnp.int32, (8, inner), 1)
        pick = ((col >= row * size) & (col < (row + 1) * size)).astype(f32).astype(bf16)
        delta_s[...] = dot_nt(pick, high) + dot_nt(pick, low)
        for h in range(heads):
            q_s[h] = qkv_ref[:, h * size : (h + 1) * size]
            do_s[h] = do_ref[:, h * size : (h + 1) * size]
        dq_s[...] = jnp.zeros(dq_s.shape, f32)
        d_s[...] = jnp.zeros(d_s.shape, f32)

    def window(first, count, lo, pairs):
        rows = pl.ds(pl.multiple_of(first * BLOCK, BLOCK), count * BLOCK)
        block = qkv_ref[rows, inner:]
        seg_col = segk_ref[rows, :]
        spans = [pl.ds(pl.multiple_of((lo + 2 * i) * BLOCK, BLOCK), PAIR) for i in range(pairs)]
        allowed = [seg_col == segq_ref[:, span] for span in spans]
        dks, dvs = [], []
        for h in range(heads):
            key = block[:, h * size : (h + 1) * size]
            value = block[:, inner + h * size : inner + (h + 1) * size]
            dk = dv = None
            for i, span in enumerate(spans):
                q = q_s[h, span, :]
                do = do_s[h, span, :]
                s = dot_nt(key, q)
                dp = dot_nt(value, do)
                at = [[clipped(first + r - lo - 2 * i - c) for c in range(2)] for r in range(count)]
                bias = jnp.concatenate(
                    [
                        jnp.concatenate([tt_ref[h, at[r][c]] for c in range(2)], axis=1)
                        for r in range(count)
                    ],
                    axis=0,
                )
                p = jnp.where(allowed[i], jnp.exp(s + bias - lse_ref[h : h + 1, span]), 0.0)
                ds = p * (dp - delta_s[h : h + 1, span])
                for r in range(count):
                    for c in range(2):
                        d_s[h, at[r][c]] += ds[
                            r * BLOCK : (r + 1) * BLOCK, c * BLOCK : (c + 1) * BLOCK
                        ]
                ds16 = ds.astype(bf16)
                dv_more = dot_nn(p.astype(bf16), do)
                dk_more = dot_nn(ds16, q)
                dv = dv_more if dv is None else dv + dv_more
                dk = dk_more if dk is None else dk + dk_more
                dq_s[h, :, span] += dot_tn(key, ds16)
            dks.append(dk)
            dvs.append(dv)
        grad_ref[rows, inner:] = jnp.concatenate(dks + dvs, axis=1).astype(bf16)

    for pairs in range(1, most + 1):
        pl.when((b < last) & (cnt_ref[b] == pairs))(partial(window, 2 * b, 2, lo_ref[b], pairs))
    pl.when(b == last)(partial(window, 2 * b, 1, lo_ref[b], 1))

    @pl.when(b == last)
    def _():
        grad_ref[:, :inner] = jnp.concatenate([jnp.transpose(dq_s[h]) for h in range(heads)], axis=1).astype(bf16)
        sub = lax.broadcasted_iota(jnp.int32, (BLOCK, BLOCK), 0)
        lane = lax.broadcasted_iota(jnp.int32, (BLOCK, BLOCK), 1)
        below = lane + sub > BLOCK - 1
        reverse = (lane + sub == BLOCK - 1).astype(f32)
        bucket_row = lax.broadcasted_iota(jnp.int32, (2 * half, BLOCK), 0)
        line_lane = lax.broadcasted_iota(jnp.int32, (2 * half, BLOCK), 1)
        picks = {}
        for d in (-1, 0, 1):
            for low in (False, True):
                offset = line_lane + (1 if low else 1 - BLOCK) + BLOCK * d
                n = jnp.abs(offset)
                bucket = jnp.where(offset > 0, half, 0)
                for e in range(1, half):
                    bucket = bucket + (n >= starts[e]).astype(jnp.int32)
                picks[d, low] = bucket == bucket_row
        for h in range(heads):
            whole = jnp.zeros((2 * half, BLOCK), f32)
            for d in (-1, 0, 1):
                tile = dot_exact(d_s[h, d + 2], reverse)
                for low in (False, True):
                    kept = jnp.where(below == low, tile, 0.0)
                    line = jnp.sum(
                        pltpu.roll(kept, 0, 1, stride=1, stride_axis=0), axis=0, keepdims=True
                    )
                    whole = whole + jnp.where(picks[d, low], line, 0.0)
            for e, d in ((half - 1, 0), (2 * half - 1, 4)):
                far = jnp.sum(d_s[h, d], axis=0, keepdims=True)
                whole = whole + jnp.where(bucket_row == e, far, 0.0)
            bias_ref[h] = whole


def attend_back(qkv, context_grad, context, lse, ranges, segs, tiles, buckets):
    lo, cnt = ranges
    segq_col, segq_row, segk_col, segk_row = segs
    total, wide = qkv.shape
    heads = tiles.shape[0]
    inner = wide // 3
    size = inner // heads
    steps = lo.shape[0]
    starts = bucket_starts(buckets)
    whole = lambda b, *_: (0, 0)
    return pl.pallas_call(
        partial(attend_back_kernel, starts, heads, size, steps - 1),
        grid_spec=pltpu.PrefetchScalarGridSpec(
            num_scalar_prefetch=2,
            grid=(steps,),
            in_specs=[
                pl.BlockSpec((total, wide), whole, pipeline_mode=pl.Buffered(1)),
                pl.BlockSpec((total, inner), whole, pipeline_mode=pl.Buffered(1)),
                pl.BlockSpec((total, inner), whole, pipeline_mode=pl.Buffered(1)),
                pl.BlockSpec((8, total), whole, pipeline_mode=pl.Buffered(1)),
                pl.BlockSpec((total, 1), whole, pipeline_mode=pl.Buffered(1)),
                pl.BlockSpec((1, total), whole, pipeline_mode=pl.Buffered(1)),
                pl.BlockSpec((heads, 5, BLOCK, BLOCK), lambda b, *_: (0, 0, 0, 0), pipeline_mode=pl.Buffered(1)),
            ],
            out_specs=[
                pl.BlockSpec((total, wide), whole),
                pl.BlockSpec((heads, buckets, BLOCK), lambda b, *_: (0, 0, 0)),
            ],
            scratch_shapes=[
                pltpu.VMEM((heads, total, size), bf16),
                pltpu.VMEM((heads, total, size), bf16),
                pltpu.VMEM((heads, size, total), f32),
                pltpu.VMEM((8, total), f32),
                pltpu.VMEM((heads, 5, BLOCK, BLOCK), f32),
            ],
        ),
        out_shape=(
            jax.ShapeDtypeStruct((total, wide), bf16),
            jax.ShapeDtypeStruct((heads, buckets, BLOCK), f32),
        ),
        compiler_params=params(16),
        cost_estimate=cost(15),
        name="attend_back",
    )(lo, cnt, qkv, context_grad, context, lse, segk_col, segq_row, tiles)


def pool_matrix(shape, axis, me, query_len, query_local):
    token = lax.broadcasted_iota(jnp.int32, shape, axis)
    query = lax.broadcasted_iota(jnp.int32, shape, 1 - axis)
    span = query_len * query_local
    holder = jnp.bitwise_xor(token // span, me)
    return (holder * query_local + token % span // query_len == query).astype(f32)


def score_kernel(query_len, query_local, docs, first_ref, emb_ref, qe_ref, seg_ref, chosen_ref, pos_ref, sums_ref, logit_ref, stat_ref, acc_s):
    b = pl.program_id(0)
    count = qe_ref.shape[0]

    @pl.when(b == 0)
    def _():
        acc_s[...] = jnp.zeros(acc_s.shape, f32)

    near = jnp.exp(sharpness * (dot_nt(emb_ref[...], qe_ref[...]) - 1.0))
    seg = seg_ref[...]
    for d in range(docs):
        acc_s[d : d + 1, :] += jnp.sum(jnp.where(seg == d, near, 0.0), axis=0, keepdims=True)

    @pl.when(b == pl.num_programs(0) - 1)
    def _():
        sums = acc_s[:docs, :]
        sums_ref[...] = acc_s[...]
        chosen = chosen_ref[:docs, :]
        smooth = 1.0 + jnp.log(sums) / sharpness
        pool = pool_matrix((count, pos_ref.shape[1]), 0, first_ref[1], query_len, query_local)
        picked = dot_exact(chosen * smooth, pool)
        counts = dot_exact(chosen, pool)
        logits = picked / jnp.maximum(counts, 1.0) / smoothing_divisor
        top = jnp.max(logits, axis=0, keepdims=True)
        spread = jnp.sum(jnp.exp(logits - top), axis=0, keepdims=True)
        doc = lax.broadcasted_iota(jnp.int32, logits.shape, 0) + first_ref[0]
        mine = doc == pos_ref[0:1, :]
        stat_ref[0:1, :] = top
        stat_ref[1:2, :] = spread
        stat_ref[2:3, :] = jnp.sum(jnp.where(mine, logits, 0.0), axis=0, keepdims=True)
        stat_ref[3:4, :] = jnp.sum(jnp.where(mine, counts, 0.0), axis=0, keepdims=True)
        stat_ref[4:8, :] = jnp.zeros((4, pos_ref.shape[1]), f32)
        logit_ref[0:docs, :] = logits
        logit_ref[docs : 2 * docs, :] = counts


def score(first, emb, query_emb, seg_col, chosen, positives, query_len, query_local, docs):
    count, width = query_emb.shape
    lanes = positives.shape[1]
    length = emb.shape[0]
    blocks = length // BLOCK
    whole = lambda b, *_: (0, 0)
    return pl.pallas_call(
        partial(score_kernel, query_len, query_local, docs),
        grid_spec=pltpu.PrefetchScalarGridSpec(
            num_scalar_prefetch=1,
            grid=(blocks,),
            in_specs=[
                pl.BlockSpec((BLOCK, width), lambda b, *_: (b, 0)),
                pl.BlockSpec((count, width), whole, pipeline_mode=pl.Buffered(1)),
                pl.BlockSpec((BLOCK, 1), lambda b, *_: (b, 0)),
                pl.BlockSpec((8, count), whole, pipeline_mode=pl.Buffered(1)),
                pl.BlockSpec((8, lanes), whole, pipeline_mode=pl.Buffered(1)),
            ],
            out_specs=[
                pl.BlockSpec((8, count), whole),
                pl.BlockSpec((8, lanes), whole),
                pl.BlockSpec((8, lanes), whole),
            ],
            scratch_shapes=[pltpu.VMEM((8, count), f32)],
        ),
        out_shape=(
            jax.ShapeDtypeStruct((8, count), f32),
            jax.ShapeDtypeStruct((8, lanes), f32),
            jax.ShapeDtypeStruct((8, lanes), f32),
        ),
        compiler_params=params(10),
        cost_estimate=cost(5),
        name="score",
    )(first, emb, query_emb, seg_col, chosen, positives)


def score_back_kernel(query_len, query_local, docs, first_ref, emb_ref, qe_ref, seg_ref, chosen_ref, pos_ref, sums_ref, logit_ref, stat_ref, demb_ref, dqe_ref, grad_s, dq_s):
    b = pl.program_id(0)
    count = qe_ref.shape[0]

    @pl.when(b == 0)
    def _():
        logits = logit_ref[0:docs, :]
        counts = logit_ref[docs : 2 * docs, :]
        doc = lax.broadcasted_iota(jnp.int32, logits.shape, 0) + first_ref[0]
        mine = (doc == pos_ref[0:1, :]).astype(f32)
        share = jnp.exp(logits - stat_ref[0:1, :]) / stat_ref[1:2, :]
        grad = (share - mine) / smoothing_divisor / jnp.maximum(counts, 1.0)
        spread = pool_matrix((logits.shape[1], count), 1, first_ref[1], query_len, query_local)
        grad_s[0:docs, :] = dot_exact(grad, spread) * chosen_ref[:docs, :] / sums_ref[:docs, :]
        dq_s[...] = jnp.zeros(dq_s.shape, f32)

    emb = emb_ref[...]
    near = jnp.exp(sharpness * (dot_nt(emb, qe_ref[...]) - 1.0))
    seg = seg_ref[...]
    weight = jnp.broadcast_to(grad_s[0:1, :], near.shape)
    for d in range(1, docs):
        weight = jnp.where(seg == d, grad_s[d : d + 1, :], weight)
    grad = (near * weight).astype(bf16)
    demb_ref[...] = dot_nn(grad, qe_ref[...])
    dq_s[...] += dot_tn(emb, grad)

    @pl.when(b == pl.num_programs(0) - 1)
    def _():
        dqe_ref[...] = jnp.transpose(dq_s[...]).astype(bf16)


def score_back(first, emb, query_emb, seg_col, chosen, positives, sums, logits, stats, query_len, query_local, docs):
    count, width = query_emb.shape
    lanes = positives.shape[1]
    length = emb.shape[0]
    blocks = length // BLOCK
    whole = lambda b, *_: (0, 0)
    return pl.pallas_call(
        partial(score_back_kernel, query_len, query_local, docs),
        grid_spec=pltpu.PrefetchScalarGridSpec(
            num_scalar_prefetch=1,
            grid=(blocks,),
            in_specs=[
                pl.BlockSpec((BLOCK, width), lambda b, *_: (b, 0)),
                pl.BlockSpec((count, width), whole, pipeline_mode=pl.Buffered(1)),
                pl.BlockSpec((BLOCK, 1), lambda b, *_: (b, 0)),
                pl.BlockSpec((8, count), whole, pipeline_mode=pl.Buffered(1)),
                pl.BlockSpec((8, lanes), whole, pipeline_mode=pl.Buffered(1)),
                pl.BlockSpec((8, count), whole, pipeline_mode=pl.Buffered(1)),
                pl.BlockSpec((8, lanes), whole, pipeline_mode=pl.Buffered(1)),
                pl.BlockSpec((8, lanes), whole, pipeline_mode=pl.Buffered(1)),
            ],
            out_specs=[
                pl.BlockSpec((BLOCK, width), lambda b, *_: (b, 0)),
                pl.BlockSpec((count, width), whole),
            ],
            scratch_shapes=[pltpu.VMEM((8, count), f32), pltpu.VMEM((width, count), f32)],
        ),
        out_shape=(
            jax.ShapeDtypeStruct((length, width), f32),
            jax.ShapeDtypeStruct((count, width), bf16),
        ),
        compiler_params=params(12),
        cost_estimate=cost(5),
        name="score_back",
    )(first, emb, query_emb, seg_col, chosen, positives, sums, logits, stats)


def full(*shape):
    return pl.BlockSpec(shape, lambda *_: (0,) * len(shape), pipeline_mode=pl.Buffered(1))


def kept(*shape):
    return pl.BlockSpec(shape, lambda *_: (0,) * len(shape))


def rows_of(count, width):
    return pl.BlockSpec((count, width), lambda b, *_: (b, 0))


SCALARS = pl.BlockSpec(memory_space=pltpu.SMEM)


def like(shape, dtype):
    return jax.ShapeDtypeStruct(shape, dtype)


def rms(values):
    return lax.rsqrt(jnp.mean(values * values, axis=-1, keepdims=True) + epsilon)


def choose_kernel(query_local, query_len, steps, place_ref, pos_ref, ret_ref, segq_ref, segk_ref, chosen_ref, rows_ref, colq_ref, colk_ref, ret_s):
    core, me = place_ref[0], place_ref[1]
    span = query_local * query_len
    blocks = ret_s.shape[0] // span

    def holder(p):
        return sum(((p >> s) & 1) << (steps - 1 - s) for s in range(steps))

    def held(p):
        return holder(jnp.bitwise_xor(me, p)) * 2 + core

    for p in range(blocks):
        start = pl.multiple_of(held(p) * span, span)
        ret_s[p * span : (p + 1) * span, :] = ret_ref[pl.ds(start, span), :].astype(f32)
    docs = ret_s.shape[1]
    row = lax.broadcasted_iota(jnp.int32, (docs, docs), 0)
    col = lax.broadcasted_iota(jnp.int32, (docs, docs), 1)
    shift = jnp.where(row < docs // 2, row + place_ref[2], -1)
    chosen_ref[...] = dot_nt((shift == col).astype(f32), ret_s[...])
    lane = lax.broadcasted_iota(jnp.int32, rows_ref.shape, 1)
    rows = jnp.full(rows_ref.shape, -1, jnp.int32)
    for p in range(blocks):
        for i in range(query_local):
            query = (holder(p) * 2 + core) * query_local + i
            rows = jnp.where(lane == p * query_local + i, pos_ref[query], rows)
    rows_ref[...] = rows
    for row_ref, col_ref in ((segq_ref, colq_ref), (segk_ref, colk_ref)):
        whole = jnp.broadcast_to(row_ref[...], (8, row_ref.shape[1]))
        col_ref[...] = jnp.transpose(whole)[:, 0:1]


def choose(place, positives, retrieved, seg_q, seg_k, query_local, query_len, steps):
    total, docs = retrieved.shape
    lanes = -(-(total // 2 // query_len) // BLOCK) * BLOCK
    tokens = seg_q.shape[1]
    return pl.pallas_call(
        partial(choose_kernel, query_local, query_len, steps),
        in_specs=[SCALARS, SCALARS] + [pl.BlockSpec(memory_space=pltpu.VMEM)] * 3,
        out_shape=(
            like((8, total // 2), f32),
            like((8, lanes), jnp.int32),
            like((tokens, 1), jnp.int32),
            like((tokens, 1), jnp.int32),
        ),
        scratch_shapes=[pltpu.VMEM((total // 2, docs), f32)],
        compiler_params=params(10),
        cost_estimate=cost(1),
        name="choose",
    )(place, positives, retrieved, seg_q, seg_k)


def pack_kernel(bit_ref, q_ref, k_ref, v_ref, o_ref, g_ref, u_ref, d_ref, b_ref, qkv_ref, half_qkv, half_o, half_gu, half_d):
    inner = q_ref.shape[1]
    hidden = g_ref.shape[1]
    for i, ref in enumerate((q_ref, k_ref, v_ref)):
        qkv_ref[:, i * inner : (i + 1) * inner] = ref[...]
    bit = bit_ref[0]
    rows = half_qkv.shape[0]
    span = pl.ds(pl.multiple_of(bit * rows, rows), rows)
    half_qkv[...] = qkv_ref[span, :]
    half_gu[:, :hidden] = g_ref[span, :]
    other = pl.ds(pl.multiple_of(bit_ref[1] * rows, rows), rows)
    half_gu[:, hidden:] = u_ref[other, :]
    rows = o_ref.shape[0] // 2
    half_o[:rows, :] = o_ref[pl.ds(pl.multiple_of(bit * rows, rows), rows), :]
    half_o[rows:, :] = jnp.zeros((half_o.shape[0] - rows, half_o.shape[1]), bf16)
    half_o[rows:, : b_ref.shape[1]] = b_ref[...]
    rows = half_d.shape[0]
    half_d[...] = d_ref[pl.ds(pl.multiple_of(bit * rows, rows), rows), :]


def pack(bit, q, k, v, o, gate, up, down, bias):
    depth, inner = q.shape
    hidden = gate.shape[1]
    return pl.pallas_call(
        pack_kernel,
        in_specs=[SCALARS] + [pl.BlockSpec(memory_space=pltpu.VMEM)] * 8,
        out_shape=(
            like((depth, 3 * inner), bf16),
            like((depth // 2, 3 * inner), bf16),
            like((inner // 2 + bias.shape[0], depth), bf16),
            like((depth // 2, 2 * hidden), bf16),
            like((hidden // 2, depth), bf16),
        ),
        compiler_params=params(12),
        cost_estimate=cost(1),
        name="pack",
    )(bit, q, k, v, o, gate, up, down, bias)


def enter_kernel(place_ref, kept_ref, near_ref, far_ref, cross_ref, gain_ref, w_ref, tok_ref, norm_ref, heads_ref):
    gain = gain_ref[...].astype(f32)
    mp = place_ref[0]
    shard = far_ref.shape[0]
    query = kept_ref.shape[0] - shard
    pieces = [(kept_ref, 0), (near_ref, 1), (far_ref, 2), (cross_ref, 3)]
    spans = [(ref, 0, shard, jnp.bitwise_xor(mp, i) * shard) for ref, i in pieces]
    spans += [
        (ref, shard, query, 4 * shard + jnp.bitwise_xor(mp % 2, i) * query) for ref, i in pieces[:2]
    ]
    for ref, first, count, start in spans:
        rows = pl.ds(pl.multiple_of(start, count), count)
        piece = ref[first : first + count, :]
        values = piece.astype(f32)
        normed = (values * rms(values) * gain).astype(bf16)
        tok_ref[rows, :] = piece
        norm_ref[rows, :] = normed
        heads_ref[rows, :] = dot_nn(normed, w_ref[...]).astype(bf16)


def enter(place, pieces, gain, weight):
    total = sum(piece.shape[0] for piece in pieces)
    depth, wide = weight.shape
    return pl.pallas_call(
        enter_kernel,
        in_specs=[SCALARS] + [pl.BlockSpec(memory_space=pltpu.VMEM)] * 6,
        out_shape=(like((total, depth), bf16), like((total, depth), bf16), like((total, wide), bf16)),
        compiler_params=params(12),
        cost_estimate=cost(3),
        name="enter",
    )(place, *pieces, gain, weight)


def gelu_parts(gate):
    inner = 0.7978845608028654 * (gate + 0.044715 * gate * gate * gate)
    return 0.5 * (1.0 + jnp.tanh(inner))


def ffn_own_kernel(tok_ref, near_ref, moved_ref, gain_ref, g_ref, u_ref, d_ref, mid_ref, norm_ref, gu_ref, part_ref):
    hidden = g_ref.shape[1]
    mid = tok_ref[...].astype(f32) + (near_ref[...].astype(f32) + moved_ref[...].astype(f32))
    mid_ref[...] = mid
    normed = (mid * rms(mid) * gain_ref[...].astype(f32)).astype(bf16)
    norm_ref[...] = normed
    gate = dot_nn(normed, g_ref[...])
    up = dot_nn(normed, u_ref[...])
    gu_ref[:, :hidden] = gate.astype(bf16)
    gu_ref[:, hidden:] = up.astype(bf16)
    part_ref[...] = dot_nn((gate * gelu_parts(gate) * up).astype(bf16), d_ref[...])


def ffn_own(tokens, near, moved, gain, gate, up, down, count):
    total, depth = tokens.shape
    hidden = gate.shape[1]
    return pl.pallas_call(
        ffn_own_kernel,
        grid=(total // count,),
        in_specs=[rows_of(count, depth)] * 3
        + [full(1, depth), full(depth, hidden), full(depth, hidden), full(hidden, depth)],
        out_specs=[
            rows_of(count, depth),
            rows_of(count, depth),
            rows_of(count, 2 * hidden),
            rows_of(count, depth),
        ],
        out_shape=(
            like((total, depth), f32),
            like((total, depth), bf16),
            like((total, 2 * hidden), bf16),
            like((total, depth), f32),
        ),
        compiler_params=params(16),
        cost_estimate=cost(5),
        name="ffn_own",
    )(tokens, near, moved, gain, gate, up, down)


def ffn_far_kernel(norm_ref, g_ref, u_ref, d_ref, part_ref, gu_ref, out_ref):
    hidden = d_ref.shape[0]
    normed = norm_ref[...]
    gate = dot_nn(normed, g_ref[...])
    up = dot_nn(normed, u_ref[...])
    gu_ref[:, :hidden] = gate.astype(bf16)
    gu_ref[:, hidden:] = up.astype(bf16)
    more = dot_nn((gate * gelu_parts(gate) * up).astype(bf16), d_ref[...])
    out_ref[...] = (part_ref[...] + more).astype(bf16)


def ffn_far(normed, gate, up, down, partial_sum, count):
    total, depth = normed.shape
    hidden = down.shape[0]
    return pl.pallas_call(
        ffn_far_kernel,
        grid=(total // count,),
        in_specs=[
            rows_of(count, depth),
            full(depth, hidden),
            full(depth, hidden),
            full(hidden, depth),
            rows_of(count, depth),
        ],
        out_specs=[rows_of(count, 2 * hidden), rows_of(count, depth)],
        out_shape=(like((total, 2 * hidden), bf16), like((total, depth), bf16)),
        compiler_params=params(14),
        cost_estimate=cost(5),
        name="ffn_far",
    )(normed, gate, up, down, partial_sum)


def leave_kernel(mid_ref, near_ref, moved_ref, gain_ref, w_ref, out_ref, proj_ref, emb_ref):
    out = mid_ref[...] + (near_ref[...].astype(f32) + moved_ref[...].astype(f32))
    out_ref[...] = out
    normed = (out * rms(out) * gain_ref[...].astype(f32)).astype(bf16)
    projected = dot_nn(normed, w_ref[...])
    proj_ref[...] = projected
    scale = lax.rsqrt(jnp.sum(projected * projected, axis=-1, keepdims=True) + epsilon)
    emb_ref[...] = (projected * scale).astype(bf16)


def leave(mid, near, moved, gain, weight, count):
    total, depth = mid.shape
    wide = weight.shape[1]
    return pl.pallas_call(
        leave_kernel,
        grid=(total // count,),
        in_specs=[rows_of(count, depth)] * 3 + [full(1, depth), full(depth, wide)],
        out_specs=[rows_of(count, depth), rows_of(count, wide), rows_of(count, wide)],
        out_shape=(like((total, depth), f32), like((total, wide), f32), like((total, wide), bf16)),
        compiler_params=params(10),
        cost_estimate=cost(4),
        name="leave",
    )(mid, near, moved, gain, weight)


def norm_back(values, gain, gradient):
    scale = rms(values)
    weighted = gradient * gain
    average = jnp.mean(weighted * values, axis=-1, keepdims=True)
    back = scale * weighted - values * (scale * scale * scale) * average
    return back, gradient * values * scale


def leave_back_kernel(core_ref, out_ref, proj_ref, near_ref, moved_ref, qn_ref, qm_ref, gain_ref, w_ref, grad_ref, wg_ref, gg_ref, emb_s):
    b = pl.program_id(0)
    last = pl.num_programs(0) - 1

    @pl.when(b == 0)
    def _():
        wg_ref[...] = jnp.zeros(wg_ref.shape, f32)
        gg_ref[...] = jnp.zeros(gg_ref.shape, f32)

    @pl.when(b < last)
    def _():
        emb_s[...] = near_ref[...] + moved_ref[...].astype(f32)

    @pl.when(b == last)
    def _():
        half = qn_ref.shape[0]
        core = core_ref[0]
        emb_s[pl.ds(pl.multiple_of(core * half, half), half), :] = qn_ref[...].astype(f32)
        emb_s[pl.ds(pl.multiple_of((1 - core) * half, half), half), :] = qm_ref[...].astype(f32)

    projected = proj_ref[...]
    scale = lax.rsqrt(jnp.sum(projected * projected, axis=-1, keepdims=True) + epsilon)
    unit = projected * scale
    grad = emb_s[...]
    grad = (scale * (grad - unit * jnp.sum(grad * unit, axis=-1, keepdims=True))).astype(bf16)
    out = out_ref[...]
    gain = gain_ref[...].astype(f32)
    normed = (out * rms(out) * gain).astype(bf16)
    wg_ref[...] += dot_tn(normed, grad)
    back, addends = norm_back(out, gain, dot_nt(grad, w_ref[...]))
    grad_ref[...] = back
    gg_ref[0:1, :] += jnp.sum(addends, axis=0, keepdims=True)


def leave_back(core, layer_out, projected, near, moved, query_near, query_moved, gain, weight):
    total, depth = layer_out.shape
    wide = weight.shape[1]
    count = total - near.shape[0]
    steps = total // count
    clamp = pl.BlockSpec((count, wide), lambda b, *_: (jnp.minimum(b, steps - 2), 0))
    return pl.pallas_call(
        leave_back_kernel,
        grid=(steps,),
        in_specs=[
            SCALARS,
            rows_of(count, depth),
            rows_of(count, wide),
            clamp,
            clamp,
            full(count // 2, wide),
            full(count // 2, wide),
            full(1, depth),
            full(depth, wide),
        ],
        out_specs=[rows_of(count, depth), kept(depth, wide), kept(8, depth)],
        out_shape=(like((total, depth), f32), like((depth, wide), f32), like((8, depth), f32)),
        scratch_shapes=[pltpu.VMEM((count, wide), f32)],
        compiler_params=params(8),
        cost_estimate=cost(5),
        name="leave_back",
    )(core, layer_out, projected, near, moved, query_near, query_moved, gain, weight)


def ffn_back_kernel(hidden, own, *refs):
    gate_s, up_s, down_s = refs[-3:]
    if own:
        index_ref, grad_ref, norm_ref, gu_ref, d_ref, g_ref, u_ref, part_in, down_in = refs[:9]
        nf_ref, a_ref, b_ref, *downs = refs[9:-3]
    else:
        grad_ref, norm_ref, gu_ref, d_ref, g_ref, u_ref, nf_ref, a_ref, b_ref, down_ref = refs[:-3]
    b = pl.program_id(0)

    @pl.when(b == 0)
    def _():
        gate_s[...] = jnp.zeros(gate_s.shape, f32)
        up_s[...] = jnp.zeros(up_s.shape, f32)
        down_s[...] = jnp.zeros(down_s.shape, f32)

    grad = grad_ref[...].astype(bf16)
    gate = gu_ref[:, :hidden].astype(f32)
    up = gu_ref[:, hidden:].astype(f32)
    hidden_grad = dot_nt(grad, d_ref[...])
    half = gelu_parts(gate)
    curve = 0.7978845608028654 * (1.0 + 0.134145 * gate * gate)
    slope = half + 2.0 * gate * half * (1.0 - half) * curve
    act = gate * half
    gate_grad = (hidden_grad * up * slope).astype(bf16)
    up_grad = (hidden_grad * act).astype(bf16)
    normed = norm_ref[...]
    gate_s[...] += dot_tn(normed, gate_grad)
    up_s[...] += dot_tn(normed, up_grad)
    down_s[...] += dot_tn(grad, (act * up).astype(bf16))
    back = dot_nt(gate_grad, g_ref[...]) + dot_nt(up_grad, u_ref[...])
    nf_ref[...] = (part_in[...] + back).astype(bf16) if own else back

    @pl.when(b == pl.num_programs(0) - 1)
    def _():
        cut = a_ref.shape[1]
        a_ref[...] = gate_s[:, :cut].astype(bf16)
        b_ref[:, : hidden - cut] = gate_s[:, cut:].astype(bf16)
        b_ref[:, hidden - cut :] = up_s[...].astype(bf16)
        if not own:
            down_ref[...] = down_s[...].astype(bf16)
        else:
            for k, ref in enumerate(downs):
                size = ref.shape[0]
                rows = pl.ds(pl.multiple_of(jnp.bitwise_xor(index_ref[0], k) * size, size), size)
                ref[:, :hidden] = down_in[rows, :]
                ref[:, hidden:] = down_s[rows, :].astype(bf16)


def ffn_back(grad, normed, gate_up, down, gate, up, count, index=None, part_sum=None, far_down=None):
    total, depth = normed.shape
    hidden = down.shape[0]
    own = index is not None
    quarter = depth // 4
    downs = [(quarter, 2 * hidden)] * 4 if own else [(depth, hidden)]
    shapes = [(depth, hidden // 2), (depth, hidden + hidden // 2)] + downs
    return pl.pallas_call(
        partial(ffn_back_kernel, hidden, own),
        grid=(total // count,),
        in_specs=([SCALARS] if own else [])
        + [
            rows_of(count, depth),
            rows_of(count, depth),
            rows_of(count, 2 * hidden),
            full(hidden, depth),
            full(depth, hidden),
            full(depth, hidden),
        ]
        + ([rows_of(count, depth), full(depth, hidden)] if own else []),
        out_specs=[rows_of(count, depth)] + [kept(*shape) for shape in shapes],
        out_shape=(like((total, depth), bf16 if own else f32),) + tuple(like(shape, bf16) for shape in shapes),
        scratch_shapes=[pltpu.VMEM((depth, hidden), f32)] * 3,
        compiler_params=params(28),
        cost_estimate=cost(10),
        name="ffn_back",
    )(*([index] if own else []), grad, normed, gate_up, down, gate, up, *([part_sum, far_down] if own else []))


def mid_back_kernel(near_ref, moved_ref, mid_ref, grad_ref, gain_ref, c0_ref, c1_ref, w0_ref, w1_ref, out_ref, dc0_ref, dc1_ref, ow0_ref, ow1_ref, gg_ref, o0_s, o1_s):
    b = pl.program_id(0)

    @pl.when(b == 0)
    def _():
        o0_s[...] = jnp.zeros(o0_s.shape, f32)
        o1_s[...] = jnp.zeros(o1_s.shape, f32)
        gg_ref[...] = jnp.zeros(gg_ref.shape, f32)

    gradient = near_ref[...].astype(f32) + moved_ref[...].astype(f32)
    back, addends = norm_back(mid_ref[...], gain_ref[...].astype(f32), gradient)
    mid_grad = grad_ref[...] + back
    out_ref[...] = mid_grad
    gg_ref[0:1, :] += jnp.sum(addends, axis=0, keepdims=True)
    rounded = mid_grad.astype(bf16)
    dc0_ref[...] = dot_nt(rounded, w0_ref[...]).astype(bf16)
    dc1_ref[...] = dot_nt(rounded, w1_ref[...]).astype(bf16)
    o0_s[...] += dot_tn(rounded, c0_ref[...])
    o1_s[...] += dot_tn(rounded, c1_ref[...])

    @pl.when(b == pl.num_programs(0) - 1)
    def _():
        ow0_ref[...] = o0_s[...].astype(bf16)
        ow1_ref[...] = o1_s[...].astype(bf16)


def mid_back(near, moved, mid, grad, gain, contexts, weights, count):
    total, depth = mid.shape
    inner = weights[0].shape[0]
    return pl.pallas_call(
        mid_back_kernel,
        grid=(total // count,),
        in_specs=[rows_of(count, depth)] * 4
        + [full(1, depth)]
        + [rows_of(count, inner)] * 2
        + [full(inner, depth)] * 2,
        out_specs=[
            rows_of(count, depth),
            rows_of(count, inner),
            rows_of(count, inner),
            kept(depth, inner),
            kept(depth, inner),
            kept(8, depth),
        ],
        out_shape=(
            like((total, depth), f32),
            like((total, inner), bf16),
            like((total, inner), bf16),
            like((depth, inner), bf16),
            like((depth, inner), bf16),
            like((8, depth), f32),
        ),
        scratch_shapes=[pltpu.VMEM((depth, inner), f32)] * 2,
        compiler_params=params(16),
        cost_estimate=cost(6),
        name="mid_back",
    )(near, moved, mid, grad, gain, *contexts, *weights)


def heads_far_kernel(norm_ref, grad_ref, ow_ref, out_ref):
    wide = grad_ref.shape[1]
    out_ref[:, :wide] = dot_tn(norm_ref[...], grad_ref[...]).astype(bf16)
    out_ref[:, wide:] = ow_ref[...]


def heads_far(normed, grads, output_grad):
    total, depth = normed.shape
    wide = grads.shape[1] + output_grad.shape[1]
    return pl.pallas_call(
        heads_far_kernel,
        in_specs=[pl.BlockSpec(memory_space=pltpu.VMEM)] * 3,
        out_shape=like((depth, wide), bf16),
        compiler_params=params(10),
        cost_estimate=cost(3),
        name="heads_far",
    )(normed, grads, output_grad)


def heads_own_kernel(index_ref, norm_ref, grad_ref, ow_ref, moved_ref, *refs):
    outs, sum_s = refs[:4], refs[4]
    wide = grad_ref.shape[1]
    sum_s[:, :wide] = dot_tn(norm_ref[...], grad_ref[...]) + moved_ref[:, :wide].astype(f32)
    sum_s[:, wide:] = ow_ref[...].astype(f32) + moved_ref[:, wide:].astype(f32)
    for k, ref in enumerate(outs):
        count = ref.shape[0]
        start = pl.multiple_of(jnp.bitwise_xor(index_ref[0], k) * count, count)
        ref[...] = sum_s[pl.ds(start, count), :].astype(bf16)


def heads_own(index, normed, grads, output_grad, moved):
    total, depth = normed.shape
    wide = moved.shape[1]
    return pl.pallas_call(
        heads_own_kernel,
        in_specs=[SCALARS] + [pl.BlockSpec(memory_space=pltpu.VMEM)] * 4,
        out_shape=(like((depth // 4, wide), bf16),) * 4,
        scratch_shapes=[pltpu.VMEM((depth, wide), f32)],
        compiler_params=params(12),
        cost_estimate=cost(3),
        name="heads_own",
    )(index, normed, grads, output_grad, moved)


def quarter_kernel(index_ref, near_ref, moved_ref, *outs):
    for k, ref in enumerate(outs):
        count = ref.shape[0]
        rows = pl.ds(pl.multiple_of(jnp.bitwise_xor(index_ref[0], k) * count, count), count)
        ref[...] = (near_ref[rows, :].astype(f32) + moved_ref[rows, :].astype(f32)).astype(bf16)


def quarter_sums(index, near, moved):
    depth, wide = near.shape
    return pl.pallas_call(
        quarter_kernel,
        in_specs=[SCALARS] + [pl.BlockSpec(memory_space=pltpu.VMEM)] * 2,
        out_shape=(like((depth // 4, wide), bf16),) * 4,
        compiler_params=params(8),
        cost_estimate=cost(1),
        name="quarter_sums",
    )(index, near, moved)


def enter_back_kernel(place_ref, tok_ref, own_ref, far_ref, w0_ref, w1_ref, kept_ref, sent_ref, gg_ref, na_s):
    core = place_ref[0] % 2
    total = tok_ref.shape[0]
    own_half = kept_ref.shape[0]
    gg_ref[...] = jnp.zeros(gg_ref.shape, f32)
    count = total // 3
    for i in range(3):
        rows = slice(i * count, (i + 1) * count)
        grad = dot_nt(own_ref[rows, :], w0_ref[...]) + dot_nt(far_ref[rows, :], w1_ref[...])
        values = tok_ref[rows, :].astype(f32)
        gg_ref[0:1, :] += jnp.sum(grad * values * rms(values), axis=0, keepdims=True)
        na_s[rows, :] = grad.astype(bf16)
    shard, query = split_of(total, own_half)
    for ref, which in ((kept_ref, core), (sent_ref, 1 - core)):
        for i in range(2):
            start = pl.multiple_of((which + 2 * i) * shard, shard)
            ref[i * shard : (i + 1) * shard, :] = na_s[pl.ds(start, shard), :]
        start = pl.multiple_of(4 * shard + which * query, query)
        ref[2 * shard :, :] = na_s[pl.ds(start, query), :]


def widen_kernel(groups, cuts, index_ref, *refs):
    outs = refs[4 * groups : 4 * groups + len(cuts)]
    scratch = list(refs[4 * groups + len(cuts) :])
    for (sources, turned), out in zip(cuts, outs):
        target = scratch.pop(0) if turned else out
        at = 0
        for group, first, last in sources:
            for k, ref in enumerate(refs[4 * group : 4 * group + 4]):
                count = ref.shape[0]
                rows = pl.ds(pl.multiple_of(jnp.bitwise_xor(index_ref[0], k) * count, count), count)
                target[rows, at : at + last - first] = ref[:, first:last].astype(f32)
            at += last - first
        if turned:
            out[...] = jnp.transpose(target[...])


def widened(index, groups, cuts, name):
    depth = groups[0][0].shape[0] * 4
    widths = [sum(last - first for _, first, last in sources) for sources, _ in cuts]
    return pl.pallas_call(
        partial(widen_kernel, len(groups), cuts),
        in_specs=[SCALARS] + [pl.BlockSpec(memory_space=pltpu.VMEM)] * (4 * len(groups)),
        out_shape=tuple(
            like((wide, depth) if turned else (depth, wide), f32) for wide, (_, turned) in zip(widths, cuts)
        ),
        scratch_shapes=[pltpu.VMEM((depth, wide), f32) for wide, (_, turned) in zip(widths, cuts) if turned],
        compiler_params=params(20),
        cost_estimate=cost(3),
        name=name,
    )(index, *[piece for group in groups for piece in group])


def split_of(total, half):
    query = half - (half // BLOCK) * BLOCK
    return (half - query) // 2, query


def enter_back(place, tokens, own, far, weights):
    total, depth = tokens.shape
    return pl.pallas_call(
        enter_back_kernel,
        in_specs=[SCALARS] + [pl.BlockSpec(memory_space=pltpu.VMEM)] * 5,
        out_shape=(like((total // 2, depth), bf16),) * 2 + (like((8, depth), f32),),
        scratch_shapes=[pltpu.VMEM((total, depth), bf16)],
        compiler_params=params(16),
        cost_estimate=cost(4),
        name="enter_back",
    )(place, tokens, own, far, *weights)


def inputs_back_kernel(place_ref, tok_ref, mid_ref, near_ref, moved_ref, gain_ref, stay_ref, leave_ref, query_ref):
    core, x = place_ref[0] % 2, place_ref[0] // 2
    total = tok_ref.shape[0]
    shard, query = split_of(total, near_ref.shape[0])
    gain = gain_ref[...].astype(f32)

    def piece(start, at, count):
        rows = pl.ds(pl.multiple_of(start, count), count)
        at = pl.ds(pl.multiple_of(at, count), count)
        gradient = near_ref[at, :].astype(f32) + moved_ref[at, :].astype(f32)
        back, _ = norm_back(tok_ref[rows, :].astype(f32), gain, gradient)
        return mid_ref[rows, :] + back

    leave_ref[...] = piece((core + 2 * (1 - x)) * shard, (1 - x) * shard, shard).astype(bf16)
    stay_ref[...] = piece((core + 2 * x) * shard, x * shard, shard)
    query_ref[...] = piece(4 * shard + core * query, 2 * shard, query)


def inputs_back(place, tokens, mid_grad, near, moved, gain):
    total, depth = tokens.shape
    shard, query = split_of(total, near.shape[0])
    return pl.pallas_call(
        inputs_back_kernel,
        in_specs=[SCALARS] + [pl.BlockSpec(memory_space=pltpu.VMEM)] * 5,
        out_shape=(like((shard, depth), f32), like((shard, depth), bf16), like((query, depth), f32)),
        compiler_params=params(12),
        cost_estimate=cost(2),
        name="inputs_back",
    )(place, tokens, mid_grad, near, moved, gain)


def swapped(bit, mine, theirs, axis=0):
    first = jnp.where(bit == 0, mine, theirs)
    second = jnp.where(bit == 0, theirs, mine)
    return jnp.concatenate([first, second], axis=axis)


def after(values, *earlier):
    return lax.optimization_barrier((values,) + earlier)[0]


def part(values, index, parts, axis=0):
    size = values.shape[axis] // parts
    return lax.dynamic_slice_in_dim(values, index * size, size, axis)


def shards(
    doc_tokens,
    query_tokens,
    doc_segments,
    query_keep,
    retrieved,
    positives,
    attn_gain,
    query_weight,
    key_weight,
    value_weight,
    output_weight,
    position_bias,
    ffn_gain,
    gate_weight,
    up_weight,
    down_weight,
    final_gain,
    proj_weight,
):
    groups = lax.axis_size("dp")
    tensor_size = lax.axis_size("mp")
    bits = groups.bit_length() - 1
    dp = lax.axis_index("dp")
    mp = lax.axis_index("mp")
    x = mp // 2
    core = mp % 2
    row_count, shard_len, width = doc_tokens.shape
    length = shard_len * tensor_size
    query_local, query_len, _ = query_tokens.shape
    chip_queries = query_local * 2
    buckets = position_bias.shape[0]
    hidden_local = gate_weight.shape[1]
    doc_local = retrieved.shape[2]
    docs_row = doc_local // row_count
    query_total = query_keep.shape[0]
    vector_width = proj_weight.shape[1]
    inner = query_weight.shape[1]

    def over(axis, size, mask):
        pairs = [(i, i ^ mask) for i in range(size)]
        return lambda values: lax.ppermute(values, axis, pairs)

    to_x = over("mp", tensor_size, 2)
    to_core = over("mp", tensor_size, 1)
    to_dp = [over("dp", groups, 1 << b) for b in range(bits)]
    dp_bit = [(dp >> b) & 1 for b in range(bits)]

    def exchange(steps):
        dp_mask = sum(1 << b for axis, b in steps if axis == "dp")
        mp_mask = 2 if any(axis == "x" for axis, b in steps) else 0
        pairs = [
            (i, ((i // tensor_size) ^ dp_mask) * tensor_size + ((i % tensor_size) ^ mp_mask))
            for i in range(groups * tensor_size)
        ]
        return lambda values: lax.ppermute(values, ("dp", "mp"), pairs)

    def rounds(order):
        out = []
        for i in range(0, len(order), 2):
            steps = order[i : i + 2]
            if len(steps) == 1:
                out.append([exchange(steps)])
            else:
                out.append([exchange(steps[:1]), exchange(steps[1:]), exchange(steps)])
        return out

    kept_rows = lax.dynamic_index_in_dim(doc_tokens, x, 0, keepdims=False)
    sent_rows = lax.dynamic_index_in_dim(doc_tokens, 1 - x, 0, keepdims=False)
    far_rows = to_x(sent_rows)
    kept_tokens = jnp.concatenate(
        [kept_rows, query_tokens.reshape(query_local * query_len, width)], axis=0
    )
    near_tokens = to_core(kept_tokens)
    cross_rows = to_core(far_rows)

    own_qkv, qkv_half, output_half, gate_up_half, down_half = pack(
        jnp.stack(dp_bit[:2]),
        after(query_weight, sent_rows),
        key_weight,
        value_weight,
        output_weight,
        gate_weight,
        up_weight,
        down_weight,
        position_bias,
    )
    qkv_half = to_x(qkv_half)
    output_half = to_x(output_half)
    gate_up_half = to_x(gate_up_half)
    down_half = to_x(down_half)
    far_bias = output_half[inner // 2 :, : position_bias.shape[1]]
    output_half = output_half[: inner // 2]

    def other_half(got, b=0):
        return swapped(dp_bit[b], got, to_dp[b](got))

    near_tiles = bias_tiles(position_bias.astype(f32))
    far_tiles = bias_tiles(far_bias.astype(f32))
    tiles = (near_tiles, far_tiles)

    row_segments = lax.dynamic_index_in_dim(doc_segments, x, 0, keepdims=False)
    chip_keep = lax.dynamic_slice_in_dim(
        query_keep, (dp * tensor_size + x * 2) * query_local, chip_queries, 0
    ).reshape(-1)
    query_ids = jnp.arange(chip_queries * query_len, dtype=jnp.int32) // query_len + docs_row
    seg_q = jnp.concatenate([row_segments, query_ids])
    seg_k = jnp.concatenate([row_segments, jnp.where(chip_keep > 0, query_ids, -1)])
    blocked = row_segments.reshape(-1, PAIR)
    low = jnp.sum((row_segments[None, :] < blocked[:, :1]).astype(jnp.int32), axis=1)
    high = jnp.sum((row_segments[None, :] <= blocked[:, -1:]).astype(jnp.int32), axis=1)
    low_block = low // BLOCK
    high_block = (high + BLOCK - 1) // BLOCK
    lo = jnp.concatenate([low_block, jnp.full((1,), length // BLOCK - 1, jnp.int32)])
    cnt = jnp.concatenate([(high_block - low_block + 1) // 2, jnp.ones((1,), jnp.int32)])
    ranges = (lo, cnt)

    order = [("dp", b) for b in reversed(range(bits))] + [("x", 0)]
    place = sum((x if axis == "x" else dp_bit[b]) << s for s, (axis, b) in enumerate(order))
    kept_retrieved = (query_keep[:, :, None] * retrieved).reshape(query_total * query_len, doc_local)
    seg_q, seg_k = seg_q[None, :], seg_k[None, :]
    chosen, pos_rows, col_q, col_k = choose(
        jnp.stack([core, place, x * docs_row]),
        positives,
        kept_retrieved,
        seg_q,
        seg_k,
        query_local,
        query_len,
        bits + 1,
    )
    segs = (col_q, seg_q, col_k, seg_k)
    half_queries = query_total // 2
    query_lanes = pos_rows.shape[1]

    place_mp = mp.reshape(1)
    gain_attn, gain_ffn, gain_final = [g.reshape(1, width) for g in (attn_gain, ffn_gain, final_gain)]
    pieces = (kept_tokens, near_tokens, far_rows, cross_rows)
    own_qkv = after(own_qkv, chosen)
    tokens, normed_attn, own_heads = enter(place_mp, pieces, gain_attn, own_qkv)
    far_qkv = other_half(after(qkv_half, own_heads))
    own_context, own_log = attend(own_heads, ranges, segs, near_tiles[0])
    far_heads = dot_nn(normed_attn, after(far_qkv, own_context)).astype(bf16)
    far_output = other_half(after(output_half, far_qkv))
    far_context, far_log = attend(far_heads, ranges, segs, far_tiles[0])
    far_output = after(far_output, far_context)
    gate_up_half = after(gate_up_half, far_output)
    far_gate = other_half(gate_up_half[:, :hidden_local])
    far_up = other_half(gate_up_half[:, hidden_local:], 1)
    heads = (own_heads, far_heads)
    contexts = (own_context, far_context)
    logs = (own_log, far_log)
    qkv_weights = (own_qkv, far_qkv)
    output_weights = (output_weight, far_output)
    attn_part = sum(dot_nn(c, w) for c, w in zip(contexts, output_weights)).astype(bf16)
    count = tokens.shape[0] // 3
    mid, normed_ffn, own_gate_up, ffn_sum = ffn_own(
        tokens, attn_part, to_core(attn_part), gain_ffn, gate_weight, up_weight, down_weight, count
    )
    far_down = other_half(after(down_half, mid))
    far_gate_up_out, ffn_part = ffn_far(
        normed_ffn, *after((far_gate, far_up), ffn_sum), far_down, ffn_sum, count
    )
    layer_out, projected, embedded = leave(
        mid, ffn_part, to_core(ffn_part), gain_final, proj_weight, count
    )

    doc_embedded = embedded[:length]
    query_emb = part(embedded[length:], core, 2)
    for moves in rounds(order):
        query_emb = jnp.concatenate([query_emb] + [move(query_emb) for move in moves], axis=0)
    first_doc = jnp.stack([dp * doc_local + x * docs_row, place])
    seg_col = col_q
    sums, logits, stats = score(
        first_doc, doc_embedded, query_emb, seg_col, chosen, pos_rows, query_len, query_local, docs_row
    )
    for moves in rounds(order[::-1]):
        every = [stats] + [move(stats) for move in moves]
        top = every[0][0:1]
        for moved in every[1:]:
            top = jnp.maximum(top, moved[0:1])
        total = sum(moved[1:2] * jnp.exp(moved[0:1] - top) for moved in every)
        stats = jnp.concatenate([top, total, sum(moved[2:] for moved in every)], axis=0)
    valid = jnp.arange(query_lanes) < half_queries
    loss_sum = jnp.sum(jnp.where(valid, stats[0] + jnp.log(stats[1]) - stats[2], 0.0))
    found_sum = jnp.sum(jnp.where(valid & (stats[3] > 0.5), 1.0, 0.0))
    ends = jnp.broadcast_to(jnp.stack([loss_sum, found_sum])[:, None], (2, BLOCK))
    ends = (ends + to_core(ends)) / query_total
    loss_value = ends[0, 0]
    found_share = ends[1, 0]

    demb, dqe = score_back(
        first_doc,
        doc_embedded,
        query_emb,
        seg_col,
        chosen,
        pos_rows,
        sums,
        logits,
        stats,
        query_len,
        query_local,
        docs_row,
    )
    demb_moved = to_core(demb.astype(bf16))
    for moves in reversed(rounds(order)):
        pieces = jnp.split(dqe, len(moves) + 1, axis=0)
        moved = [move(piece).astype(f32) for move, piece in zip(moves, pieces[1:])]
        dqe = sum(moved, pieces[0].astype(f32)).astype(bf16)
    dqe_moved = to_core(dqe)

    def widen(values):
        return values.astype(f32)

    def narrow(values):
        return values.astype(bf16)

    def added(*values):
        return narrow(sum(widen(v) for v in values[1:]) + widen(values[0]))

    four = [exchange([("dp", 0)]), exchange([("dp", 1)]), exchange([("dp", 0), ("dp", 1)])]
    four_index = (dp % 4).reshape(1)
    rest = range(2, bits)

    def scattered(pieces):
        return (pieces[0],) + tuple(move(piece) for move, piece in zip(four, pieces[1:]))

    def rest_of(values, moved):
        values = added(values, moved)
        for b in rest[1:]:
            values = added(values, to_dp[b](values))
        return values

    def gathered(values):
        return (values,) + tuple(move(values) for move in four)

    def assembled(pieces):
        low = [jnp.where(dp_bit[0] == 0, pieces[0], pieces[1]), jnp.where(dp_bit[0] == 0, pieces[1], pieces[0])]
        high = [jnp.where(dp_bit[0] == 0, pieces[2], pieces[3]), jnp.where(dp_bit[0] == 0, pieces[3], pieces[2])]
        return jnp.concatenate(
            [jnp.where(dp_bit[1] == 0, u, v) for u, v in zip(low + high, high + low)], axis=0
        )

    layer_out_grad, proj_grad, final_gain_part = leave_back(
        core.reshape(1), layer_out, projected, demb, demb_moved, dqe, dqe_moved, gain_final, proj_weight
    )
    proj_part = narrow(part(proj_grad, core, 2))
    proj_moved = to_x(proj_part)
    nf_sum, far_first, far_rest, far_down_grad = ffn_back(
        after(layer_out_grad, proj_part), normed_ffn, far_gate_up_out, far_down, far_gate, far_up, count
    )
    first_moved = to_x(far_first)
    proj_part = added(proj_part, after(proj_moved, far_first))
    proj_moves = [move(proj_part) for move in four]
    nf_part, own_first, own_rest, *down_pieces = ffn_back(
        after(layer_out_grad, proj_part),
        normed_ffn,
        own_gate_up,
        down_weight,
        gate_weight,
        up_weight,
        count,
        four_index,
        nf_sum,
        far_down_grad,
    )
    first_pieces = quarter_sums(four_index, own_first, after(first_moved, nf_part))
    first_moves = scattered(first_pieces)
    rest_moved = to_x(after(far_rest, first_pieces))
    down_moves = scattered(tuple(down_pieces))
    proj_part = added(*after((proj_part, *proj_moves), first_pieces))
    proj_moved = to_dp[rest[0]](proj_part)
    nf_part = after(nf_part, proj_part)
    mid_grad, own_context_grad, far_context_grad, own_out, far_out, ffn_gain_part = mid_back(
        nf_part, to_core(nf_part), mid, layer_out_grad, gain_ffn, contexts, output_weights, count
    )

    far_grads, far_bias_grad = attend_back(
        far_heads,
        far_context_grad,
        far_context,
        far_log,
        ranges,
        segs,
        far_tiles[1],
        buckets,
    )
    far_all = heads_far(normed_attn, far_grads, far_out)

    down = added(*after(down_moves, far_all))
    down_kept, down_moved = down[:, hidden_local:], to_x(down[:, :hidden_local])
    all_moved = to_x(after(far_all, down))
    first = added(*after(first_moves, far_all))
    first_moved = to_dp[rest[0]](first)
    rest_pieces = quarter_sums(four_index, own_rest, after(rest_moved, far_all))
    rest_moves = scattered(rest_pieces)
    proj_part = rest_of(proj_part, after(proj_moved, far_all))
    own_grads, own_bias_grad = attend_back(
        own_heads,
        after(own_context_grad, rest_pieces, first, down, proj_part),
        own_context,
        own_log,
        ranges,
        segs,
        near_tiles[1],
        buckets,
    )

    others = added(*after(rest_moves, own_grads))
    others_moved = to_dp[rest[0]](others)
    down = added(after(down_moved, own_grads), down_kept)
    down_moved = to_dp[rest[0]](down)
    first = rest_of(first, after(first_moved, own_grads))
    first_all = gathered(first)
    na_kept, na_sent, attn_gain_part = enter_back(
        place_mp, tokens, after(own_grads, others, down, first), far_grads, qkv_weights
    )
    all_pieces = heads_own(four_index, normed_attn, own_grads, own_out, after(all_moved, na_sent))
    all_moves = scattered(all_pieces)
    na_moved = to_core(after(na_sent, all_pieces))

    stay, leaving, query_grad = inputs_back(place_mp, tokens, mid_grad, na_kept, na_moved, gain_attn)
    back = to_x(leaving)
    others = rest_of(others, after(others_moved, leaving))
    down = rest_of(down, after(down_moved, leaving))
    others_all = gathered(others)
    down_all = gathered(down)
    both = added(*after(all_moves, others, down))
    both_moved = to_dp[rest[0]](both)

    lanes = BLOCK
    gains = jnp.concatenate(
        [
            (0.5 * final_gain_part[0]).reshape(-1, lanes),
            (0.5 * ffn_gain_part[0]).reshape(-1, lanes),
            attn_gain_part[0].reshape(-1, lanes),
        ],
        axis=0,
    )
    gain_rows = gains.shape[0]
    bias_rows = [
        jnp.pad(jnp.sum(g, axis=-1), ((0, 0), (0, lanes - buckets)))
        for g in (own_bias_grad, far_bias_grad)
    ]
    packet = jnp.concatenate([gains, bias_rows[0]], axis=0)
    packet_moved = to_x(after(jnp.concatenate([gains, bias_rows[1]], axis=0), all_pieces))
    packet = packet + after(packet_moved, both)
    packet_moves = [move(packet) for move in four]
    proj_moved = to_core(after(proj_part, both))

    both = rest_of(both, after(both_moved, packet))
    both_all = gathered(both)
    packet = sum(after(packet_moves, both), packet)
    for b in rest:
        packet = packet + to_dp[b](packet)
    cut = hidden_local // 2
    gate_weight_grad, up_weight_grad, down_weight_grad = widened(
        four_index,
        after((first_all, others_all, down_all), both),
        (
            (((0, 0, cut), (1, 0, cut)), False),
            (((1, cut, cut + hidden_local),), False),
            (((2, 0, hidden_local),), True),
        ),
        "widen_ffn",
    )
    packet = after(packet, up_weight_grad)
    position_bias_grad = jnp.transpose(packet[gain_rows:, :buckets])
    gains = packet[:gain_rows]
    gains = (gains + to_core(gains)).reshape(3, width)
    proj_weight_grad = widen(swapped(core, proj_part, after(proj_moved, up_weight_grad)))
    back = widen(after(back, up_weight_grad))
    doc_grad = jnp.stack([jnp.where(x == 0, stay, back), jnp.where(x == 0, back, stay)], axis=0)

    query_weight_grad, key_weight_grad, value_weight_grad, output_weight_grad = widened(
        four_index,
        (after(both_all, doc_grad),),
        tuple((((0, i * inner, (i + 1) * inner),), i == 3) for i in range(4)),
        "widen_heads",
    )

    return (
        loss_value,
        found_share,
        doc_grad,
        query_grad.reshape(query_local, query_len, width),
        gains[2],
        query_weight_grad,
        key_weight_grad,
        value_weight_grad,
        output_weight_grad,
        position_bias_grad,
        gains[1],
        gate_weight_grad,
        up_weight_grad,
        down_weight_grad,
        gains[0],
        proj_weight_grad,
    )


def solution(mesh):
    placed = (
        P("dp", "mp", None),
        P(("dp", "mp"), None, None),
        P("dp", None),
        P(),
        P(None, None, "dp"),
        P(),
        P(),
        P(None, "mp"),
        P(None, "mp"),
        P(None, "mp"),
        P("mp", None),
        P(None, "mp"),
        P(),
        P(None, "mp"),
        P(None, "mp"),
        P("mp", None),
        P(),
        P(),
    )
    return jax.shard_map(
        shards,
        mesh=mesh,
        in_specs=placed,
        out_specs=(
            P(),
            P(),
            P("dp", "mp", None),
            P(("dp", "mp"), None, None),
            P(),
            P(None, "mp"),
            P(None, "mp"),
            P(None, "mp"),
            P("mp", None),
            P(None, "mp"),
            P(),
            P(None, "mp"),
            P(None, "mp"),
            P("mp", None),
            P(),
            P(),
        ),
        check_vma=False,
    )
```

```python
from functools import partial

import jax
import jax.numpy as jnp
import numpy as np
from jax import lax
from jax.experimental import pallas as pl
from jax.experimental.pallas import tpu as pltpu
from jax.sharding import PartitionSpec as P

epsilon = 1e-06
sharpness = 16.0
smoothing_divisor = 0.05
masked_score = -1e30
BLOCK = 128
PAIR = 2 * BLOCK
bf16 = jnp.bfloat16
f32 = jnp.float32


def bucket_starts(buckets):
    half = buckets // 2
    exact = half // 2
    distance = np.arange(0, 2048)
    scaled = (
        np.log(np.maximum(distance, 1) / exact) / np.log(128.0 / exact) * (half - exact)
    )
    far = np.minimum(exact + np.floor(np.maximum(scaled, 0.0)), half - 1)
    bucket = np.where(distance < exact, distance, far)
    return [int(np.argmax(bucket >= b)) for b in range(half)]


def dot_nn(a, b):
    return lax.dot_general(a, b, (((1,), (0,)), ((), ())), preferred_element_type=f32)


def dot_nt(a, b):
    return lax.dot_general(a, b, (((1,), (1,)), ((), ())), preferred_element_type=f32)


def dot_tn(a, b):
    return lax.dot_general(a, b, (((0,), (0,)), ((), ())), preferred_element_type=f32)


def dot_exact(a, b):
    return lax.dot_general(
        a, b, (((1,), (0,)), ((), ())), precision=lax.Precision.HIGHEST, preferred_element_type=f32
    )


def params(limit_mib=40):
    return pltpu.CompilerParams(vmem_limit_bytes=limit_mib << 20)


def cost(micros):
    return pl.CostEstimate(flops=int(micros * 3e9), transcendentals=0, bytes_accessed=1 << 10)


def bias_kernel(starts, heads, tab_ref, t_ref, tt_ref):
    half = len(starts)
    sub = lax.broadcasted_iota(jnp.int32, (BLOCK, BLOCK), 0)
    lane = lax.broadcasted_iota(jnp.int32, (BLOCK, BLOCK), 1)
    for ref, base in ((t_ref, lane - sub), (tt_ref, sub - lane)):
        for d in (-1, 0, 1):
            offset = base + BLOCK * d
            n = jnp.abs(offset)
            for h in range(heads):
                low = high = None
                if d <= 0:
                    low = jnp.full((BLOCK, BLOCK), tab_ref[0, h], f32)
                    for b in range(1, half):
                        low = jnp.where(n >= starts[b], tab_ref[b, h], low)
                if d >= 0:
                    high = jnp.full((BLOCK, BLOCK), tab_ref[half, h], f32)
                    for b in range(1, half):
                        high = jnp.where(n >= starts[b], tab_ref[half + b, h], high)
                if d < 0:
                    tile = low
                elif d > 0:
                    tile = high
                else:
                    tile = jnp.where(offset > 0, high, low)
                ref[h, d + 2] = tile
        for h in range(heads):
            ref[h, 0] = jnp.full((BLOCK, BLOCK), tab_ref[half - 1, h], f32)
            ref[h, 4] = jnp.full((BLOCK, BLOCK), tab_ref[2 * half - 1, h], f32)


def bias_tiles(table):
    buckets, heads = table.shape
    starts = bucket_starts(buckets)
    shape = jax.ShapeDtypeStruct((heads, 5, BLOCK, BLOCK), f32)
    return pl.pallas_call(
        partial(bias_kernel, starts, heads),
        in_specs=[pl.BlockSpec(memory_space=pltpu.SMEM)],
        out_shape=(shape, shape),
        compiler_params=params(6),
        cost_estimate=cost(2),
        name="bias_tiles",
    )(table)


def clipped(d):
    return jnp.minimum(jnp.maximum(d, -2), 2) + 2


def column(row):
    return jnp.transpose(jnp.broadcast_to(row, (8, row.shape[1])))[:, 0:1]


def attend_kernel(heads, size, most, lo_ref, cnt_ref, qkv_ref, segq_ref, segk_ref, t_ref, ctx_ref, lse_ref, k_s, v_s):
    b = pl.program_id(0)
    inner = heads * size
    last = pl.num_programs(0) - 1

    @pl.when(b == 0)
    def _():
        for h in range(heads):
            k_s[h] = qkv_ref[:, inner + h * size : inner + (h + 1) * size]
            v_s[h] = qkv_ref[:, 2 * inner + h * size : 2 * inner + (h + 1) * size]

    def window(first, count, lo, pairs):
        rows = pl.ds(pl.multiple_of(first * BLOCK, BLOCK), count * BLOCK)
        block = qkv_ref[rows, :inner]
        seg_col = column(segq_ref[:, rows])
        spans = [pl.ds(pl.multiple_of((lo + 2 * i) * BLOCK, BLOCK), PAIR) for i in range(pairs)]
        allowed = [seg_col == segk_ref[:, span] for span in spans]
        outs, logs = [], []
        for h in range(heads):
            query = block[:, h * size : (h + 1) * size]
            scores = []
            for i, span in enumerate(spans):
                s = dot_nt(query, k_s[h, span, :])
                bias = jnp.concatenate(
                    [
                        jnp.concatenate(
                            [t_ref[h, clipped(lo + 2 * i + c - first - r)] for c in range(2)], axis=1
                        )
                        for r in range(count)
                    ],
                    axis=0,
                )
                scores.append(jnp.where(allowed[i], s + bias, masked_score))
            top = scores[0]
            for s in scores[1:]:
                top = jnp.maximum(top, s)
            largest = jnp.max(top, axis=1, keepdims=True)
            total = acc = None
            for i, span in enumerate(spans):
                p = jnp.exp(scores[i] - largest)
                total = p if total is None else total + p
                more = dot_nn(p.astype(bf16), v_s[h, span, :])
                acc = more if acc is None else acc + more
            total = jnp.sum(total, axis=1, keepdims=True)
            outs.append((acc / total).astype(bf16))
            lse = jnp.broadcast_to(largest + jnp.log(total), (count * BLOCK, BLOCK))
            lse_ref[h : h + 1, rows] = jnp.transpose(lse)[0:1, :]
        ctx_ref[rows, :] = jnp.concatenate(outs, axis=1)

    for pairs in range(1, most + 1):
        pl.when((b < last) & (cnt_ref[b] == pairs))(partial(window, 2 * b, 2, lo_ref[b], pairs))
    pl.when(b == last)(partial(window, 2 * b, 1, lo_ref[b], 1))


def attend(qkv, ranges, segs, tiles):
    lo, cnt = ranges
    seg_q, seg_k = segs
    total, wide = qkv.shape
    heads = tiles.shape[0]
    inner = wide // 3
    size = inner // heads
    steps = lo.shape[0]
    whole = lambda b, *_: (0, 0)
    return pl.pallas_call(
        partial(attend_kernel, heads, size, steps - 1),
        grid_spec=pltpu.PrefetchScalarGridSpec(
            num_scalar_prefetch=2,
            grid=(steps,),
            in_specs=[
                pl.BlockSpec((total, wide), whole, pipeline_mode=pl.Buffered(1)),
                pl.BlockSpec((1, total), whole, pipeline_mode=pl.Buffered(1)),
                pl.BlockSpec((1, total), whole, pipeline_mode=pl.Buffered(1)),
                pl.BlockSpec((heads, 5, BLOCK, BLOCK), lambda b, *_: (0, 0, 0, 0), pipeline_mode=pl.Buffered(1)),
            ],
            out_specs=[
                pl.BlockSpec((total, inner), whole),
                pl.BlockSpec((8, total), whole),
            ],
            scratch_shapes=[
                pltpu.VMEM((heads, total, size), bf16),
                pltpu.VMEM((heads, total, size), bf16),
            ],
        ),
        out_shape=(
            jax.ShapeDtypeStruct((total, inner), bf16),
            jax.ShapeDtypeStruct((8, total), f32),
        ),
        compiler_params=params(12),
        cost_estimate=cost(9),
        name="attend",
    )(lo, cnt, qkv, seg_q, seg_k, tiles)


def attend_back_kernel(
    starts,
    heads,
    size,
    most,
    lo_ref,
    cnt_ref,
    qkv_ref,
    do_ref,
    ctx_ref,
    lse_ref,
    segk_ref,
    segq_ref,
    tt_ref,
    grad_ref,
    bias_ref,
    q_s,
    do_s,
    dq_s,
    delta_s,
    d_s,
):
    b = pl.program_id(0)
    last = pl.num_programs(0) - 1
    inner = heads * size
    half = len(starts)

    @pl.when(b == 0)
    def _():
        prod = do_ref[...].astype(f32) * ctx_ref[...].astype(f32)
        high = prod.astype(bf16)
        low = (prod - high.astype(f32)).astype(bf16)
        row = lax.broadcasted_iota(jnp.int32, (8, inner), 0)
        col = lax.broadcasted_iota(jnp.int32, (8, inner), 1)
        pick = ((col >= row * size) & (col < (row + 1) * size)).astype(f32).astype(bf16)
        delta_s[...] = dot_nt(pick, high) + dot_nt(pick, low)
        for h in range(heads):
            q_s[h] = qkv_ref[:, h * size : (h + 1) * size]
            do_s[h] = do_ref[:, h * size : (h + 1) * size]
        dq_s[...] = jnp.zeros(dq_s.shape, f32)
        d_s[...] = jnp.zeros(d_s.shape, f32)

    def window(first, count, lo, pairs):
        rows = pl.ds(pl.multiple_of(first * BLOCK, BLOCK), count * BLOCK)
        block = qkv_ref[rows, inner:]
        seg_col = column(segk_ref[:, rows])
        spans = [pl.ds(pl.multiple_of((lo + 2 * i) * BLOCK, BLOCK), PAIR) for i in range(pairs)]
        allowed = [seg_col == segq_ref[:, span] for span in spans]
        dks, dvs = [], []
        for h in range(heads):
            key = block[:, h * size : (h + 1) * size]
            value = block[:, inner + h * size : inner + (h + 1) * size]
            dk = dv = None
            for i, span in enumerate(spans):
                q = q_s[h, span, :]
                do = do_s[h, span, :]
                s = dot_nt(key, q)
                dp = dot_nt(value, do)
                at = [[clipped(first + r - lo - 2 * i - c) for c in range(2)] for r in range(count)]
                bias = jnp.concatenate(
                    [
                        jnp.concatenate([tt_ref[h, at[r][c]] for c in range(2)], axis=1)
                        for r in range(count)
                    ],
                    axis=0,
                )
                p = jnp.where(allowed[i], jnp.exp(s + bias - lse_ref[h : h + 1, span]), 0.0)
                ds = p * (dp - delta_s[h : h + 1, span])
                for r in range(count):
                    for c in range(2):
                        d_s[h, at[r][c]] += ds[
                            r * BLOCK : (r + 1) * BLOCK, c * BLOCK : (c + 1) * BLOCK
                        ]
                ds16 = ds.astype(bf16)
                dv_more = dot_nn(p.astype(bf16), do)
                dk_more = dot_nn(ds16, q)
                dv = dv_more if dv is None else dv + dv_more
                dk = dk_more if dk is None else dk + dk_more
                dq_s[h, :, span] += dot_tn(key, ds16)
            dks.append(dk)
            dvs.append(dv)
        grad_ref[rows, inner:] = jnp.concatenate(dks + dvs, axis=1).astype(bf16)

    for pairs in range(1, most + 1):
        pl.when((b < last) & (cnt_ref[b] == pairs))(partial(window, 2 * b, 2, lo_ref[b], pairs))
    pl.when(b == last)(partial(window, 2 * b, 1, lo_ref[b], 1))

    @pl.when(b == last)
    def _():
        grad_ref[:, :inner] = jnp.concatenate([jnp.transpose(dq_s[h]) for h in range(heads)], axis=1).astype(bf16)
        sub = lax.broadcasted_iota(jnp.int32, (BLOCK, BLOCK), 0)
        lane = lax.broadcasted_iota(jnp.int32, (BLOCK, BLOCK), 1)
        below = lane + sub > BLOCK - 1
        reverse = (lane + sub == BLOCK - 1).astype(f32)
        bucket_row = lax.broadcasted_iota(jnp.int32, (2 * half, BLOCK), 0)
        line_lane = lax.broadcasted_iota(jnp.int32, (2 * half, BLOCK), 1)
        picks = {}
        for d in (-1, 0, 1):
            for low in (False, True):
                offset = line_lane + (1 if low else 1 - BLOCK) + BLOCK * d
                n = jnp.abs(offset)
                bucket = jnp.where(offset > 0, half, 0)
                for e in range(1, half):
                    bucket = bucket + (n >= starts[e]).astype(jnp.int32)
                picks[d, low] = bucket == bucket_row
        for h in range(heads):
            whole = jnp.zeros((2 * half, BLOCK), f32)
            for d in (-1, 0, 1):
                tile = dot_exact(d_s[h, d + 2], reverse)
                for low in (False, True):
                    kept = jnp.where(below == low, tile, 0.0)
                    line = jnp.sum(
                        pltpu.roll(kept, 0, 1, stride=1, stride_axis=0), axis=0, keepdims=True
                    )
                    whole = whole + jnp.where(picks[d, low], line, 0.0)
            for e, d in ((half - 1, 0), (2 * half - 1, 4)):
                far = jnp.sum(d_s[h, d], axis=0, keepdims=True)
                whole = whole + jnp.where(bucket_row == e, far, 0.0)
            bias_ref[h] = whole


def attend_back(qkv, context_grad, context, lse, ranges, segs, tiles, buckets):
    lo, cnt = ranges
    seg_q, seg_k = segs
    total, wide = qkv.shape
    heads = tiles.shape[0]
    inner = wide // 3
    size = inner // heads
    steps = lo.shape[0]
    starts = bucket_starts(buckets)
    whole = lambda b, *_: (0, 0)
    return pl.pallas_call(
        partial(attend_back_kernel, starts, heads, size, steps - 1),
        grid_spec=pltpu.PrefetchScalarGridSpec(
            num_scalar_prefetch=2,
            grid=(steps,),
            in_specs=[
                pl.BlockSpec((total, wide), whole, pipeline_mode=pl.Buffered(1)),
                pl.BlockSpec((total, inner), whole, pipeline_mode=pl.Buffered(1)),
                pl.BlockSpec((total, inner), whole, pipeline_mode=pl.Buffered(1)),
                pl.BlockSpec((8, total), whole, pipeline_mode=pl.Buffered(1)),
                pl.BlockSpec((1, total), whole, pipeline_mode=pl.Buffered(1)),
                pl.BlockSpec((1, total), whole, pipeline_mode=pl.Buffered(1)),
                pl.BlockSpec((heads, 5, BLOCK, BLOCK), lambda b, *_: (0, 0, 0, 0), pipeline_mode=pl.Buffered(1)),
            ],
            out_specs=[
                pl.BlockSpec((total, wide), whole),
                pl.BlockSpec((heads, buckets, BLOCK), lambda b, *_: (0, 0, 0)),
            ],
            scratch_shapes=[
                pltpu.VMEM((heads, total, size), bf16),
                pltpu.VMEM((heads, total, size), bf16),
                pltpu.VMEM((heads, size, total), f32),
                pltpu.VMEM((8, total), f32),
                pltpu.VMEM((heads, 5, BLOCK, BLOCK), f32),
            ],
        ),
        out_shape=(
            jax.ShapeDtypeStruct((total, wide), bf16),
            jax.ShapeDtypeStruct((heads, buckets, BLOCK), f32),
        ),
        compiler_params=params(16),
        cost_estimate=cost(15),
        name="attend_back",
    )(lo, cnt, qkv, context_grad, context, lse, seg_k, seg_q, tiles)


def pool_matrix(shape, axis, me, query_len, query_local):
    token = lax.broadcasted_iota(jnp.int32, shape, axis)
    query = lax.broadcasted_iota(jnp.int32, shape, 1 - axis)
    span = query_len * query_local
    holder = jnp.bitwise_xor(token // span, me)
    return (holder * query_local + token % span // query_len == query).astype(f32)


def score_kernel(query_len, query_local, docs, first_ref, emb_ref, qe_ref, seg_ref, chosen_ref, pos_ref, sums_ref, logit_ref, stat_ref, acc_s):
    b = pl.program_id(0)
    count = qe_ref.shape[0]

    @pl.when(b == 0)
    def _():
        acc_s[...] = jnp.zeros(acc_s.shape, f32)

    near = jnp.exp(sharpness * (dot_nt(emb_ref[...], qe_ref[...]) - 1.0))
    seg = column(seg_ref[...])
    for d in range(docs):
        acc_s[d : d + 1, :] += jnp.sum(jnp.where(seg == d, near, 0.0), axis=0, keepdims=True)

    @pl.when(b == pl.num_programs(0) - 1)
    def _():
        sums = acc_s[:docs, :]
        sums_ref[...] = acc_s[...]
        chosen = chosen_ref[:docs, :]
        smooth = 1.0 + jnp.log(sums) / sharpness
        pool = pool_matrix((count, pos_ref.shape[1]), 0, first_ref[1], query_len, query_local)
        picked = dot_exact(chosen * smooth, pool)
        counts = dot_exact(chosen, pool)
        logits = picked / jnp.maximum(counts, 1.0) / smoothing_divisor
        top = jnp.max(logits, axis=0, keepdims=True)
        spread = jnp.sum(jnp.exp(logits - top), axis=0, keepdims=True)
        doc = lax.broadcasted_iota(jnp.int32, logits.shape, 0) + first_ref[0]
        mine = doc == pos_ref[0:1, :]
        stat_ref[0:1, :] = top
        stat_ref[1:2, :] = spread
        stat_ref[2:3, :] = jnp.sum(jnp.where(mine, logits, 0.0), axis=0, keepdims=True)
        stat_ref[3:4, :] = jnp.sum(jnp.where(mine, counts, 0.0), axis=0, keepdims=True)
        stat_ref[4:8, :] = jnp.zeros((4, pos_ref.shape[1]), f32)
        logit_ref[0:docs, :] = logits
        logit_ref[docs : 2 * docs, :] = counts


def score(first, emb, query_emb, seg_col, chosen, positives, query_len, query_local, docs):
    count, width = query_emb.shape
    lanes = positives.shape[1]
    length = emb.shape[0]
    blocks = length // BLOCK
    whole = lambda b, *_: (0, 0)
    return pl.pallas_call(
        partial(score_kernel, query_len, query_local, docs),
        grid_spec=pltpu.PrefetchScalarGridSpec(
            num_scalar_prefetch=1,
            grid=(blocks,),
            in_specs=[
                pl.BlockSpec((BLOCK, width), lambda b, *_: (b, 0)),
                pl.BlockSpec((count, width), whole, pipeline_mode=pl.Buffered(1)),
                pl.BlockSpec((1, BLOCK), lambda b, *_: (0, b)),
                pl.BlockSpec((8, count), whole, pipeline_mode=pl.Buffered(1)),
                pl.BlockSpec((8, lanes), whole, pipeline_mode=pl.Buffered(1)),
            ],
            out_specs=[
                pl.BlockSpec((8, count), whole),
                pl.BlockSpec((8, lanes), whole),
                pl.BlockSpec((8, lanes), whole),
            ],
            scratch_shapes=[pltpu.VMEM((8, count), f32)],
        ),
        out_shape=(
            jax.ShapeDtypeStruct((8, count), f32),
            jax.ShapeDtypeStruct((8, lanes), f32),
            jax.ShapeDtypeStruct((8, lanes), f32),
        ),
        compiler_params=params(10),
        cost_estimate=cost(5),
        name="score",
    )(first, emb, query_emb, seg_col, chosen, positives)


def score_back_kernel(query_len, query_local, docs, first_ref, emb_ref, qe_ref, seg_ref, chosen_ref, pos_ref, sums_ref, logit_ref, stat_ref, demb_ref, dqe_ref, grad_s, dq_s):
    b = pl.program_id(0)
    count = qe_ref.shape[0]

    @pl.when(b == 0)
    def _():
        logits = logit_ref[0:docs, :]
        counts = logit_ref[docs : 2 * docs, :]
        doc = lax.broadcasted_iota(jnp.int32, logits.shape, 0) + first_ref[0]
        mine = (doc == pos_ref[0:1, :]).astype(f32)
        share = jnp.exp(logits - stat_ref[0:1, :]) / stat_ref[1:2, :]
        grad = (share - mine) / smoothing_divisor / jnp.maximum(counts, 1.0)
        spread = pool_matrix((logits.shape[1], count), 1, first_ref[1], query_len, query_local)
        grad_s[0:docs, :] = dot_exact(grad, spread) * chosen_ref[:docs, :] / sums_ref[:docs, :]
        dq_s[...] = jnp.zeros(dq_s.shape, f32)

    emb = emb_ref[...]
    near = jnp.exp(sharpness * (dot_nt(emb, qe_ref[...]) - 1.0))
    seg = column(seg_ref[...])
    weight = jnp.broadcast_to(grad_s[0:1, :], near.shape)
    for d in range(1, docs):
        weight = jnp.where(seg == d, grad_s[d : d + 1, :], weight)
    grad = (near * weight).astype(bf16)
    demb_ref[...] = dot_nn(grad, qe_ref[...])
    dq_s[...] += dot_tn(emb, grad)

    @pl.when(b == pl.num_programs(0) - 1)
    def _():
        dqe_ref[...] = jnp.transpose(dq_s[...]).astype(bf16)


def score_back(first, emb, query_emb, seg_col, chosen, positives, sums, logits, stats, query_len, query_local, docs):
    count, width = query_emb.shape
    lanes = positives.shape[1]
    length = emb.shape[0]
    blocks = length // BLOCK
    whole = lambda b, *_: (0, 0)
    return pl.pallas_call(
        partial(score_back_kernel, query_len, query_local, docs),
        grid_spec=pltpu.PrefetchScalarGridSpec(
            num_scalar_prefetch=1,
            grid=(blocks,),
            in_specs=[
                pl.BlockSpec((BLOCK, width), lambda b, *_: (b, 0)),
                pl.BlockSpec((count, width), whole, pipeline_mode=pl.Buffered(1)),
                pl.BlockSpec((1, BLOCK), lambda b, *_: (0, b)),
                pl.BlockSpec((8, count), whole, pipeline_mode=pl.Buffered(1)),
                pl.BlockSpec((8, lanes), whole, pipeline_mode=pl.Buffered(1)),
                pl.BlockSpec((8, count), whole, pipeline_mode=pl.Buffered(1)),
                pl.BlockSpec((8, lanes), whole, pipeline_mode=pl.Buffered(1)),
                pl.BlockSpec((8, lanes), whole, pipeline_mode=pl.Buffered(1)),
            ],
            out_specs=[
                pl.BlockSpec((BLOCK, width), lambda b, *_: (b, 0)),
                pl.BlockSpec((count, width), whole),
            ],
            scratch_shapes=[pltpu.VMEM((8, count), f32), pltpu.VMEM((width, count), f32)],
        ),
        out_shape=(
            jax.ShapeDtypeStruct((length, width), f32),
            jax.ShapeDtypeStruct((count, width), bf16),
        ),
        compiler_params=params(12),
        cost_estimate=cost(5),
        name="score_back",
    )(first, emb, query_emb, seg_col, chosen, positives, sums, logits, stats)


def full(*shape):
    return pl.BlockSpec(shape, lambda *_: (0,) * len(shape), pipeline_mode=pl.Buffered(1))


def kept(*shape):
    return pl.BlockSpec(shape, lambda *_: (0,) * len(shape))


def rows_of(count, width):
    return pl.BlockSpec((count, width), lambda b, *_: (b, 0))


SCALARS = pl.BlockSpec(memory_space=pltpu.SMEM)


def like(shape, dtype):
    return jax.ShapeDtypeStruct(shape, dtype)


def rms(values):
    return lax.rsqrt(jnp.mean(values * values, axis=-1, keepdims=True) + epsilon)


def choose_kernel(query_local, query_len, steps, place_ref, pos_ref, ret_ref, chosen_ref, rows_ref, ret_s):
    core, me = place_ref[0], place_ref[1]
    span = query_local * query_len
    blocks = ret_s.shape[0] // span

    def holder(p):
        return sum(((p >> s) & 1) << (steps - 1 - s) for s in range(steps))

    def held(p):
        return holder(jnp.bitwise_xor(me, p)) * 2 + core

    for p in range(blocks):
        start = pl.multiple_of(held(p) * span, span)
        ret_s[p * span : (p + 1) * span, :] = ret_ref[pl.ds(start, span), :].astype(f32)
    docs = ret_s.shape[1]
    row = lax.broadcasted_iota(jnp.int32, (docs, docs), 0)
    col = lax.broadcasted_iota(jnp.int32, (docs, docs), 1)
    shift = jnp.where(row < docs // 2, row + place_ref[2], -1)
    chosen_ref[...] = dot_nt((shift == col).astype(f32), ret_s[...])
    lane = lax.broadcasted_iota(jnp.int32, rows_ref.shape, 1)
    rows = jnp.full(rows_ref.shape, -1, jnp.int32)
    for p in range(blocks):
        for i in range(query_local):
            query = (holder(p) * 2 + core) * query_local + i
            rows = jnp.where(lane == p * query_local + i, pos_ref[query], rows)
    rows_ref[...] = rows


def choose(place, positives, retrieved, query_local, query_len, steps):
    total, docs = retrieved.shape
    lanes = -(-(total // 2 // query_len) // BLOCK) * BLOCK
    return pl.pallas_call(
        partial(choose_kernel, query_local, query_len, steps),
        in_specs=[SCALARS, SCALARS, pl.BlockSpec(memory_space=pltpu.VMEM)],
        out_shape=(like((8, total // 2), f32), like((8, lanes), jnp.int32)),
        scratch_shapes=[pltpu.VMEM((total // 2, docs), f32)],
        compiler_params=params(20),
        cost_estimate=cost(1),
        name="choose",
    )(place, positives, retrieved)


def pack_kernel(bit_ref, q_ref, k_ref, v_ref, o_ref, g_ref, u_ref, d_ref, b_ref, qkv_ref, half_qkv, half_o, half_g, half_u, half_d0, half_d1):
    inner = q_ref.shape[0]

    def half(ref, bit):
        rows = ref.shape[0] // 2
        return ref[pl.ds(pl.multiple_of(bit_ref[bit] * rows, rows), rows), :]

    for i, ref in enumerate((q_ref, k_ref, v_ref)):
        qkv_ref[:, i * inner : (i + 1) * inner] = jnp.transpose(ref[...])
    half_qkv[...] = half(qkv_ref, 0)
    rows = o_ref.shape[0] // 2
    half_o[:rows, :] = half(o_ref, 0)
    half_o[rows:, :] = jnp.zeros((half_o.shape[0] - rows, half_o.shape[1]), bf16)
    half_o[rows:, : b_ref.shape[1]] = b_ref[...]
    half_g[...] = half(g_ref, 0)
    half_u[...] = half(u_ref, 1)
    cut = half_d0.shape[1]
    half_d0[...] = half(d_ref, 0)[:, :cut]
    half_d1[...] = half(d_ref, 1)[:, cut:]


def pack(bits, q, k, v, o, gate, up, down, bias):
    inner, depth = q.shape
    hidden = gate.shape[1]
    return pl.pallas_call(
        pack_kernel,
        in_specs=[SCALARS] + [pl.BlockSpec(memory_space=pltpu.VMEM)] * 8,
        out_shape=(
            like((depth, 3 * inner), bf16),
            like((depth // 2, 3 * inner), bf16),
            like((inner // 2 + bias.shape[0], depth), bf16),
            like((depth // 2, hidden), bf16),
            like((depth // 2, hidden), bf16),
            like((hidden // 2, depth // 2), bf16),
            like((hidden // 2, depth // 2), bf16),
        ),
        compiler_params=params(12),
        cost_estimate=cost(1),
        name="pack",
    )(bits, q, k, v, o, gate, up, down, bias)


def enter_kernel(place_ref, kept_ref, near_ref, far_ref, cross_ref, gain_ref, w_ref, tok_ref, norm_ref, heads_ref):
    gain = gain_ref[...].astype(f32)
    mp = place_ref[0]
    shard = far_ref.shape[0]
    query = kept_ref.shape[0] - shard
    pieces = [(kept_ref, 0), (near_ref, 1), (far_ref, 2), (cross_ref, 3)]
    spans = [(ref, 0, shard, jnp.bitwise_xor(mp, i) * shard) for ref, i in pieces]
    spans += [
        (ref, shard, query, 4 * shard + jnp.bitwise_xor(mp % 2, i) * query) for ref, i in pieces[:2]
    ]
    for ref, first, count, start in spans:
        rows = pl.ds(pl.multiple_of(start, count), count)
        piece = ref[first : first + count, :]
        values = piece.astype(f32)
        normed = (values * rms(values) * gain).astype(bf16)
        tok_ref[rows, :] = piece
        norm_ref[rows, :] = normed
        heads_ref[rows, :] = dot_nn(normed, w_ref[...]).astype(bf16)


def enter(place, pieces, gain, weight):
    total = sum(piece.shape[0] for piece in pieces)
    depth, wide = weight.shape
    return pl.pallas_call(
        enter_kernel,
        in_specs=[SCALARS] + [pl.BlockSpec(memory_space=pltpu.VMEM)] * 6,
        out_shape=(like((total, depth), bf16), like((total, depth), bf16), like((total, wide), bf16)),
        compiler_params=params(12),
        cost_estimate=cost(3),
        name="enter",
    )(place, *pieces, gain, weight)


def gelu_parts(gate):
    inner = 0.7978845608028654 * (gate + 0.044715 * gate * gate * gate)
    return 0.5 * (1.0 + jnp.tanh(inner))


def ffn_own_kernel(tok_ref, near_ref, moved_ref, gain_ref, g_ref, u_ref, d_ref, mid_ref, norm_ref, gu_ref, part_ref):
    hidden = g_ref.shape[1]
    mid = tok_ref[...].astype(f32) + (near_ref[...].astype(f32) + moved_ref[...].astype(f32))
    mid_ref[...] = mid
    normed = (mid * rms(mid) * gain_ref[...].astype(f32)).astype(bf16)
    norm_ref[...] = normed
    gate = dot_nn(normed, g_ref[...])
    up = dot_nn(normed, u_ref[...])
    gu_ref[:, :hidden] = gate.astype(bf16)
    gu_ref[:, hidden:] = up.astype(bf16)
    part_ref[...] = dot_nn((gate * gelu_parts(gate) * up).astype(bf16), d_ref[...])


def ffn_own(tokens, near, moved, gain, gate, up, down, count):
    total, depth = tokens.shape
    hidden = gate.shape[1]
    return pl.pallas_call(
        ffn_own_kernel,
        grid=(total // count,),
        in_specs=[rows_of(count, depth)] * 3
        + [full(1, depth), full(depth, hidden), full(depth, hidden), full(hidden, depth)],
        out_specs=[
            rows_of(count, depth),
            rows_of(count, depth),
            rows_of(count, 2 * hidden),
            rows_of(count, depth),
        ],
        out_shape=(
            like((total, depth), f32),
            like((total, depth), bf16),
            like((total, 2 * hidden), bf16),
            like((total, depth), f32),
        ),
        compiler_params=params(16),
        cost_estimate=cost(5),
        name="ffn_own",
    )(tokens, near, moved, gain, gate, up, down)


def ffn_far_kernel(norm_ref, g_ref, u_ref, d_ref, part_ref, gu_ref, out_ref):
    hidden = d_ref.shape[0]
    normed = norm_ref[...]
    gate = dot_nn(normed, g_ref[...])
    up = dot_nn(normed, u_ref[...])
    gu_ref[:, :hidden] = gate.astype(bf16)
    gu_ref[:, hidden:] = up.astype(bf16)
    more = dot_nn((gate * gelu_parts(gate) * up).astype(bf16), d_ref[...])
    out_ref[...] = (part_ref[...] + more).astype(bf16)


def ffn_far(normed, gate, up, down, partial_sum, count):
    total, depth = normed.shape
    hidden = down.shape[0]
    return pl.pallas_call(
        ffn_far_kernel,
        grid=(total // count,),
        in_specs=[
            rows_of(count, depth),
            full(depth, hidden),
            full(depth, hidden),
            full(hidden, depth),
            rows_of(count, depth),
        ],
        out_specs=[rows_of(count, 2 * hidden), rows_of(count, depth)],
        out_shape=(like((total, 2 * hidden), bf16), like((total, depth), bf16)),
        compiler_params=params(14),
        cost_estimate=cost(5),
        name="ffn_far",
    )(normed, gate, up, down, partial_sum)


def leave_kernel(mid_ref, near_ref, moved_ref, gain_ref, w_ref, out_ref, proj_ref, emb_ref):
    out = mid_ref[...] + (near_ref[...].astype(f32) + moved_ref[...].astype(f32))
    out_ref[...] = out
    normed = (out * rms(out) * gain_ref[...].astype(f32)).astype(bf16)
    projected = dot_nn(normed, w_ref[...])
    proj_ref[...] = projected
    scale = lax.rsqrt(jnp.sum(projected * projected, axis=-1, keepdims=True) + epsilon)
    emb_ref[...] = (projected * scale).astype(bf16)


def leave(mid, near, moved, gain, weight, count):
    total, depth = mid.shape
    wide = weight.shape[1]
    return pl.pallas_call(
        leave_kernel,
        grid=(total // count,),
        in_specs=[rows_of(count, depth)] * 3 + [full(1, depth), full(depth, wide)],
        out_specs=[rows_of(count, depth), rows_of(count, wide), rows_of(count, wide)],
        out_shape=(like((total, depth), f32), like((total, wide), f32), like((total, wide), bf16)),
        compiler_params=params(10),
        cost_estimate=cost(4),
        name="leave",
    )(mid, near, moved, gain, weight)


def norm_back(values, gain, gradient):
    scale = rms(values)
    weighted = gradient * gain
    average = jnp.mean(weighted * values, axis=-1, keepdims=True)
    back = scale * weighted - values * (scale * scale * scale) * average
    return back, gradient * values * scale


def leave_back_kernel(core_ref, out_ref, proj_ref, near_ref, moved_ref, qn_ref, qm_ref, gain_ref, w_ref, grad_ref, wg_ref, gg_ref, emb_s):
    b = pl.program_id(0)
    last = pl.num_programs(0) - 1

    @pl.when(b == 0)
    def _():
        wg_ref[...] = jnp.zeros(wg_ref.shape, f32)
        gg_ref[...] = jnp.zeros(gg_ref.shape, f32)

    @pl.when(b < last)
    def _():
        emb_s[...] = near_ref[...] + moved_ref[...].astype(f32)

    @pl.when(b == last)
    def _():
        half = qn_ref.shape[0]
        core = core_ref[0]
        emb_s[pl.ds(pl.multiple_of(core * half, half), half), :] = qn_ref[...].astype(f32)
        emb_s[pl.ds(pl.multiple_of((1 - core) * half, half), half), :] = qm_ref[...].astype(f32)

    projected = proj_ref[...]
    scale = lax.rsqrt(jnp.sum(projected * projected, axis=-1, keepdims=True) + epsilon)
    unit = projected * scale
    grad = emb_s[...]
    grad = (scale * (grad - unit * jnp.sum(grad * unit, axis=-1, keepdims=True))).astype(bf16)
    out = out_ref[...]
    gain = gain_ref[...].astype(f32)
    normed = (out * rms(out) * gain).astype(bf16)
    wg_ref[...] += dot_tn(normed, grad)
    back, addends = norm_back(out, gain, dot_nt(grad, w_ref[...]))
    grad_ref[...] = back
    gg_ref[0:1, :] += jnp.sum(addends, axis=0, keepdims=True)


def leave_back(core, layer_out, projected, near, moved, query_near, query_moved, gain, weight):
    total, depth = layer_out.shape
    wide = weight.shape[1]
    count = total - near.shape[0]
    steps = total // count
    clamp = pl.BlockSpec((count, wide), lambda b, *_: (jnp.minimum(b, steps - 2), 0))
    return pl.pallas_call(
        leave_back_kernel,
        grid=(steps,),
        in_specs=[
            SCALARS,
            rows_of(count, depth),
            rows_of(count, wide),
            clamp,
            clamp,
            full(count // 2, wide),
            full(count // 2, wide),
            full(1, depth),
            full(depth, wide),
        ],
        out_specs=[rows_of(count, depth), kept(depth, wide), kept(8, depth)],
        out_shape=(like((total, depth), f32), like((depth, wide), f32), like((8, depth), f32)),
        scratch_shapes=[pltpu.VMEM((count, wide), f32)],
        compiler_params=params(8),
        cost_estimate=cost(5),
        name="leave_back",
    )(core, layer_out, projected, near, moved, query_near, query_moved, gain, weight)


def ffn_back_kernel(hidden, own, *refs):
    gate_s, up_s, down_s = refs[-3:]
    if own:
        index_ref, grad_ref, norm_ref, gu_ref, d_ref, g_ref, u_ref, part_in, down_in = refs[:9]
        nf_ref, a_ref, b_ref, *downs = refs[9:-3]
    else:
        grad_ref, norm_ref, gu_ref, d_ref, g_ref, u_ref, nf_ref, a_ref, b_ref, down_ref = refs[:-3]
    b = pl.program_id(0)

    @pl.when(b == 0)
    def _():
        gate_s[...] = jnp.zeros(gate_s.shape, f32)
        up_s[...] = jnp.zeros(up_s.shape, f32)
        down_s[...] = jnp.zeros(down_s.shape, f32)

    grad = grad_ref[...].astype(bf16)
    gate = gu_ref[:, :hidden].astype(f32)
    up = gu_ref[:, hidden:].astype(f32)
    hidden_grad = dot_nt(grad, d_ref[...])
    half = gelu_parts(gate)
    curve = 0.7978845608028654 * (1.0 + 0.134145 * gate * gate)
    slope = half + 2.0 * gate * half * (1.0 - half) * curve
    act = gate * half
    gate_grad = (hidden_grad * up * slope).astype(bf16)
    up_grad = (hidden_grad * act).astype(bf16)
    normed = norm_ref[...]
    gate_s[...] += dot_tn(normed, gate_grad)
    up_s[...] += dot_tn(normed, up_grad)
    down_s[...] += dot_tn(grad, (act * up).astype(bf16))
    back = dot_nt(gate_grad, g_ref[...]) + dot_nt(up_grad, u_ref[...])
    nf_ref[...] = (part_in[...] + back).astype(bf16) if own else back

    @pl.when(b == pl.num_programs(0) - 1)
    def _():
        cut = a_ref.shape[1]
        a_ref[...] = gate_s[:, :cut].astype(bf16)
        b_ref[:, : hidden - cut] = gate_s[:, cut:].astype(bf16)
        b_ref[:, hidden - cut :] = up_s[...].astype(bf16)
        if not own:
            down_ref[...] = down_s[...].astype(bf16)
        else:
            for k, ref in enumerate(downs):
                size = ref.shape[0]
                rows = pl.ds(pl.multiple_of(jnp.bitwise_xor(index_ref[0], k) * size, size), size)
                ref[:, :hidden] = down_in[rows, :]
                ref[:, hidden:] = down_s[rows, :].astype(bf16)


def ffn_back(grad, normed, gate_up, down, gate, up, count, index=None, part_sum=None, far_down=None):
    total, depth = normed.shape
    hidden = down.shape[0]
    own = index is not None
    quarter = depth // 4
    downs = [(quarter, 2 * hidden)] * 4 if own else [(depth, hidden)]
    shapes = [(depth, hidden // 2), (depth, hidden + hidden // 2)] + downs
    return pl.pallas_call(
        partial(ffn_back_kernel, hidden, own),
        grid=(total // count,),
        in_specs=([SCALARS] if own else [])
        + [
            rows_of(count, depth),
            rows_of(count, depth),
            rows_of(count, 2 * hidden),
            full(hidden, depth),
            full(depth, hidden),
            full(depth, hidden),
        ]
        + ([rows_of(count, depth), full(depth, hidden)] if own else []),
        out_specs=[rows_of(count, depth)] + [kept(*shape) for shape in shapes],
        out_shape=(like((total, depth), bf16 if own else f32),) + tuple(like(shape, bf16) for shape in shapes),
        scratch_shapes=[pltpu.VMEM((depth, hidden), f32)] * 3,
        compiler_params=params(28),
        cost_estimate=cost(10),
        name="ffn_back",
    )(*([index] if own else []), grad, normed, gate_up, down, gate, up, *([part_sum, far_down] if own else []))


def mid_back_kernel(near_ref, moved_ref, mid_ref, grad_ref, gain_ref, c0_ref, c1_ref, w0_ref, w1_ref, out_ref, dc0_ref, dc1_ref, ow0_ref, ow1_ref, gg_ref, o0_s, o1_s):
    b = pl.program_id(0)

    @pl.when(b == 0)
    def _():
        o0_s[...] = jnp.zeros(o0_s.shape, f32)
        o1_s[...] = jnp.zeros(o1_s.shape, f32)
        gg_ref[...] = jnp.zeros(gg_ref.shape, f32)

    gradient = near_ref[...].astype(f32) + moved_ref[...].astype(f32)
    back, addends = norm_back(mid_ref[...], gain_ref[...].astype(f32), gradient)
    mid_grad = grad_ref[...] + back
    out_ref[...] = mid_grad
    gg_ref[0:1, :] += jnp.sum(addends, axis=0, keepdims=True)
    rounded = mid_grad.astype(bf16)
    dc0_ref[...] = dot_nt(rounded, w0_ref[...]).astype(bf16)
    dc1_ref[...] = dot_nt(rounded, w1_ref[...]).astype(bf16)
    o0_s[...] += dot_tn(rounded, c0_ref[...])
    o1_s[...] += dot_tn(rounded, c1_ref[...])

    @pl.when(b == pl.num_programs(0) - 1)
    def _():
        ow0_ref[...] = o0_s[...].astype(bf16)
        ow1_ref[...] = o1_s[...].astype(bf16)


def mid_back(near, moved, mid, grad, gain, contexts, weights, count):
    total, depth = mid.shape
    inner = weights[0].shape[0]
    return pl.pallas_call(
        mid_back_kernel,
        grid=(total // count,),
        in_specs=[rows_of(count, depth)] * 4
        + [full(1, depth)]
        + [rows_of(count, inner)] * 2
        + [full(inner, depth)] * 2,
        out_specs=[
            rows_of(count, depth),
            rows_of(count, inner),
            rows_of(count, inner),
            kept(depth, inner),
            kept(depth, inner),
            kept(8, depth),
        ],
        out_shape=(
            like((total, depth), f32),
            like((total, inner), bf16),
            like((total, inner), bf16),
            like((depth, inner), bf16),
            like((depth, inner), bf16),
            like((8, depth), f32),
        ),
        scratch_shapes=[pltpu.VMEM((depth, inner), f32)] * 2,
        compiler_params=params(16),
        cost_estimate=cost(6),
        name="mid_back",
    )(near, moved, mid, grad, gain, *contexts, *weights)


EXTRA = 16


def extra_rows(ref, start, final_ref, ffn_ref, attn_ref, bias_ref):
    rows = [final_ref[0:1, :], ffn_ref[0:1, :]]
    rows.append(jnp.zeros_like(rows[0]) if attn_ref is None else attn_ref[0:1, :])
    ones = jnp.ones((8, bias_ref.shape[2]), f32)
    ref[start : start + EXTRA, :] = jnp.zeros((EXTRA, ref.shape[1]), f32).astype(ref.dtype)
    for i, row in enumerate(rows):
        ref[start + i : start + i + 1, :] = row.astype(ref.dtype)
    for h in range(bias_ref.shape[0]):
        sums = lax.dot_general(
            ones,
            bias_ref[h],
            (((1,), (1,)), ((), ())),
            precision=lax.Precision.HIGHEST,
            preferred_element_type=f32,
        )
        ref[start + 3 + h : start + 4 + h, : sums.shape[1]] = sums[0:1, :].astype(ref.dtype)


def heads_far_kernel(norm_ref, grad_ref, ow_ref, final_ref, ffn_ref, bias_ref, a_ref, b_ref, all_s):
    wide = grad_ref.shape[1]
    depth = norm_ref.shape[1]
    all_s[:depth, :wide] = dot_tn(norm_ref[...], grad_ref[...])
    all_s[:depth, wide:] = ow_ref[...].astype(f32)
    extra_rows(all_s, depth, final_ref, ffn_ref, None, bias_ref)
    cut = a_ref.shape[1]
    a_ref[...] = all_s[:, :cut].astype(bf16)
    b_ref[...] = all_s[:, cut:].astype(bf16)


def heads_far(normed, grads, output_grad, final_gain, ffn_gain, bias_grad):
    total, depth = normed.shape
    wide = grads.shape[1] + output_grad.shape[1]
    cut = wide * 2 // 3 // BLOCK * BLOCK
    return pl.pallas_call(
        heads_far_kernel,
        in_specs=[pl.BlockSpec(memory_space=pltpu.VMEM)] * 6,
        out_shape=(like((depth + EXTRA, cut), bf16), like((depth + EXTRA, wide - cut), bf16)),
        scratch_shapes=[pltpu.VMEM((depth + EXTRA, wide), f32)],
        compiler_params=params(14),
        cost_estimate=cost(3),
        name="heads_far",
    )(normed, grads, output_grad, final_gain, ffn_gain, bias_grad)


def heads_own_kernel(index_ref, norm_ref, grad_ref, ow_ref, final_ref, ffn_ref, attn_ref, bias_ref, a_ref, b_ref, *refs):
    outs, all_s = refs[:4], refs[4]
    wide = grad_ref.shape[1]
    depth = norm_ref.shape[1]
    all_s[:depth, :wide] = dot_tn(norm_ref[...], grad_ref[...])
    all_s[:depth, wide:] = ow_ref[...].astype(f32)
    extra_rows(all_s, depth, final_ref, ffn_ref, attn_ref, bias_ref)
    cut = a_ref.shape[1]
    all_s[:, :cut] += a_ref[...].astype(f32)
    all_s[:, cut:] += b_ref[...].astype(f32)
    count = depth // 4
    for k, ref in enumerate(outs):
        start = pl.multiple_of(jnp.bitwise_xor(index_ref[0], k) * count, count)
        ref[:count, :] = all_s[pl.ds(start, count), :].astype(bf16)
        ref[count:, :] = all_s[depth:, :].astype(bf16)


def heads_own(index, normed, grads, output_grad, final_gain, ffn_gain, attn_gain, bias_grad, moved, more):
    total, depth = normed.shape
    wide = moved.shape[1] + more.shape[1]
    return pl.pallas_call(
        heads_own_kernel,
        in_specs=[SCALARS] + [pl.BlockSpec(memory_space=pltpu.VMEM)] * 9,
        out_shape=(like((depth // 4 + EXTRA, wide), bf16),) * 4,
        scratch_shapes=[pltpu.VMEM((depth + EXTRA, wide), f32)],
        compiler_params=params(16),
        cost_estimate=cost(3),
        name="heads_own",
    )(index, normed, grads, output_grad, final_gain, ffn_gain, attn_gain, bias_grad, moved, more)


def quarter_kernel(index_ref, near_ref, moved_ref, *outs):
    for k, ref in enumerate(outs):
        count = ref.shape[0]
        rows = pl.ds(pl.multiple_of(jnp.bitwise_xor(index_ref[0], k) * count, count), count)
        ref[...] = (near_ref[rows, :].astype(f32) + moved_ref[rows, :].astype(f32)).astype(bf16)


def quarter_sums(index, near, moved):
    depth, wide = near.shape
    return pl.pallas_call(
        quarter_kernel,
        in_specs=[SCALARS] + [pl.BlockSpec(memory_space=pltpu.VMEM)] * 2,
        out_shape=(like((depth // 4, wide), bf16),) * 4,
        compiler_params=params(8),
        cost_estimate=cost(1),
        name="quarter_sums",
    )(index, near, moved)


def enter_back_kernel(place_ref, tok_ref, own_ref, far_ref, w0_ref, w1_ref, kept_ref, sent_ref, gg_ref, na_s):
    core = place_ref[0] % 2
    total = tok_ref.shape[0]
    own_half = kept_ref.shape[0]
    gg_ref[...] = jnp.zeros(gg_ref.shape, f32)
    count = total // 3
    for i in range(3):
        rows = slice(i * count, (i + 1) * count)
        grad = dot_nt(own_ref[rows, :], w0_ref[...]) + dot_nt(far_ref[rows, :], w1_ref[...])
        values = tok_ref[rows, :].astype(f32)
        gg_ref[0:1, :] += jnp.sum(grad * values * rms(values), axis=0, keepdims=True)
        na_s[rows, :] = grad.astype(bf16)
    shard, query = split_of(total, own_half)
    for ref, which in ((kept_ref, core), (sent_ref, 1 - core)):
        for i in range(2):
            start = pl.multiple_of((which + 2 * i) * shard, shard)
            ref[i * shard : (i + 1) * shard, :] = na_s[pl.ds(start, shard), :]
        start = pl.multiple_of(4 * shard + which * query, query)
        ref[2 * shard :, :] = na_s[pl.ds(start, query), :]


def widen_kernel(groups, cuts, index_ref, *refs):
    outs = refs[4 * groups : 4 * groups + len(cuts)]
    scratch = list(refs[4 * groups + len(cuts) :])
    for (sources, turned), out in zip(cuts, outs):
        target = scratch.pop(0) if turned else out
        at = 0
        for group, first, last in sources:
            for k, ref in enumerate(refs[4 * group : 4 * group + 4]):
                count = target.shape[0] // 4
                rows = pl.ds(pl.multiple_of(jnp.bitwise_xor(index_ref[0], k) * count, count), count)
                target[rows, at : at + last - first] = ref[:count, first:last].astype(f32)
            at += last - first
        if turned:
            out[...] = jnp.transpose(target[...])


def widened(index, depth, groups, cuts, name):
    widths = [sum(last - first for _, first, last in sources) for sources, _ in cuts]
    return pl.pallas_call(
        partial(widen_kernel, len(groups), cuts),
        in_specs=[SCALARS] + [pl.BlockSpec(memory_space=pltpu.VMEM)] * (4 * len(groups)),
        out_shape=tuple(
            like((wide, depth) if turned else (depth, wide), f32) for wide, (_, turned) in zip(widths, cuts)
        ),
        scratch_shapes=[pltpu.VMEM((depth, wide), f32) for wide, (_, turned) in zip(widths, cuts) if turned],
        compiler_params=params(20),
        cost_estimate=cost(3),
        name=name,
    )(index, *[piece for group in groups for piece in group])


def split_of(total, half):
    query = half - (half // BLOCK) * BLOCK
    return (half - query) // 2, query


def enter_back(place, tokens, own, far, weights):
    total, depth = tokens.shape
    return pl.pallas_call(
        enter_back_kernel,
        in_specs=[SCALARS] + [pl.BlockSpec(memory_space=pltpu.VMEM)] * 5,
        out_shape=(like((total // 2, depth), bf16),) * 2 + (like((8, depth), f32),),
        scratch_shapes=[pltpu.VMEM((total, depth), bf16)],
        compiler_params=params(16),
        cost_estimate=cost(4),
        name="enter_back",
    )(place, tokens, own, far, *weights)


def inputs_back_kernel(place_ref, tok_ref, mid_ref, near_ref, moved_ref, gain_ref, stay_ref, leave_ref, query_ref):
    core, x = place_ref[0] % 2, place_ref[0] // 2
    total = tok_ref.shape[0]
    shard, query = split_of(total, near_ref.shape[0])
    gain = gain_ref[...].astype(f32)

    def piece(start, at, count):
        rows = pl.ds(pl.multiple_of(start, count), count)
        at = pl.ds(pl.multiple_of(at, count), count)
        gradient = near_ref[at, :].astype(f32) + moved_ref[at, :].astype(f32)
        back, _ = norm_back(tok_ref[rows, :].astype(f32), gain, gradient)
        return mid_ref[rows, :] + back

    leave_ref[...] = piece((core + 2 * (1 - x)) * shard, (1 - x) * shard, shard).astype(bf16)
    stay_ref[...] = piece((core + 2 * x) * shard, x * shard, shard)
    query_ref[...] = piece(4 * shard + core * query, 2 * shard, query)


def inputs_back(place, tokens, mid_grad, near, moved, gain):
    total, depth = tokens.shape
    shard, query = split_of(total, near.shape[0])
    return pl.pallas_call(
        inputs_back_kernel,
        in_specs=[SCALARS] + [pl.BlockSpec(memory_space=pltpu.VMEM)] * 5,
        out_shape=(like((shard, depth), f32), like((shard, depth), bf16), like((query, depth), f32)),
        compiler_params=params(12),
        cost_estimate=cost(2),
        name="inputs_back",
    )(place, tokens, mid_grad, near, moved, gain)


def swapped(bit, mine, theirs, axis=0):
    first = jnp.where(bit == 0, mine, theirs)
    second = jnp.where(bit == 0, theirs, mine)
    return jnp.concatenate([first, second], axis=axis)


def after(values, *earlier):
    return lax.optimization_barrier((values,) + earlier)[0]


def part(values, index, parts, axis=0):
    size = values.shape[axis] // parts
    return lax.dynamic_slice_in_dim(values, index * size, size, axis)


def shards(
    doc_tokens,
    query_tokens,
    doc_segments,
    query_keep,
    retrieved,
    positives,
    attn_gain,
    query_weight,
    key_weight,
    value_weight,
    output_weight,
    position_bias,
    ffn_gain,
    gate_weight,
    up_weight,
    down_weight,
    final_gain,
    proj_weight,
):
    groups = lax.axis_size("dp")
    tensor_size = lax.axis_size("mp")
    bits = groups.bit_length() - 1
    dp = lax.axis_index("dp")
    mp = lax.axis_index("mp")
    x = mp // 2
    core = mp % 2
    row_count, shard_len, width = doc_tokens.shape
    length = shard_len * tensor_size
    query_local, query_len, _ = query_tokens.shape
    chip_queries = query_local * 2
    buckets = position_bias.shape[0]
    hidden_local = gate_weight.shape[1]
    doc_local = retrieved.shape[2]
    docs_row = doc_local // row_count
    query_total = query_keep.shape[0]
    vector_width = proj_weight.shape[1]
    inner = query_weight.shape[1]

    def over(axis, size, mask):
        pairs = [(i, i ^ mask) for i in range(size)]
        return lambda values: lax.ppermute(values, axis, pairs)

    to_x = over("mp", tensor_size, 2)
    to_core = over("mp", tensor_size, 1)
    to_dp = [over("dp", groups, 1 << b) for b in range(bits)]
    dp_bit = [(dp >> b) & 1 for b in range(bits)]

    def exchange(steps):
        dp_mask = sum(1 << b for axis, b in steps if axis == "dp")
        mp_mask = 2 if any(axis == "x" for axis, b in steps) else 0
        pairs = [
            (i, ((i // tensor_size) ^ dp_mask) * tensor_size + ((i % tensor_size) ^ mp_mask))
            for i in range(groups * tensor_size)
        ]
        return lambda values: lax.ppermute(values, ("dp", "mp"), pairs)

    def rounds(order):
        out = []
        for i in range(0, len(order), 2):
            steps = order[i : i + 2]
            if len(steps) == 1:
                out.append([exchange(steps)])
            else:
                out.append([exchange(steps[:1]), exchange(steps[1:]), exchange(steps)])
        return out

    kept_rows = lax.dynamic_index_in_dim(doc_tokens, x, 0, keepdims=False)
    sent_rows = lax.dynamic_index_in_dim(doc_tokens, 1 - x, 0, keepdims=False)
    far_rows = to_x(sent_rows)
    kept_tokens = jnp.concatenate(
        [kept_rows, query_tokens.reshape(query_local * query_len, width)], axis=0
    )
    near_tokens = to_core(kept_tokens)
    cross_rows = to_core(far_rows)

    own_qkv, qkv_half, output_half, gate_half, up_half, *down_halves = pack(
        jnp.stack(dp_bit[:2]),
        jnp.transpose(after(query_weight, sent_rows)),
        jnp.transpose(key_weight),
        jnp.transpose(value_weight),
        output_weight,
        gate_weight,
        up_weight,
        down_weight,
        position_bias,
    )
    near_tiles = bias_tiles(after(position_bias.astype(f32), qkv_half))
    qkv_half = to_x(qkv_half)
    output_half = to_x(output_half)
    far_bias = output_half[inner // 2 :, : position_bias.shape[1]]
    output_half = output_half[: inner // 2]

    def other_half(got, b=0, earlier=()):
        return swapped(dp_bit[b], got, after(to_dp[b](got), earlier))


    row_segments = lax.dynamic_index_in_dim(doc_segments, x, 0, keepdims=False)
    chip_keep = lax.dynamic_slice_in_dim(
        query_keep, (dp * tensor_size + x * 2) * query_local, chip_queries, 0
    ).reshape(-1)
    query_ids = jnp.arange(chip_queries * query_len, dtype=jnp.int32) // query_len + docs_row
    seg_q = jnp.concatenate([row_segments, query_ids])
    seg_k = jnp.concatenate([row_segments, jnp.where(chip_keep > 0, query_ids, -1)])
    blocked = row_segments.reshape(-1, PAIR)
    low = jnp.sum((row_segments[None, :] < blocked[:, :1]).astype(jnp.int32), axis=1)
    high = jnp.sum((row_segments[None, :] <= blocked[:, -1:]).astype(jnp.int32), axis=1)
    low_block = low // BLOCK
    high_block = (high + BLOCK - 1) // BLOCK
    lo = jnp.concatenate([low_block, jnp.full((1,), length // BLOCK - 1, jnp.int32)])
    cnt = jnp.concatenate([(high_block - low_block + 1) // 2, jnp.ones((1,), jnp.int32)])
    ranges = (lo, cnt)

    order = [("dp", b) for b in reversed(range(bits))] + [("x", 0)]
    place = sum((x if axis == "x" else dp_bit[b]) << s for s, (axis, b) in enumerate(order))
    kept_retrieved = (query_keep[:, :, None] * retrieved).reshape(query_total * query_len, doc_local)
    seg_q, seg_k = seg_q[None, :], seg_k[None, :]
    segs = (seg_q, seg_k)
    half_queries = query_total // 2
    query_lanes = -(-half_queries // BLOCK) * BLOCK

    place_mp = mp.reshape(1)
    gain_attn, gain_ffn, gain_final = [g.reshape(1, width) for g in (attn_gain, ffn_gain, final_gain)]
    pieces = (kept_tokens, near_tokens, far_rows, cross_rows)
    tokens, normed_attn, own_heads = enter(place_mp, pieces, gain_attn, own_qkv)
    far_tiles = bias_tiles(after(far_bias.astype(f32), own_heads))
    qkv_half = after(qkv_half, far_tiles)
    gate_half = to_x(after(gate_half, own_heads))
    own_context, own_log = attend(own_heads, ranges, segs, near_tiles[0])
    far_qkv = other_half(qkv_half, 0, own_context)
    gate_half = after(gate_half, own_context)
    up_half = to_x(after(up_half, own_context))
    far_heads = dot_nn(normed_attn, after(far_qkv, gate_half)).astype(bf16)
    far_context, far_log = attend(far_heads, ranges, segs, far_tiles[0])
    far_output = other_half(after(output_half, far_qkv), 0, far_context)
    far_gate = other_half(after(gate_half, far_qkv), 0, far_context)
    up_half = after(up_half, far_context)
    down_halves = [to_x(after(half, far_context)) for half in down_halves]
    tiles = (near_tiles, far_tiles)
    heads = (own_heads, far_heads)
    contexts = (own_context, far_context)
    logs = (own_log, far_log)
    qkv_weights = (own_qkv, far_qkv)
    output_weights = (output_weight, far_output)
    attn_part = sum(
        dot_nn(c, w) for c, w in zip(after(contexts, far_gate, up_half), output_weights)
    ).astype(bf16)
    chosen, pos_rows = choose(
        jnp.stack([core, place, x * docs_row]),
        positives,
        after(kept_retrieved, attn_part),
        query_local,
        query_len,
        bits + 1,
    )
    count = tokens.shape[0] // 3
    mid, normed_ffn, own_gate_up, ffn_sum = ffn_own(
        tokens, attn_part, to_core(attn_part), gain_ffn, gate_weight, up_weight, down_weight, count
    )
    far_up = other_half(after(up_half, attn_part), 1, ffn_sum)
    down_halves = after(down_halves, ffn_sum)
    far_down = jnp.concatenate([other_half(half, b) for b, half in enumerate(down_halves)], axis=1)
    far_gate_up_out, ffn_part = ffn_far(normed_ffn, far_gate, far_up, far_down, ffn_sum, count)
    layer_out, projected, embedded = leave(
        mid, ffn_part, to_core(ffn_part), gain_final, proj_weight, count
    )

    doc_embedded = embedded[:length]
    query_emb = part(embedded[length:], core, 2)
    for moves in rounds(order):
        query_emb = jnp.concatenate([query_emb] + [move(query_emb) for move in moves], axis=0)
    first_doc = jnp.stack([dp * doc_local + x * docs_row, place])
    seg_col = seg_q[:, :length]
    sums, logits, stats = score(
        first_doc, doc_embedded, query_emb, seg_col, chosen, pos_rows, query_len, query_local, docs_row
    )
    for moves in rounds(order[::-1]):
        every = [stats] + [move(stats) for move in moves]
        top = every[0][0:1]
        for moved in every[1:]:
            top = jnp.maximum(top, moved[0:1])
        total = sum(moved[1:2] * jnp.exp(moved[0:1] - top) for moved in every)
        stats = jnp.concatenate([top, total, sum(moved[2:] for moved in every)], axis=0)
    valid = jnp.arange(query_lanes) < half_queries
    loss_sum = jnp.sum(jnp.where(valid, stats[0] + jnp.log(stats[1]) - stats[2], 0.0))
    found_sum = jnp.sum(jnp.where(valid & (stats[3] > 0.5), 1.0, 0.0))
    ends = jnp.broadcast_to(jnp.stack([loss_sum, found_sum])[:, None], (2, BLOCK))
    ends = (ends + to_core(ends)) / query_total
    loss_value = ends[0, 0]
    found_share = ends[1, 0]

    demb, dqe = score_back(
        first_doc,
        doc_embedded,
        query_emb,
        seg_col,
        chosen,
        pos_rows,
        sums,
        logits,
        stats,
        query_len,
        query_local,
        docs_row,
    )
    demb_moved = to_core(demb.astype(bf16))
    for moves in reversed(rounds(order)):
        pieces = jnp.split(dqe, len(moves) + 1, axis=0)
        moved = [move(piece).astype(f32) for move, piece in zip(moves, pieces[1:])]
        dqe = sum(moved, pieces[0].astype(f32)).astype(bf16)
    dqe_moved = to_core(dqe)

    def widen(values):
        return values.astype(f32)

    def narrow(values):
        return values.astype(bf16)

    def added(*values):
        return narrow(sum(widen(v) for v in values[1:]) + widen(values[0]))

    four = [exchange([("dp", 0)]), exchange([("dp", 1)]), exchange([("dp", 0), ("dp", 1)])]
    four_index = (dp % 4).reshape(1)
    rest = range(2, bits)

    def scattered(pieces):
        return (pieces[0],) + tuple(move(piece) for move, piece in zip(four, pieces[1:]))

    def rest_of(values, moved):
        values = added(values, moved)
        for b in rest[1:]:
            values = added(values, to_dp[b](values))
        return values

    def gathered(values):
        return (values,) + tuple(move(values) for move in four)

    def assembled(pieces):
        low = [jnp.where(dp_bit[0] == 0, pieces[0], pieces[1]), jnp.where(dp_bit[0] == 0, pieces[1], pieces[0])]
        high = [jnp.where(dp_bit[0] == 0, pieces[2], pieces[3]), jnp.where(dp_bit[0] == 0, pieces[3], pieces[2])]
        return jnp.concatenate(
            [jnp.where(dp_bit[1] == 0, u, v) for u, v in zip(low + high, high + low)], axis=0
        )

    layer_out_grad, proj_grad, final_gain_part = leave_back(
        core.reshape(1), layer_out, projected, demb, demb_moved, dqe, dqe_moved, gain_final, proj_weight
    )
    proj_part = narrow(part(proj_grad, core, 2))
    proj_moved = to_x(proj_part)
    nf_sum, far_first, far_rest, far_down_grad = ffn_back(
        after(layer_out_grad, proj_part), normed_ffn, far_gate_up_out, far_down, far_gate, far_up, count
    )
    first_moved = to_x(far_first)
    proj_part = added(proj_part, after(proj_moved, far_first))
    proj_moves = [move(proj_part) for move in four]
    nf_part, own_first, own_rest, *down_pieces = ffn_back(
        after(layer_out_grad, proj_part),
        normed_ffn,
        own_gate_up,
        down_weight,
        gate_weight,
        up_weight,
        count,
        four_index,
        nf_sum,
        far_down_grad,
    )
    first_pieces = quarter_sums(four_index, own_first, after(first_moved, nf_part))
    first_moves = scattered(first_pieces)
    rest_moved = to_x(after(far_rest, first_pieces))
    down_moves = scattered(tuple(down_pieces))
    proj_part = added(*after((proj_part, *proj_moves), first_pieces))
    proj_moved = to_dp[rest[0]](proj_part)
    nf_part = after(nf_part, proj_part)
    mid_grad, own_context_grad, far_context_grad, own_out, far_out, ffn_gain_part = mid_back(
        nf_part, to_core(nf_part), mid, layer_out_grad, gain_ffn, contexts, output_weights, count
    )

    far_grads, far_bias_grad = attend_back(
        far_heads,
        far_context_grad,
        far_context,
        far_log,
        ranges,
        segs,
        far_tiles[1],
        buckets,
    )
    down = added(*after(down_moves, far_grads))
    down_kept, down_moved = down[:, hidden_local:], to_x(down[:, :hidden_local])
    far_all, far_more = heads_far(normed_attn, after(far_grads, down), far_out, final_gain_part, ffn_gain_part, far_bias_grad)

    down = added(after(down_moved, far_all), down_kept)
    all_moved = to_x(after(far_all, down))
    first = added(*after(first_moves, far_all))
    rest_pieces = quarter_sums(four_index, own_rest, after(rest_moved, far_all))
    rest_moves = scattered(rest_pieces)
    early = jnp.concatenate([first, down], axis=1)
    early_moved = to_dp[rest[0]](early)
    proj_part = rest_of(proj_part, after(proj_moved, far_all))
    own_grads, own_bias_grad = attend_back(
        own_heads,
        after(own_context_grad, rest_pieces, early, proj_part),
        own_context,
        own_log,
        ranges,
        segs,
        near_tiles[1],
        buckets,
    )

    early = rest_of(early, after(early_moved, own_grads))
    early_all = gathered(early)
    others = added(*after(rest_moves, own_grads))
    others_moved = to_dp[rest[0]](others)
    all_moved = after(all_moved, own_grads)
    more_moved = to_x(after(far_more, all_moved))
    na_kept, na_sent, attn_gain_part = enter_back(
        place_mp, tokens, after(own_grads, others, early, all_moved), far_grads, qkv_weights
    )
    early_all = after(early_all, na_sent)
    proj_moved = to_core(after(proj_part, na_sent))
    all_pieces = heads_own(
        four_index,
        normed_attn,
        own_grads,
        own_out,
        final_gain_part,
        ffn_gain_part,
        attn_gain_part,
        own_bias_grad,
        all_moved,
        after(more_moved, na_sent, early_all, proj_moved),
    )
    all_moves = scattered(all_pieces)
    others = rest_of(others, after(others_moved, all_pieces))

    both = added(*after(all_moves, others))
    both_moved = to_dp[rest[0]](both)
    others_all = gathered(after(others, both))
    na_moved = to_core(after(na_sent, both))

    stay, leaving, query_grad = inputs_back(place_mp, tokens, mid_grad, na_kept, na_moved, gain_attn)
    both = rest_of(both, after(both_moved, others_all, leaving))
    both_all = gathered(both)
    back = to_x(after(leaving, both))
    extra = both[width // 4 :]
    crossing = [(i, i ^ 3) for i in range(tensor_size)]
    extra_moves = (to_x(extra), to_core(extra), lax.ppermute(extra, "mp", crossing))
    cut = hidden_local // 2
    gate_weight_grad, up_weight_grad, down_weight_grad = widened(
        four_index,
        width,
        after((early_all, others_all), extra_moves),
        (
            (((0, 0, cut), (1, 0, cut)), False),
            (((1, cut, cut + hidden_local),), False),
            (((0, cut, cut + hidden_local),), True),
        ),
        "widen_ffn",
    )
    extra_moves, back = after((extra_moves, back), up_weight_grad)
    extra = widen(extra)
    attn_gain_grad = extra[2] + sum(widen(moved[2]) for moved in extra_moves)
    proj_weight_grad = widen(swapped(core, proj_part, proj_moved))
    position_bias_grad = jnp.transpose(extra[3 : 3 + position_bias.shape[1], :buckets])
    back = widen(back)
    doc_grad = jnp.stack([jnp.where(x == 0, stay, back), jnp.where(x == 0, back, stay)], axis=0)

    query_weight_grad, key_weight_grad, value_weight_grad, output_weight_grad = widened(
        four_index,
        width,
        (after(both_all, doc_grad, attn_gain_grad, proj_weight_grad),),
        tuple((((0, i * inner, (i + 1) * inner),), True) for i in range(4)),
        "widen_heads",
    )

    return (
        loss_value,
        found_share,
        doc_grad,
        query_grad.reshape(query_local, query_len, width),
        attn_gain_grad,
        jnp.transpose(query_weight_grad),
        jnp.transpose(key_weight_grad),
        jnp.transpose(value_weight_grad),
        output_weight_grad,
        position_bias_grad,
        extra[1],
        gate_weight_grad,
        up_weight_grad,
        down_weight_grad,
        extra[0],
        proj_weight_grad,
    )


def solution(mesh):
    placed = (
        P("dp", "mp", None),
        P(("dp", "mp"), None, None),
        P("dp", None),
        P(),
        P(None, None, "dp"),
        P(),
        P(),
        P(None, "mp"),
        P(None, "mp"),
        P(None, "mp"),
        P("mp", None),
        P(None, "mp"),
        P(),
        P(None, "mp"),
        P(None, "mp"),
        P("mp", None),
        P(),
        P(),
    )
    return jax.shard_map(
        shards,
        mesh=mesh,
        in_specs=placed,
        out_specs=(
            P(),
            P(),
            P("dp", "mp", None),
            P(("dp", "mp"), None, None),
            P(),
            P(None, "mp"),
            P(None, "mp"),
            P(None, "mp"),
            P("mp", None),
            P(None, "mp"),
            P(),
            P(None, "mp"),
            P(None, "mp"),
            P("mp", None),
            P(),
            P(),
        ),
        check_vma=False,
    )
```

```python
from functools import partial

import jax
import jax.numpy as jnp
import numpy as np
from jax import lax
from jax.experimental import pallas as pl
from jax.experimental.pallas import tpu as pltpu
from jax.sharding import PartitionSpec as P

epsilon = 1e-06
sharpness = 16.0
smoothing_divisor = 0.05
masked_score = -1e30
BLOCK = 128
PAIR = 2 * BLOCK
bf16 = jnp.bfloat16
f32 = jnp.float32


def bucket_starts(buckets):
    half = buckets // 2
    exact = half // 2
    distance = np.arange(0, 2048)
    scaled = (
        np.log(np.maximum(distance, 1) / exact) / np.log(128.0 / exact) * (half - exact)
    )
    far = np.minimum(exact + np.floor(np.maximum(scaled, 0.0)), half - 1)
    bucket = np.where(distance < exact, distance, far)
    return [int(np.argmax(bucket >= b)) for b in range(half)]


def dot_nn(a, b):
    return lax.dot_general(a, b, (((1,), (0,)), ((), ())), preferred_element_type=f32)


def dot_nt(a, b):
    return lax.dot_general(a, b, (((1,), (1,)), ((), ())), preferred_element_type=f32)


def dot_tn(a, b):
    return lax.dot_general(a, b, (((0,), (0,)), ((), ())), preferred_element_type=f32)


def dot_exact(a, b):
    return lax.dot_general(
        a, b, (((1,), (0,)), ((), ())), precision=lax.Precision.HIGHEST, preferred_element_type=f32
    )


def params(limit_mib=40):
    return pltpu.CompilerParams(vmem_limit_bytes=limit_mib << 20)


def cost(micros):
    return pl.CostEstimate(flops=int(micros * 3e9), transcendentals=0, bytes_accessed=1 << 10)


def bias_kernel(starts, heads, tab_ref, t_ref, tt_ref):
    half = len(starts)
    sub = lax.broadcasted_iota(jnp.int32, (BLOCK, BLOCK), 0)
    lane = lax.broadcasted_iota(jnp.int32, (BLOCK, BLOCK), 1)
    for ref, base in ((t_ref, lane - sub), (tt_ref, sub - lane)):
        for d in (-1, 0, 1):
            offset = base + BLOCK * d
            n = jnp.abs(offset)
            for h in range(heads):
                low = high = None
                if d <= 0:
                    low = jnp.full((BLOCK, BLOCK), tab_ref[0, h], f32)
                    for b in range(1, half):
                        low = jnp.where(n >= starts[b], tab_ref[b, h], low)
                if d >= 0:
                    high = jnp.full((BLOCK, BLOCK), tab_ref[half, h], f32)
                    for b in range(1, half):
                        high = jnp.where(n >= starts[b], tab_ref[half + b, h], high)
                if d < 0:
                    tile = low
                elif d > 0:
                    tile = high
                else:
                    tile = jnp.where(offset > 0, high, low)
                ref[h, d + 2] = tile
        for h in range(heads):
            ref[h, 0] = jnp.full((BLOCK, BLOCK), tab_ref[half - 1, h], f32)
            ref[h, 4] = jnp.full((BLOCK, BLOCK), tab_ref[2 * half - 1, h], f32)


def bias_tiles(table):
    buckets, heads = table.shape
    starts = bucket_starts(buckets)
    shape = jax.ShapeDtypeStruct((heads, 5, BLOCK, BLOCK), f32)
    return pl.pallas_call(
        partial(bias_kernel, starts, heads),
        in_specs=[pl.BlockSpec(memory_space=pltpu.SMEM)],
        out_shape=(shape, shape),
        compiler_params=params(6),
        cost_estimate=cost(2),
        name="bias_tiles",
    )(table)


def clipped(d):
    return jnp.minimum(jnp.maximum(d, -2), 2) + 2


def column(row):
    return jnp.transpose(jnp.broadcast_to(row, (8, row.shape[1])))[:, 0:1]


def attend_kernel(heads, size, most, lo_ref, cnt_ref, qkv_ref, segq_ref, segk_ref, t_ref, ctx_ref, lse_ref, k_s, v_s):
    b = pl.program_id(0)
    inner = heads * size
    last = pl.num_programs(0) - 1

    @pl.when(b == 0)
    def _():
        for h in range(heads):
            k_s[h] = qkv_ref[:, inner + h * size : inner + (h + 1) * size]
            v_s[h] = qkv_ref[:, 2 * inner + h * size : 2 * inner + (h + 1) * size]

    def window(first, count, lo, pairs):
        rows = pl.ds(pl.multiple_of(first * BLOCK, BLOCK), count * BLOCK)
        block = qkv_ref[rows, :inner]
        seg_col = column(segq_ref[:, rows])
        spans = [pl.ds(pl.multiple_of((lo + 2 * i) * BLOCK, BLOCK), PAIR) for i in range(pairs)]
        allowed = [seg_col == segk_ref[:, span] for span in spans]
        outs, logs = [], []
        for h in range(heads):
            query = block[:, h * size : (h + 1) * size]
            scores = []
            for i, span in enumerate(spans):
                s = dot_nt(query, k_s[h, span, :])
                bias = jnp.concatenate(
                    [
                        jnp.concatenate(
                            [t_ref[h, clipped(lo + 2 * i + c - first - r)] for c in range(2)], axis=1
                        )
                        for r in range(count)
                    ],
                    axis=0,
                )
                scores.append(jnp.where(allowed[i], s + bias, masked_score))
            top = scores[0]
            for s in scores[1:]:
                top = jnp.maximum(top, s)
            largest = jnp.max(top, axis=1, keepdims=True)
            total = acc = None
            for i, span in enumerate(spans):
                p = jnp.exp(scores[i] - largest)
                total = p if total is None else total + p
                more = dot_nn(p.astype(bf16), v_s[h, span, :])
                acc = more if acc is None else acc + more
            total = jnp.sum(total, axis=1, keepdims=True)
            outs.append((acc / total).astype(bf16))
            lse = jnp.broadcast_to(largest + jnp.log(total), (count * BLOCK, BLOCK))
            lse_ref[h : h + 1, rows] = jnp.transpose(lse)[0:1, :]
        ctx_ref[rows, :] = jnp.concatenate(outs, axis=1)

    for pairs in range(1, most + 1):
        pl.when((b < last) & (cnt_ref[b] == pairs))(partial(window, 2 * b, 2, lo_ref[b], pairs))
    pl.when(b == last)(partial(window, 2 * b, 1, lo_ref[b], 1))


def attend(qkv, ranges, segs, tiles):
    lo, cnt = ranges
    seg_q, seg_k = segs
    total, wide = qkv.shape
    heads = tiles.shape[0]
    inner = wide // 3
    size = inner // heads
    steps = lo.shape[0]
    whole = lambda b, *_: (0, 0)
    return pl.pallas_call(
        partial(attend_kernel, heads, size, steps - 1),
        grid_spec=pltpu.PrefetchScalarGridSpec(
            num_scalar_prefetch=2,
            grid=(steps,),
            in_specs=[
                pl.BlockSpec((total, wide), whole, pipeline_mode=pl.Buffered(1)),
                pl.BlockSpec((1, total), whole, pipeline_mode=pl.Buffered(1)),
                pl.BlockSpec((1, total), whole, pipeline_mode=pl.Buffered(1)),
                pl.BlockSpec((heads, 5, BLOCK, BLOCK), lambda b, *_: (0, 0, 0, 0), pipeline_mode=pl.Buffered(1)),
            ],
            out_specs=[
                pl.BlockSpec((total, inner), whole),
                pl.BlockSpec((8, total), whole),
            ],
            scratch_shapes=[
                pltpu.VMEM((heads, total, size), bf16),
                pltpu.VMEM((heads, total, size), bf16),
            ],
        ),
        out_shape=(
            jax.ShapeDtypeStruct((total, inner), bf16),
            jax.ShapeDtypeStruct((8, total), f32),
        ),
        compiler_params=params(12),
        cost_estimate=cost(9),
        name="attend",
    )(lo, cnt, qkv, seg_q, seg_k, tiles)


def attend_back_kernel(
    starts,
    heads,
    size,
    most,
    lo_ref,
    cnt_ref,
    qkv_ref,
    do_ref,
    ctx_ref,
    lse_ref,
    segk_ref,
    segq_ref,
    tt_ref,
    grad_ref,
    bias_ref,
    q_s,
    do_s,
    dq_s,
    delta_s,
    d_s,
):
    b = pl.program_id(0)
    last = pl.num_programs(0) - 1
    inner = heads * size
    half = len(starts)

    @pl.when(b == 0)
    def _():
        prod = do_ref[...].astype(f32) * ctx_ref[...].astype(f32)
        high = prod.astype(bf16)
        low = (prod - high.astype(f32)).astype(bf16)
        row = lax.broadcasted_iota(jnp.int32, (8, inner), 0)
        col = lax.broadcasted_iota(jnp.int32, (8, inner), 1)
        pick = ((col >= row * size) & (col < (row + 1) * size)).astype(f32).astype(bf16)
        delta_s[...] = dot_nt(pick, high) + dot_nt(pick, low)
        for h in range(heads):
            q_s[h] = qkv_ref[:, h * size : (h + 1) * size]
            do_s[h] = do_ref[:, h * size : (h + 1) * size]
        dq_s[...] = jnp.zeros(dq_s.shape, f32)
        d_s[...] = jnp.zeros(d_s.shape, f32)

    def window(first, count, lo, pairs):
        rows = pl.ds(pl.multiple_of(first * BLOCK, BLOCK), count * BLOCK)
        block = qkv_ref[rows, inner:]
        seg_col = column(segk_ref[:, rows])
        spans = [pl.ds(pl.multiple_of((lo + 2 * i) * BLOCK, BLOCK), PAIR) for i in range(pairs)]
        allowed = [seg_col == segq_ref[:, span] for span in spans]
        dks, dvs = [], []
        for h in range(heads):
            key = block[:, h * size : (h + 1) * size]
            value = block[:, inner + h * size : inner + (h + 1) * size]
            dk = dv = None
            for i, span in enumerate(spans):
                q = q_s[h, span, :]
                do = do_s[h, span, :]
                s = dot_nt(key, q)
                dp = dot_nt(value, do)
                at = [[clipped(first + r - lo - 2 * i - c) for c in range(2)] for r in range(count)]
                bias = jnp.concatenate(
                    [
                        jnp.concatenate([tt_ref[h, at[r][c]] for c in range(2)], axis=1)
                        for r in range(count)
                    ],
                    axis=0,
                )
                p = jnp.where(allowed[i], jnp.exp(s + bias - lse_ref[h : h + 1, span]), 0.0)
                ds = p * (dp - delta_s[h : h + 1, span])
                for r in range(count):
                    for c in range(2):
                        d_s[h, at[r][c]] += ds[
                            r * BLOCK : (r + 1) * BLOCK, c * BLOCK : (c + 1) * BLOCK
                        ]
                ds16 = ds.astype(bf16)
                dv_more = dot_nn(p.astype(bf16), do)
                dk_more = dot_nn(ds16, q)
                dv = dv_more if dv is None else dv + dv_more
                dk = dk_more if dk is None else dk + dk_more
                dq_s[h, :, span] += dot_tn(key, ds16)
            dks.append(dk)
            dvs.append(dv)
        grad_ref[rows, inner:] = jnp.concatenate(dks + dvs, axis=1).astype(bf16)

    for pairs in range(1, most + 1):
        pl.when((b < last) & (cnt_ref[b] == pairs))(partial(window, 2 * b, 2, lo_ref[b], pairs))
    pl.when(b == last)(partial(window, 2 * b, 1, lo_ref[b], 1))

    @pl.when(b == last)
    def _():
        grad_ref[:, :inner] = jnp.concatenate([jnp.transpose(dq_s[h]) for h in range(heads)], axis=1).astype(bf16)
        sub = lax.broadcasted_iota(jnp.int32, (BLOCK, BLOCK), 0)
        lane = lax.broadcasted_iota(jnp.int32, (BLOCK, BLOCK), 1)
        below = lane + sub > BLOCK - 1
        reverse = (lane + sub == BLOCK - 1).astype(f32)
        bucket_row = lax.broadcasted_iota(jnp.int32, (2 * half, BLOCK), 0)
        line_lane = lax.broadcasted_iota(jnp.int32, (2 * half, BLOCK), 1)
        picks = {}
        for d in (-1, 0, 1):
            for low in (False, True):
                offset = line_lane + (1 if low else 1 - BLOCK) + BLOCK * d
                n = jnp.abs(offset)
                bucket = jnp.where(offset > 0, half, 0)
                for e in range(1, half):
                    bucket = bucket + (n >= starts[e]).astype(jnp.int32)
                picks[d, low] = bucket == bucket_row
        for h in range(heads):
            whole = jnp.zeros((2 * half, BLOCK), f32)
            for d in (-1, 0, 1):
                tile = dot_exact(d_s[h, d + 2], reverse)
                for low in (False, True):
                    kept = jnp.where(below == low, tile, 0.0)
                    line = jnp.sum(
                        pltpu.roll(kept, 0, 1, stride=1, stride_axis=0), axis=0, keepdims=True
                    )
                    whole = whole + jnp.where(picks[d, low], line, 0.0)
            for e, d in ((half - 1, 0), (2 * half - 1, 4)):
                far = jnp.sum(d_s[h, d], axis=0, keepdims=True)
                whole = whole + jnp.where(bucket_row == e, far, 0.0)
            bias_ref[h] = whole


def attend_back(qkv, context_grad, context, lse, ranges, segs, tiles, buckets):
    lo, cnt = ranges
    seg_q, seg_k = segs
    total, wide = qkv.shape
    heads = tiles.shape[0]
    inner = wide // 3
    size = inner // heads
    steps = lo.shape[0]
    starts = bucket_starts(buckets)
    whole = lambda b, *_: (0, 0)
    return pl.pallas_call(
        partial(attend_back_kernel, starts, heads, size, steps - 1),
        grid_spec=pltpu.PrefetchScalarGridSpec(
            num_scalar_prefetch=2,
            grid=(steps,),
            in_specs=[
                pl.BlockSpec((total, wide), whole, pipeline_mode=pl.Buffered(1)),
                pl.BlockSpec((total, inner), whole, pipeline_mode=pl.Buffered(1)),
                pl.BlockSpec((total, inner), whole, pipeline_mode=pl.Buffered(1)),
                pl.BlockSpec((8, total), whole, pipeline_mode=pl.Buffered(1)),
                pl.BlockSpec((1, total), whole, pipeline_mode=pl.Buffered(1)),
                pl.BlockSpec((1, total), whole, pipeline_mode=pl.Buffered(1)),
                pl.BlockSpec((heads, 5, BLOCK, BLOCK), lambda b, *_: (0, 0, 0, 0), pipeline_mode=pl.Buffered(1)),
            ],
            out_specs=[
                pl.BlockSpec((total, wide), whole),
                pl.BlockSpec((heads, buckets, BLOCK), lambda b, *_: (0, 0, 0)),
            ],
            scratch_shapes=[
                pltpu.VMEM((heads, total, size), bf16),
                pltpu.VMEM((heads, total, size), bf16),
                pltpu.VMEM((heads, size, total), f32),
                pltpu.VMEM((8, total), f32),
                pltpu.VMEM((heads, 5, BLOCK, BLOCK), f32),
            ],
        ),
        out_shape=(
            jax.ShapeDtypeStruct((total, wide), bf16),
            jax.ShapeDtypeStruct((heads, buckets, BLOCK), f32),
        ),
        compiler_params=params(16),
        cost_estimate=cost(15),
        name="attend_back",
    )(lo, cnt, qkv, context_grad, context, lse, seg_k, seg_q, tiles)


def pool_matrix(shape, axis, me, query_len, query_local):
    token = lax.broadcasted_iota(jnp.int32, shape, axis)
    query = lax.broadcasted_iota(jnp.int32, shape, 1 - axis)
    span = query_len * query_local
    holder = jnp.bitwise_xor(token // span, me)
    return (holder * query_local + token % span // query_len == query).astype(f32)


def score_kernel(query_len, query_local, docs, first_ref, emb_ref, qe_ref, seg_ref, chosen_ref, pos_ref, sums_ref, logit_ref, stat_ref, acc_s):
    b = pl.program_id(0)
    count = qe_ref.shape[0]

    @pl.when(b == 0)
    def _():
        acc_s[...] = jnp.zeros(acc_s.shape, f32)

    near = jnp.exp(sharpness * (dot_nt(emb_ref[...], qe_ref[...]) - 1.0))
    seg = column(seg_ref[...])
    for d in range(docs):
        acc_s[d : d + 1, :] += jnp.sum(jnp.where(seg == d, near, 0.0), axis=0, keepdims=True)

    @pl.when(b == pl.num_programs(0) - 1)
    def _():
        sums = acc_s[:docs, :]
        sums_ref[...] = acc_s[...]
        chosen = chosen_ref[:docs, :]
        smooth = 1.0 + jnp.log(sums) / sharpness
        pool = pool_matrix((count, pos_ref.shape[1]), 0, first_ref[1], query_len, query_local)
        picked = dot_exact(chosen * smooth, pool)
        counts = dot_exact(chosen, pool)
        logits = picked / jnp.maximum(counts, 1.0) / smoothing_divisor
        top = jnp.max(logits, axis=0, keepdims=True)
        spread = jnp.sum(jnp.exp(logits - top), axis=0, keepdims=True)
        doc = lax.broadcasted_iota(jnp.int32, logits.shape, 0) + first_ref[0]
        mine = doc == pos_ref[0:1, :]
        stat_ref[0:1, :] = top
        stat_ref[1:2, :] = spread
        stat_ref[2:3, :] = jnp.sum(jnp.where(mine, logits, 0.0), axis=0, keepdims=True)
        stat_ref[3:4, :] = jnp.sum(jnp.where(mine, counts, 0.0), axis=0, keepdims=True)
        stat_ref[4:8, :] = jnp.zeros((4, pos_ref.shape[1]), f32)
        logit_ref[0:docs, :] = logits
        logit_ref[docs : 2 * docs, :] = counts


def score(first, emb, query_emb, seg_col, chosen, positives, query_len, query_local, docs):
    count, width = query_emb.shape
    lanes = positives.shape[1]
    length = emb.shape[0]
    blocks = length // PAIR
    whole = lambda b, *_: (0, 0)
    return pl.pallas_call(
        partial(score_kernel, query_len, query_local, docs),
        grid_spec=pltpu.PrefetchScalarGridSpec(
            num_scalar_prefetch=1,
            grid=(blocks,),
            in_specs=[
                pl.BlockSpec((PAIR, width), lambda b, *_: (b, 0)),
                pl.BlockSpec((count, width), whole, pipeline_mode=pl.Buffered(1)),
                pl.BlockSpec((1, PAIR), lambda b, *_: (0, b)),
                pl.BlockSpec((8, count), whole, pipeline_mode=pl.Buffered(1)),
                pl.BlockSpec((8, lanes), whole, pipeline_mode=pl.Buffered(1)),
            ],
            out_specs=[
                pl.BlockSpec((8, count), whole),
                pl.BlockSpec((8, lanes), whole),
                pl.BlockSpec((8, lanes), whole),
            ],
            scratch_shapes=[pltpu.VMEM((8, count), f32)],
        ),
        out_shape=(
            jax.ShapeDtypeStruct((8, count), f32),
            jax.ShapeDtypeStruct((8, lanes), f32),
            jax.ShapeDtypeStruct((8, lanes), f32),
        ),
        compiler_params=params(14),
        cost_estimate=cost(5),
        name="score",
    )(first, emb, query_emb, seg_col, chosen, positives)


def score_back_kernel(query_len, query_local, docs, first_ref, emb_ref, qe_ref, seg_ref, chosen_ref, pos_ref, sums_ref, logit_ref, stat_ref, demb_ref, dqe_ref, grad_s, dq_s):
    b = pl.program_id(0)
    count = qe_ref.shape[0]

    @pl.when(b == 0)
    def _():
        logits = logit_ref[0:docs, :]
        counts = logit_ref[docs : 2 * docs, :]
        doc = lax.broadcasted_iota(jnp.int32, logits.shape, 0) + first_ref[0]
        mine = (doc == pos_ref[0:1, :]).astype(f32)
        share = jnp.exp(logits - stat_ref[0:1, :]) / stat_ref[1:2, :]
        grad = (share - mine) / smoothing_divisor / jnp.maximum(counts, 1.0)
        spread = pool_matrix((logits.shape[1], count), 1, first_ref[1], query_len, query_local)
        grad_s[0:docs, :] = dot_exact(grad, spread) * chosen_ref[:docs, :] / sums_ref[:docs, :]
        dq_s[...] = jnp.zeros(dq_s.shape, f32)

    emb = emb_ref[...]
    near = jnp.exp(sharpness * (dot_nt(emb, qe_ref[...]) - 1.0))
    seg = column(seg_ref[...])
    weight = jnp.broadcast_to(grad_s[0:1, :], near.shape)
    for d in range(1, docs):
        weight = jnp.where(seg == d, grad_s[d : d + 1, :], weight)
    grad = (near * weight).astype(bf16)
    demb_ref[...] = dot_nn(grad, qe_ref[...])
    dq_s[...] += dot_tn(emb, grad)

    @pl.when(b == pl.num_programs(0) - 1)
    def _():
        dqe_ref[...] = jnp.transpose(dq_s[...]).astype(bf16)


def score_back(first, emb, query_emb, seg_col, chosen, positives, sums, logits, stats, query_len, query_local, docs):
    count, width = query_emb.shape
    lanes = positives.shape[1]
    length = emb.shape[0]
    blocks = length // PAIR
    whole = lambda b, *_: (0, 0)
    return pl.pallas_call(
        partial(score_back_kernel, query_len, query_local, docs),
        grid_spec=pltpu.PrefetchScalarGridSpec(
            num_scalar_prefetch=1,
            grid=(blocks,),
            in_specs=[
                pl.BlockSpec((PAIR, width), lambda b, *_: (b, 0)),
                pl.BlockSpec((count, width), whole, pipeline_mode=pl.Buffered(1)),
                pl.BlockSpec((1, PAIR), lambda b, *_: (0, b)),
                pl.BlockSpec((8, count), whole, pipeline_mode=pl.Buffered(1)),
                pl.BlockSpec((8, lanes), whole, pipeline_mode=pl.Buffered(1)),
                pl.BlockSpec((8, count), whole, pipeline_mode=pl.Buffered(1)),
                pl.BlockSpec((8, lanes), whole, pipeline_mode=pl.Buffered(1)),
                pl.BlockSpec((8, lanes), whole, pipeline_mode=pl.Buffered(1)),
            ],
            out_specs=[
                pl.BlockSpec((PAIR, width), lambda b, *_: (b, 0)),
                pl.BlockSpec((count, width), whole),
            ],
            scratch_shapes=[pltpu.VMEM((8, count), f32), pltpu.VMEM((width, count), f32)],
        ),
        out_shape=(
            jax.ShapeDtypeStruct((length, width), f32),
            jax.ShapeDtypeStruct((count, width), bf16),
        ),
        compiler_params=params(18),
        cost_estimate=cost(5),
        name="score_back",
    )(first, emb, query_emb, seg_col, chosen, positives, sums, logits, stats)


def full(*shape):
    return pl.BlockSpec(shape, lambda *_: (0,) * len(shape), pipeline_mode=pl.Buffered(1))


def kept(*shape):
    return pl.BlockSpec(shape, lambda *_: (0,) * len(shape))


def rows_of(count, width):
    return pl.BlockSpec((count, width), lambda b, *_: (b, 0))


SCALARS = pl.BlockSpec(memory_space=pltpu.SMEM)


def like(shape, dtype):
    return jax.ShapeDtypeStruct(shape, dtype)


def rms(values):
    return lax.rsqrt(jnp.mean(values * values, axis=-1, keepdims=True) + epsilon)


def choose_kernel(query_local, query_len, steps, place_ref, pos_ref, ret_ref, chosen_ref, rows_ref, ret_s):
    core, me = place_ref[0], place_ref[1]
    span = query_local * query_len
    blocks = ret_s.shape[0] // span

    def holder(p):
        return sum(((p >> s) & 1) << (steps - 1 - s) for s in range(steps))

    def held(p):
        return holder(jnp.bitwise_xor(me, p)) * 2 + core

    for p in range(blocks):
        start = pl.multiple_of(held(p) * span, span)
        ret_s[p * span : (p + 1) * span, :] = ret_ref[pl.ds(start, span), :].astype(f32)
    docs = ret_s.shape[1]
    row = lax.broadcasted_iota(jnp.int32, (docs, docs), 0)
    col = lax.broadcasted_iota(jnp.int32, (docs, docs), 1)
    shift = jnp.where(row < docs // 2, row + place_ref[2], -1)
    chosen_ref[...] = dot_nt((shift == col).astype(f32), ret_s[...])
    lane = lax.broadcasted_iota(jnp.int32, rows_ref.shape, 1)
    rows = jnp.full(rows_ref.shape, -1, jnp.int32)
    for p in range(blocks):
        for i in range(query_local):
            query = (holder(p) * 2 + core) * query_local + i
            rows = jnp.where(lane == p * query_local + i, pos_ref[query], rows)
    rows_ref[...] = rows


def choose(place, positives, retrieved, query_local, query_len, steps):
    total, docs = retrieved.shape
    lanes = -(-(total // 2 // query_len) // BLOCK) * BLOCK
    return pl.pallas_call(
        partial(choose_kernel, query_local, query_len, steps),
        in_specs=[SCALARS, SCALARS, pl.BlockSpec(memory_space=pltpu.VMEM)],
        out_shape=(like((8, total // 2), f32), like((8, lanes), jnp.int32)),
        scratch_shapes=[pltpu.VMEM((total // 2, docs), f32)],
        compiler_params=params(20),
        cost_estimate=cost(1),
        name="choose",
    )(place, positives, retrieved)


def pack_kernel(bit_ref, q_ref, k_ref, v_ref, o_ref, g_ref, u_ref, d_ref, b_ref, qkv_ref, half_qkv, half_o, half_g, half_u, half_d0, half_d1):
    inner = q_ref.shape[0]

    def half(ref, bit):
        rows = ref.shape[0] // 2
        return ref[pl.ds(pl.multiple_of(bit_ref[bit] * rows, rows), rows), :]

    for i, ref in enumerate((q_ref, k_ref, v_ref)):
        qkv_ref[:, i * inner : (i + 1) * inner] = jnp.transpose(ref[...])
    half_qkv[...] = half(qkv_ref, 0)
    rows = o_ref.shape[0] // 2
    half_o[:rows, :] = half(o_ref, 0)
    half_o[rows:, :] = jnp.zeros((half_o.shape[0] - rows, half_o.shape[1]), bf16)
    half_o[rows:, : b_ref.shape[1]] = b_ref[...]
    half_g[...] = half(g_ref, 0)
    half_u[...] = half(u_ref, 1)
    cut = half_d0.shape[1]
    half_d0[...] = half(d_ref, 0)[:, :cut]
    half_d1[...] = half(d_ref, 1)[:, cut:]


def pack(bits, q, k, v, o, gate, up, down, bias):
    inner, depth = q.shape
    hidden = gate.shape[1]
    shapes = (
        (depth, 3 * inner),
        (depth // 2, 3 * inner),
        (inner // 2 + bias.shape[0], depth),
        (depth // 2, hidden),
        (depth // 2, hidden),
        (hidden // 2, depth // 2),
        (hidden // 2, depth // 2),
    )
    weights = (q, k, v, o, gate, up, down, bias)
    return pl.pallas_call(
        pack_kernel,
        grid=(1,),
        in_specs=[SCALARS] + [kept(*w.shape) for w in weights],
        out_specs=[kept(*shape) for shape in shapes],
        out_shape=tuple(like(shape, bf16) for shape in shapes),
        compiler_params=params(60),
        cost_estimate=cost(3),
        name="pack",
    )(bits, *weights)


def enter_kernel(place_ref, kept_ref, near_ref, far_ref, cross_ref, gain_ref, w_ref, tok_ref, norm_ref, heads_ref):
    gain = gain_ref[...].astype(f32)
    mp = place_ref[0]
    shard = far_ref.shape[0]
    query = kept_ref.shape[0] - shard
    pieces = [(kept_ref, 0), (near_ref, 1), (far_ref, 2), (cross_ref, 3)]
    spans = [(ref, 0, shard, jnp.bitwise_xor(mp, i) * shard) for ref, i in pieces]
    spans += [
        (ref, shard, query, 4 * shard + jnp.bitwise_xor(mp % 2, i) * query) for ref, i in pieces[:2]
    ]
    for ref, first, count, start in spans:
        rows = pl.ds(pl.multiple_of(start, count), count)
        piece = ref[first : first + count, :]
        values = piece.astype(f32)
        normed = (values * rms(values) * gain).astype(bf16)
        tok_ref[rows, :] = piece
        norm_ref[rows, :] = normed
        heads_ref[rows, :] = dot_nn(normed, w_ref[...]).astype(bf16)


def enter(place, pieces, gain, weight):
    total = sum(piece.shape[0] for piece in pieces)
    depth, wide = weight.shape
    return pl.pallas_call(
        enter_kernel,
        in_specs=[SCALARS] + [pl.BlockSpec(memory_space=pltpu.VMEM)] * 6,
        out_shape=(like((total, depth), bf16), like((total, depth), bf16), like((total, wide), bf16)),
        compiler_params=params(12),
        cost_estimate=cost(3),
        name="enter",
    )(place, *pieces, gain, weight)


def gelu_parts(gate):
    inner = 0.7978845608028654 * (gate + 0.044715 * gate * gate * gate)
    return 0.5 * (1.0 + jnp.tanh(inner))


def ffn_own_kernel(tok_ref, near_ref, moved_ref, gain_ref, g_ref, u_ref, d_ref, mid_ref, norm_ref, gu_ref, part_ref):
    hidden = g_ref.shape[1]
    mid = tok_ref[...].astype(f32) + (near_ref[...].astype(f32) + moved_ref[...].astype(f32))
    mid_ref[...] = mid.astype(bf16)
    normed = (mid * rms(mid) * gain_ref[...].astype(f32)).astype(bf16)
    norm_ref[...] = normed
    gate = dot_nn(normed, g_ref[...])
    up = dot_nn(normed, u_ref[...])
    gu_ref[:, :hidden] = gate.astype(bf16)
    gu_ref[:, hidden:] = up.astype(bf16)
    part_ref[...] = dot_nn((gate * gelu_parts(gate) * up).astype(bf16), d_ref[...]).astype(bf16)


def ffn_own(tokens, near, moved, gain, gate, up, down, count):
    total, depth = tokens.shape
    hidden = gate.shape[1]
    return pl.pallas_call(
        ffn_own_kernel,
        grid=(total // count,),
        in_specs=[rows_of(count, depth)] * 3
        + [full(1, depth), full(depth, hidden), full(depth, hidden), full(hidden, depth)],
        out_specs=[
            rows_of(count, depth),
            rows_of(count, depth),
            rows_of(count, 2 * hidden),
            rows_of(count, depth),
        ],
        out_shape=(
            like((total, depth), bf16),
            like((total, depth), bf16),
            like((total, 2 * hidden), bf16),
            like((total, depth), bf16),
        ),
        compiler_params=params(16),
        cost_estimate=cost(5),
        name="ffn_own",
    )(tokens, near, moved, gain, gate, up, down)


def ffn_far_kernel(norm_ref, g_ref, u_ref, d_ref, part_ref, gu_ref, out_ref):
    hidden = d_ref.shape[0]
    normed = norm_ref[...]
    gate = dot_nn(normed, g_ref[...])
    up = dot_nn(normed, u_ref[...])
    gu_ref[:, :hidden] = gate.astype(bf16)
    gu_ref[:, hidden:] = up.astype(bf16)
    more = dot_nn((gate * gelu_parts(gate) * up).astype(bf16), d_ref[...])
    out_ref[...] = (part_ref[...].astype(f32) + more).astype(bf16)


def ffn_far(normed, gate, up, down, partial_sum, count):
    total, depth = normed.shape
    hidden = down.shape[0]
    return pl.pallas_call(
        ffn_far_kernel,
        grid=(total // count,),
        in_specs=[
            rows_of(count, depth),
            full(depth, hidden),
            full(depth, hidden),
            full(hidden, depth),
            rows_of(count, depth),
        ],
        out_specs=[rows_of(count, 2 * hidden), rows_of(count, depth)],
        out_shape=(like((total, 2 * hidden), bf16), like((total, depth), bf16)),
        compiler_params=params(14),
        cost_estimate=cost(5),
        name="ffn_far",
    )(normed, gate, up, down, partial_sum)


def leave_kernel(mid_ref, near_ref, moved_ref, gain_ref, w_ref, out_ref, proj_ref, emb_ref):
    out = mid_ref[...].astype(f32) + (near_ref[...].astype(f32) + moved_ref[...].astype(f32))
    out_ref[...] = out.astype(bf16)
    normed = (out * rms(out) * gain_ref[...].astype(f32)).astype(bf16)
    projected = dot_nn(normed, w_ref[...])
    proj_ref[...] = projected
    scale = lax.rsqrt(jnp.sum(projected * projected, axis=-1, keepdims=True) + epsilon)
    emb_ref[...] = (projected * scale).astype(bf16)


def leave(mid, near, moved, gain, weight, count):
    total, depth = mid.shape
    wide = weight.shape[1]
    return pl.pallas_call(
        leave_kernel,
        grid=(total // count,),
        in_specs=[rows_of(count, depth)] * 3 + [full(1, depth), full(depth, wide)],
        out_specs=[rows_of(count, depth), rows_of(count, wide), rows_of(count, wide)],
        out_shape=(like((total, depth), bf16), like((total, wide), f32), like((total, wide), bf16)),
        compiler_params=params(10),
        cost_estimate=cost(4),
        name="leave",
    )(mid, near, moved, gain, weight)


def norm_back(values, gain, gradient):
    scale = rms(values)
    weighted = gradient * gain
    average = jnp.mean(weighted * values, axis=-1, keepdims=True)
    back = scale * weighted - values * (scale * scale * scale) * average
    return back, gradient * values * scale


def leave_back_kernel(core_ref, out_ref, proj_ref, near_ref, moved_ref, qn_ref, qm_ref, gain_ref, w_ref, grad_ref, wg_ref, gg_ref, emb_s):
    b = pl.program_id(0)

    @pl.when(b == 0)
    def _():
        wg_ref[...] = jnp.zeros(wg_ref.shape, f32)
        gg_ref[...] = jnp.zeros(gg_ref.shape, f32)
        length, half = near_ref.shape[0], qn_ref.shape[0]
        core = core_ref[0]
        emb_s[:length, :] = near_ref[...] + moved_ref[...].astype(f32)
        start = pl.multiple_of(length + core * half, half)
        emb_s[pl.ds(start, half), :] = qn_ref[...].astype(f32)
        start = pl.multiple_of(length + (1 - core) * half, half)
        emb_s[pl.ds(start, half), :] = qm_ref[...].astype(f32)

    count = out_ref.shape[0]
    projected = proj_ref[...]
    scale = lax.rsqrt(jnp.sum(projected * projected, axis=-1, keepdims=True) + epsilon)
    unit = projected * scale
    grad = emb_s[pl.ds(pl.multiple_of(b * count, count), count), :]
    grad = (scale * (grad - unit * jnp.sum(grad * unit, axis=-1, keepdims=True))).astype(bf16)
    out = out_ref[...].astype(f32)
    gain = gain_ref[...].astype(f32)
    normed = (out * rms(out) * gain).astype(bf16)
    wg_ref[...] += dot_tn(normed, grad)
    back, addends = norm_back(out, gain, dot_nt(grad, w_ref[...]))
    grad_ref[...] = back.astype(bf16)
    gg_ref[0:1, :] += jnp.sum(addends, axis=0, keepdims=True)


def leave_back(core, layer_out, projected, near, moved, query_near, query_moved, gain, weight, count):
    total, depth = layer_out.shape
    wide = weight.shape[1]
    return pl.pallas_call(
        leave_back_kernel,
        grid=(total // count,),
        in_specs=[
            SCALARS,
            rows_of(count, depth),
            rows_of(count, wide),
            full(*near.shape),
            full(*moved.shape),
            full(*query_near.shape),
            full(*query_moved.shape),
            full(1, depth),
            full(depth, wide),
        ],
        out_specs=[rows_of(count, depth), kept(depth, wide), kept(8, depth)],
        out_shape=(like((total, depth), bf16), like((depth, wide), f32), like((8, depth), f32)),
        scratch_shapes=[pltpu.VMEM((total, wide), f32)],
        compiler_params=params(14),
        cost_estimate=cost(5),
        name="leave_back",
    )(core, layer_out, projected, near, moved, query_near, query_moved, gain, weight)


def ffn_back_kernel(hidden, own, *refs):
    gate_s, up_s, down_s = refs[-3:]
    if own:
        index_ref, grad_ref, norm_ref, gu_ref, d_ref, g_ref, u_ref, part_in, down_in = refs[:9]
        nf_ref, a_ref, b_ref, *downs = refs[9:-3]
    else:
        grad_ref, norm_ref, gu_ref, d_ref, g_ref, u_ref, nf_ref, a_ref, b_ref, down_ref = refs[:-3]
    b = pl.program_id(0)

    @pl.when(b == 0)
    def _():
        gate_s[...] = jnp.zeros(gate_s.shape, f32)
        up_s[...] = jnp.zeros(up_s.shape, f32)
        down_s[...] = jnp.zeros(down_s.shape, f32)

    grad = grad_ref[...]
    gate = gu_ref[:, :hidden].astype(f32)
    up = gu_ref[:, hidden:].astype(f32)
    hidden_grad = dot_nt(grad, d_ref[...])
    half = gelu_parts(gate)
    curve = 0.7978845608028654 * (1.0 + 0.134145 * gate * gate)
    slope = half + 2.0 * gate * half * (1.0 - half) * curve
    act = gate * half
    gate_grad = (hidden_grad * up * slope).astype(bf16)
    up_grad = (hidden_grad * act).astype(bf16)
    normed = norm_ref[...]
    gate_s[...] += dot_tn(normed, gate_grad)
    up_s[...] += dot_tn(normed, up_grad)
    down_s[...] += dot_tn(grad, (act * up).astype(bf16))
    back = dot_nt(gate_grad, g_ref[...]) + dot_nt(up_grad, u_ref[...])
    nf_ref[...] = (part_in[...].astype(f32) + back if own else back).astype(bf16)

    @pl.when(b == pl.num_programs(0) - 1)
    def _():
        cut = a_ref.shape[1]
        a_ref[...] = gate_s[:, :cut].astype(bf16)
        b_ref[:, : hidden - cut] = gate_s[:, cut:].astype(bf16)
        b_ref[:, hidden - cut :] = up_s[...].astype(bf16)
        if not own:
            down_ref[...] = down_s[...].astype(bf16)
        else:
            for k, ref in enumerate(downs):
                size = ref.shape[0]
                rows = pl.ds(pl.multiple_of(jnp.bitwise_xor(index_ref[0], k) * size, size), size)
                ref[:, :hidden] = down_in[rows, :]
                ref[:, hidden:] = down_s[rows, :].astype(bf16)


def ffn_back(grad, normed, gate_up, down, gate, up, count, index=None, part_sum=None, far_down=None):
    total, depth = normed.shape
    hidden = down.shape[0]
    own = index is not None
    quarter = depth // 4
    downs = [(quarter, 2 * hidden)] * 4 if own else [(depth, hidden)]
    shapes = [(depth, hidden // 2), (depth, hidden + hidden // 2)] + downs
    return pl.pallas_call(
        partial(ffn_back_kernel, hidden, own),
        grid=(total // count,),
        in_specs=([SCALARS] if own else [])
        + [
            rows_of(count, depth),
            rows_of(count, depth),
            rows_of(count, 2 * hidden),
            full(hidden, depth),
            full(depth, hidden),
            full(depth, hidden),
        ]
        + ([rows_of(count, depth), full(depth, hidden)] if own else []),
        out_specs=[rows_of(count, depth)] + [kept(*shape) for shape in shapes],
        out_shape=(like((total, depth), bf16),) + tuple(like(shape, bf16) for shape in shapes),
        scratch_shapes=[pltpu.VMEM((depth, hidden), f32)] * 3,
        compiler_params=params(28),
        cost_estimate=cost(10),
        name="ffn_back",
    )(*([index] if own else []), grad, normed, gate_up, down, gate, up, *([part_sum, far_down] if own else []))


def mid_back_kernel(near_ref, moved_ref, mid_ref, grad_ref, gain_ref, c0_ref, c1_ref, w0_ref, w1_ref, out_ref, dc0_ref, dc1_ref, ow0_ref, ow1_ref, gg_ref, o0_s, o1_s):
    b = pl.program_id(0)

    @pl.when(b == 0)
    def _():
        o0_s[...] = jnp.zeros(o0_s.shape, f32)
        o1_s[...] = jnp.zeros(o1_s.shape, f32)
        gg_ref[...] = jnp.zeros(gg_ref.shape, f32)

    gradient = near_ref[...].astype(f32) + moved_ref[...].astype(f32)
    back, addends = norm_back(mid_ref[...].astype(f32), gain_ref[...].astype(f32), gradient)
    rounded = (grad_ref[...].astype(f32) + back).astype(bf16)
    out_ref[...] = rounded
    gg_ref[0:1, :] += jnp.sum(addends, axis=0, keepdims=True)
    dc0_ref[...] = dot_nt(rounded, w0_ref[...]).astype(bf16)
    dc1_ref[...] = dot_nt(rounded, w1_ref[...]).astype(bf16)
    o0_s[...] += dot_tn(rounded, c0_ref[...])
    o1_s[...] += dot_tn(rounded, c1_ref[...])

    @pl.when(b == pl.num_programs(0) - 1)
    def _():
        ow0_ref[...] = o0_s[...].astype(bf16)
        ow1_ref[...] = o1_s[...].astype(bf16)


def mid_back(near, moved, mid, grad, gain, contexts, weights, count):
    total, depth = mid.shape
    inner = weights[0].shape[0]
    return pl.pallas_call(
        mid_back_kernel,
        grid=(total // count,),
        in_specs=[rows_of(count, depth)] * 4
        + [full(1, depth)]
        + [rows_of(count, inner)] * 2
        + [full(inner, depth)] * 2,
        out_specs=[
            rows_of(count, depth),
            rows_of(count, inner),
            rows_of(count, inner),
            kept(depth, inner),
            kept(depth, inner),
            kept(8, depth),
        ],
        out_shape=(
            like((total, depth), bf16),
            like((total, inner), bf16),
            like((total, inner), bf16),
            like((depth, inner), bf16),
            like((depth, inner), bf16),
            like((8, depth), f32),
        ),
        scratch_shapes=[pltpu.VMEM((depth, inner), f32)] * 2,
        compiler_params=params(16),
        cost_estimate=cost(6),
        name="mid_back",
    )(near, moved, mid, grad, gain, *contexts, *weights)


EXTRA = 16


def extra_rows(ref, start, final_ref, ffn_ref, attn_ref, bias_ref):
    rows = [final_ref[0:1, :], ffn_ref[0:1, :]]
    rows.append(jnp.zeros_like(rows[0]) if attn_ref is None else attn_ref[0:1, :])
    ones = jnp.ones((8, bias_ref.shape[2]), f32)
    ref[start : start + EXTRA, :] = jnp.zeros((EXTRA, ref.shape[1]), f32).astype(ref.dtype)
    for i, row in enumerate(rows):
        ref[start + i : start + i + 1, :] = row.astype(ref.dtype)
    for h in range(bias_ref.shape[0]):
        sums = lax.dot_general(
            ones,
            bias_ref[h],
            (((1,), (1,)), ((), ())),
            precision=lax.Precision.HIGHEST,
            preferred_element_type=f32,
        )
        ref[start + 3 + h : start + 4 + h, : sums.shape[1]] = sums[0:1, :].astype(ref.dtype)


def heads_far_kernel(norm_ref, grad_ref, ow_ref, final_ref, ffn_ref, bias_ref, a_ref, b_ref, all_s):
    wide = grad_ref.shape[1]
    depth = norm_ref.shape[1]
    all_s[:depth, :wide] = dot_tn(norm_ref[...], grad_ref[...])
    all_s[:depth, wide:] = ow_ref[...].astype(f32)
    extra_rows(all_s, depth, final_ref, ffn_ref, None, bias_ref)
    cut = a_ref.shape[1]
    a_ref[...] = all_s[:, :cut].astype(bf16)
    b_ref[...] = all_s[:, cut:].astype(bf16)


def heads_far(normed, grads, output_grad, final_gain, ffn_gain, bias_grad):
    total, depth = normed.shape
    wide = grads.shape[1] + output_grad.shape[1]
    cut = wide * 2 // 3 // BLOCK * BLOCK
    return pl.pallas_call(
        heads_far_kernel,
        in_specs=[pl.BlockSpec(memory_space=pltpu.VMEM)] * 6,
        out_shape=(like((depth + EXTRA, cut), bf16), like((depth + EXTRA, wide - cut), bf16)),
        scratch_shapes=[pltpu.VMEM((depth + EXTRA, wide), f32)],
        compiler_params=params(14),
        cost_estimate=cost(3),
        name="heads_far",
    )(normed, grads, output_grad, final_gain, ffn_gain, bias_grad)


def heads_own_kernel(index_ref, norm_ref, grad_ref, ow_ref, final_ref, ffn_ref, attn_ref, bias_ref, a_ref, b_ref, *refs):
    outs, all_s = refs[:4], refs[4]
    wide = grad_ref.shape[1]
    depth = norm_ref.shape[1]
    all_s[:depth, :wide] = dot_tn(norm_ref[...], grad_ref[...])
    all_s[:depth, wide:] = ow_ref[...].astype(f32)
    extra_rows(all_s, depth, final_ref, ffn_ref, attn_ref, bias_ref)
    cut = a_ref.shape[1]
    all_s[:, :cut] += a_ref[...].astype(f32)
    all_s[:, cut:] += b_ref[...].astype(f32)
    count = depth // 4
    for k, ref in enumerate(outs):
        start = pl.multiple_of(jnp.bitwise_xor(index_ref[0], k) * count, count)
        ref[:count, :] = all_s[pl.ds(start, count), :].astype(bf16)
        ref[count:, :] = all_s[depth:, :].astype(bf16)


def heads_own(index, normed, grads, output_grad, final_gain, ffn_gain, attn_gain, bias_grad, moved, more):
    total, depth = normed.shape
    wide = moved.shape[1] + more.shape[1]
    return pl.pallas_call(
        heads_own_kernel,
        in_specs=[SCALARS] + [pl.BlockSpec(memory_space=pltpu.VMEM)] * 9,
        out_shape=(like((depth // 4 + EXTRA, wide), bf16),) * 4,
        scratch_shapes=[pltpu.VMEM((depth + EXTRA, wide), f32)],
        compiler_params=params(16),
        cost_estimate=cost(3),
        name="heads_own",
    )(index, normed, grads, output_grad, final_gain, ffn_gain, attn_gain, bias_grad, moved, more)


def quarter_kernel(index_ref, near_ref, moved_ref, *outs):
    for k, ref in enumerate(outs):
        count = ref.shape[0]
        rows = pl.ds(pl.multiple_of(jnp.bitwise_xor(index_ref[0], k) * count, count), count)
        ref[...] = (near_ref[rows, :].astype(f32) + moved_ref[rows, :].astype(f32)).astype(bf16)


def quarter_sums(index, near, moved):
    depth, wide = near.shape
    return pl.pallas_call(
        quarter_kernel,
        in_specs=[SCALARS] + [pl.BlockSpec(memory_space=pltpu.VMEM)] * 2,
        out_shape=(like((depth // 4, wide), bf16),) * 4,
        compiler_params=params(8),
        cost_estimate=cost(1),
        name="quarter_sums",
    )(index, near, moved)


def enter_back_kernel(place_ref, tok_ref, own_ref, far_ref, w0_ref, w1_ref, kept_ref, sent_ref, gg_ref, na_s):
    core = place_ref[0] % 2
    total = tok_ref.shape[0]
    own_half = kept_ref.shape[0]
    gg_ref[...] = jnp.zeros(gg_ref.shape, f32)
    count = total // 3
    for i in range(3):
        rows = slice(i * count, (i + 1) * count)
        grad = dot_nt(own_ref[rows, :], w0_ref[...]) + dot_nt(far_ref[rows, :], w1_ref[...])
        values = tok_ref[rows, :].astype(f32)
        gg_ref[0:1, :] += jnp.sum(grad * values * rms(values), axis=0, keepdims=True)
        na_s[rows, :] = grad.astype(bf16)
    shard, query = split_of(total, own_half)
    for ref, which in ((kept_ref, core), (sent_ref, 1 - core)):
        for i in range(2):
            start = pl.multiple_of((which + 2 * i) * shard, shard)
            ref[i * shard : (i + 1) * shard, :] = na_s[pl.ds(start, shard), :]
        start = pl.multiple_of(4 * shard + which * query, query)
        ref[2 * shard :, :] = na_s[pl.ds(start, query), :]


def widen_kernel(groups, cuts, index_ref, *refs):
    outs = refs[4 * groups : 4 * groups + len(cuts)]
    scratch = list(refs[4 * groups + len(cuts) :])
    for (sources, turned), out in zip(cuts, outs):
        target = scratch.pop(0) if turned else out
        at = 0
        for group, first, last in sources:
            for k, ref in enumerate(refs[4 * group : 4 * group + 4]):
                count = target.shape[0] // 4
                rows = pl.ds(pl.multiple_of(jnp.bitwise_xor(index_ref[0], k) * count, count), count)
                target[rows, at : at + last - first] = ref[:count, first:last].astype(f32)
            at += last - first
        if turned:
            out[...] = jnp.transpose(target[...])


def widened(index, depth, groups, cuts, name):
    widths = [sum(last - first for _, first, last in sources) for sources, _ in cuts]
    return pl.pallas_call(
        partial(widen_kernel, len(groups), cuts),
        in_specs=[SCALARS] + [pl.BlockSpec(memory_space=pltpu.VMEM)] * (4 * len(groups)),
        out_shape=tuple(
            like((wide, depth) if turned else (depth, wide), f32) for wide, (_, turned) in zip(widths, cuts)
        ),
        scratch_shapes=[pltpu.VMEM((depth, wide), f32) for wide, (_, turned) in zip(widths, cuts) if turned],
        compiler_params=params(20),
        cost_estimate=cost(3),
        name=name,
    )(index, *[piece for group in groups for piece in group])


def split_of(total, half):
    query = half - (half // BLOCK) * BLOCK
    return (half - query) // 2, query


def enter_back(place, tokens, own, far, weights):
    total, depth = tokens.shape
    return pl.pallas_call(
        enter_back_kernel,
        in_specs=[SCALARS] + [pl.BlockSpec(memory_space=pltpu.VMEM)] * 5,
        out_shape=(like((total // 2, depth), bf16),) * 2 + (like((8, depth), f32),),
        scratch_shapes=[pltpu.VMEM((total, depth), bf16)],
        compiler_params=params(16),
        cost_estimate=cost(4),
        name="enter_back",
    )(place, tokens, own, far, *weights)


def inputs_back_kernel(place_ref, tok_ref, mid_ref, near_ref, moved_ref, gain_ref, stay_ref, leave_ref, query_ref):
    core, x = place_ref[0] % 2, place_ref[0] // 2
    total = tok_ref.shape[0]
    shard, query = split_of(total, near_ref.shape[0])
    gain = gain_ref[...].astype(f32)

    def piece(start, at, count):
        rows = pl.ds(pl.multiple_of(start, count), count)
        at = pl.ds(pl.multiple_of(at, count), count)
        gradient = near_ref[at, :].astype(f32) + moved_ref[at, :].astype(f32)
        back, _ = norm_back(tok_ref[rows, :].astype(f32), gain, gradient)
        return mid_ref[rows, :].astype(f32) + back

    leave_ref[...] = piece((core + 2 * (1 - x)) * shard, (1 - x) * shard, shard).astype(bf16)
    stay_ref[...] = piece((core + 2 * x) * shard, x * shard, shard)
    query_ref[...] = piece(4 * shard + core * query, 2 * shard, query)


def inputs_back(place, tokens, mid_grad, near, moved, gain):
    total, depth = tokens.shape
    shard, query = split_of(total, near.shape[0])
    return pl.pallas_call(
        inputs_back_kernel,
        in_specs=[SCALARS] + [pl.BlockSpec(memory_space=pltpu.VMEM)] * 5,
        out_shape=(like((shard, depth), f32), like((shard, depth), bf16), like((query, depth), f32)),
        compiler_params=params(12),
        cost_estimate=cost(2),
        name="inputs_back",
    )(place, tokens, mid_grad, near, moved, gain)


def swapped(bit, mine, theirs, axis=0):
    first = jnp.where(bit == 0, mine, theirs)
    second = jnp.where(bit == 0, theirs, mine)
    return jnp.concatenate([first, second], axis=axis)


def after(values, *earlier):
    return lax.optimization_barrier((values,) + earlier)[0]


def part(values, index, parts, axis=0):
    size = values.shape[axis] // parts
    return lax.dynamic_slice_in_dim(values, index * size, size, axis)


def shards(
    doc_tokens,
    query_tokens,
    doc_segments,
    query_keep,
    retrieved,
    positives,
    attn_gain,
    query_weight,
    key_weight,
    value_weight,
    output_weight,
    position_bias,
    ffn_gain,
    gate_weight,
    up_weight,
    down_weight,
    final_gain,
    proj_weight,
):
    groups = lax.axis_size("dp")
    tensor_size = lax.axis_size("mp")
    bits = groups.bit_length() - 1
    dp = lax.axis_index("dp")
    mp = lax.axis_index("mp")
    x = mp // 2
    core = mp % 2
    row_count, shard_len, width = doc_tokens.shape
    length = shard_len * tensor_size
    query_local, query_len, _ = query_tokens.shape
    chip_queries = query_local * 2
    buckets = position_bias.shape[0]
    hidden_local = gate_weight.shape[1]
    doc_local = retrieved.shape[2]
    docs_row = doc_local // row_count
    query_total = query_keep.shape[0]
    vector_width = proj_weight.shape[1]
    inner = query_weight.shape[1]

    def over(axis, size, mask):
        pairs = [(i, i ^ mask) for i in range(size)]
        return lambda values: lax.ppermute(values, axis, pairs)

    to_x = over("mp", tensor_size, 2)
    to_core = over("mp", tensor_size, 1)
    to_dp = [over("dp", groups, 1 << b) for b in range(bits)]
    dp_bit = [(dp >> b) & 1 for b in range(bits)]

    def exchange(steps):
        dp_mask = sum(1 << b for axis, b in steps if axis == "dp")
        mp_mask = 2 if any(axis == "x" for axis, b in steps) else 0
        pairs = [
            (i, ((i // tensor_size) ^ dp_mask) * tensor_size + ((i % tensor_size) ^ mp_mask))
            for i in range(groups * tensor_size)
        ]
        return lambda values: lax.ppermute(values, ("dp", "mp"), pairs)

    def rounds(order):
        out = []
        for i in range(0, len(order), 2):
            steps = order[i : i + 2]
            if len(steps) == 1:
                out.append([exchange(steps)])
            else:
                out.append([exchange(steps[:1]), exchange(steps[1:]), exchange(steps)])
        return out

    kept_rows = lax.dynamic_index_in_dim(doc_tokens, x, 0, keepdims=False)
    sent_rows = lax.dynamic_index_in_dim(doc_tokens, 1 - x, 0, keepdims=False)
    far_rows = to_x(sent_rows)
    kept_tokens = jnp.concatenate(
        [kept_rows, query_tokens.reshape(query_local * query_len, width)], axis=0
    )
    near_tokens = to_core(kept_tokens)
    cross_rows = to_core(far_rows)

    own_qkv, qkv_half, output_half, gate_half, up_half, *down_halves = pack(
        jnp.stack(dp_bit[:2]),
        jnp.transpose(after(query_weight, sent_rows)),
        jnp.transpose(key_weight),
        jnp.transpose(value_weight),
        output_weight,
        gate_weight,
        up_weight,
        down_weight,
        position_bias,
    )
    near_tiles = bias_tiles(after(position_bias.astype(f32), qkv_half))
    qkv_half = to_x(qkv_half)
    output_half = to_x(output_half)
    far_bias = output_half[inner // 2 :, : position_bias.shape[1]]
    output_half = output_half[: inner // 2]

    def other_half(got, b=0, earlier=()):
        return swapped(dp_bit[b], got, after(to_dp[b](got), earlier))


    row_segments = lax.dynamic_index_in_dim(doc_segments, x, 0, keepdims=False)
    chip_keep = lax.dynamic_slice_in_dim(
        query_keep, (dp * tensor_size + x * 2) * query_local, chip_queries, 0
    ).reshape(-1)
    query_ids = jnp.arange(chip_queries * query_len, dtype=jnp.int32) // query_len + docs_row
    seg_q = jnp.concatenate([row_segments, query_ids])
    seg_k = jnp.concatenate([row_segments, jnp.where(chip_keep > 0, query_ids, -1)])
    blocked = row_segments.reshape(-1, PAIR)
    low = jnp.sum((row_segments[None, :] < blocked[:, :1]).astype(jnp.int32), axis=1)
    high = jnp.sum((row_segments[None, :] <= blocked[:, -1:]).astype(jnp.int32), axis=1)
    low_block = low // BLOCK
    high_block = (high + BLOCK - 1) // BLOCK
    lo = jnp.concatenate([low_block, jnp.full((1,), length // BLOCK - 1, jnp.int32)])
    cnt = jnp.concatenate([(high_block - low_block + 1) // 2, jnp.ones((1,), jnp.int32)])
    ranges = (lo, cnt)

    order = [("dp", b) for b in reversed(range(bits))] + [("x", 0)]
    place = sum((x if axis == "x" else dp_bit[b]) << s for s, (axis, b) in enumerate(order))
    kept_retrieved = (query_keep[:, :, None] * retrieved).reshape(query_total * query_len, doc_local)
    seg_q, seg_k = seg_q[None, :], seg_k[None, :]
    segs = (seg_q, seg_k)
    half_queries = query_total // 2
    query_lanes = -(-half_queries // BLOCK) * BLOCK

    place_mp = mp.reshape(1)
    gain_attn, gain_ffn, gain_final = [g.reshape(1, width) for g in (attn_gain, ffn_gain, final_gain)]
    pieces = (kept_tokens, near_tokens, far_rows, cross_rows)
    tokens, normed_attn, own_heads = enter(place_mp, pieces, gain_attn, own_qkv)
    far_tiles = bias_tiles(after(far_bias.astype(f32), own_heads))
    qkv_half = after(qkv_half, far_tiles)
    gate_half = to_x(after(gate_half, own_heads))
    own_context, own_log = attend(own_heads, ranges, segs, near_tiles[0])
    far_qkv = other_half(qkv_half, 0, own_context)
    gate_half = after(gate_half, own_context)
    up_half = to_x(after(up_half, own_context))
    far_heads = dot_nn(normed_attn, after(far_qkv, gate_half)).astype(bf16)
    far_context, far_log = attend(far_heads, ranges, segs, far_tiles[0])
    far_output = other_half(after(output_half, far_qkv), 0, far_context)
    far_gate = other_half(after(gate_half, far_qkv), 0, far_context)
    up_half = after(up_half, far_context)
    down_halves = [to_x(after(half, far_context)) for half in down_halves]
    tiles = (near_tiles, far_tiles)
    heads = (own_heads, far_heads)
    contexts = (own_context, far_context)
    logs = (own_log, far_log)
    qkv_weights = (own_qkv, far_qkv)
    output_weights = (output_weight, far_output)
    attn_part = sum(
        dot_nn(c, w) for c, w in zip(after(contexts, far_gate, up_half), output_weights)
    ).astype(bf16)
    chosen, pos_rows = choose(
        jnp.stack([core, place, x * docs_row]),
        positives,
        after(kept_retrieved, attn_part),
        query_local,
        query_len,
        bits + 1,
    )
    count = tokens.shape[0] // 3
    mid, normed_ffn, own_gate_up, ffn_sum = ffn_own(
        tokens, attn_part, to_core(attn_part), gain_ffn, gate_weight, up_weight, down_weight, count
    )
    far_up = other_half(after(up_half, attn_part), 1, ffn_sum)
    down_halves = after(down_halves, ffn_sum)
    far_down = jnp.concatenate([other_half(half, b) for b, half in enumerate(down_halves)], axis=1)
    far_gate_up_out, ffn_part = ffn_far(normed_ffn, far_gate, far_up, far_down, ffn_sum, count)
    layer_out, projected, embedded = leave(
        mid, ffn_part, to_core(ffn_part), gain_final, proj_weight, count
    )

    doc_embedded = embedded[:length]
    query_emb = part(embedded[length:], core, 2)
    for moves in rounds(order):
        query_emb = jnp.concatenate([query_emb] + [move(query_emb) for move in moves], axis=0)
    first_doc = jnp.stack([dp * doc_local + x * docs_row, place])
    seg_col = seg_q[:, :length]
    sums, logits, stats = score(
        first_doc, doc_embedded, query_emb, seg_col, chosen, pos_rows, query_len, query_local, docs_row
    )
    for moves in rounds(order[::-1]):
        every = [stats] + [move(stats) for move in moves]
        top = every[0][0:1]
        for moved in every[1:]:
            top = jnp.maximum(top, moved[0:1])
        total = sum(moved[1:2] * jnp.exp(moved[0:1] - top) for moved in every)
        stats = jnp.concatenate([top, total, sum(moved[2:] for moved in every)], axis=0)
    valid = jnp.arange(query_lanes) < half_queries
    loss_sum = jnp.sum(jnp.where(valid, stats[0] + jnp.log(stats[1]) - stats[2], 0.0))
    found_sum = jnp.sum(jnp.where(valid & (stats[3] > 0.5), 1.0, 0.0))
    ends = jnp.broadcast_to(jnp.stack([loss_sum, found_sum])[:, None], (2, BLOCK))
    ends = (ends + to_core(ends)) / query_total
    loss_value = ends[0, 0]
    found_share = ends[1, 0]

    demb, dqe = score_back(
        first_doc,
        doc_embedded,
        query_emb,
        seg_col,
        chosen,
        pos_rows,
        sums,
        logits,
        stats,
        query_len,
        query_local,
        docs_row,
    )
    demb_moved = to_core(demb.astype(bf16))
    for moves in reversed(rounds(order)):
        pieces = jnp.split(dqe, len(moves) + 1, axis=0)
        moved = [move(piece).astype(f32) for move, piece in zip(moves, pieces[1:])]
        dqe = sum(moved, pieces[0].astype(f32)).astype(bf16)
    dqe_moved = to_core(dqe)

    def widen(values):
        return values.astype(f32)

    def narrow(values):
        return values.astype(bf16)

    def added(*values):
        return narrow(sum(widen(v) for v in values[1:]) + widen(values[0]))

    four = [exchange([("dp", 0)]), exchange([("dp", 1)]), exchange([("dp", 0), ("dp", 1)])]
    four_index = (dp % 4).reshape(1)
    rest = range(2, bits)

    def scattered(pieces):
        return (pieces[0],) + tuple(move(piece) for move, piece in zip(four, pieces[1:]))

    def rest_of(values, moved):
        values = added(values, moved)
        for b in rest[1:]:
            values = added(values, to_dp[b](values))
        return values

    def gathered(values):
        return (values,) + tuple(move(values) for move in four)

    def assembled(pieces):
        low = [jnp.where(dp_bit[0] == 0, pieces[0], pieces[1]), jnp.where(dp_bit[0] == 0, pieces[1], pieces[0])]
        high = [jnp.where(dp_bit[0] == 0, pieces[2], pieces[3]), jnp.where(dp_bit[0] == 0, pieces[3], pieces[2])]
        return jnp.concatenate(
            [jnp.where(dp_bit[1] == 0, u, v) for u, v in zip(low + high, high + low)], axis=0
        )

    layer_out_grad, proj_grad, final_gain_part = leave_back(
        core.reshape(1), layer_out, projected, demb, demb_moved, dqe, dqe_moved, gain_final, proj_weight, count
    )
    proj_part = narrow(part(proj_grad, core, 2))
    proj_moved = to_x(proj_part)
    nf_sum, far_first, far_rest, far_down_grad = ffn_back(
        after(layer_out_grad, proj_part), normed_ffn, far_gate_up_out, far_down, far_gate, far_up, count
    )
    first_moved = to_x(far_first)
    proj_part = added(proj_part, after(proj_moved, far_first))
    proj_moves = [move(proj_part) for move in four]
    nf_part, own_first, own_rest, *down_pieces = ffn_back(
        after(layer_out_grad, proj_part),
        normed_ffn,
        own_gate_up,
        down_weight,
        gate_weight,
        up_weight,
        count,
        four_index,
        nf_sum,
        far_down_grad,
    )
    first_pieces = quarter_sums(four_index, own_first, after(first_moved, nf_part))
    first_moves = scattered(first_pieces)
    rest_moved = to_x(after(far_rest, first_pieces))
    down_moves = scattered(tuple(down_pieces))
    proj_part = added(*after((proj_part, *proj_moves), first_pieces))
    proj_moved = to_dp[rest[0]](proj_part)
    nf_part = after(nf_part, proj_part)
    mid_grad, own_context_grad, far_context_grad, own_out, far_out, ffn_gain_part = mid_back(
        nf_part, to_core(nf_part), mid, layer_out_grad, gain_ffn, contexts, output_weights, count
    )

    far_grads, far_bias_grad = attend_back(
        far_heads,
        far_context_grad,
        far_context,
        far_log,
        ranges,
        segs,
        far_tiles[1],
        buckets,
    )
    down = added(*after(down_moves, far_grads))
    down_kept, down_moved = down[:, hidden_local:], to_x(down[:, :hidden_local])
    far_all, far_more = heads_far(normed_attn, after(far_grads, down), far_out, final_gain_part, ffn_gain_part, far_bias_grad)

    down = added(after(down_moved, far_all), down_kept)
    all_moved = to_x(after(far_all, down))
    first = added(*after(first_moves, far_all))
    rest_pieces = quarter_sums(four_index, own_rest, after(rest_moved, far_all))
    rest_moves = scattered(rest_pieces)
    early = jnp.concatenate([first, down], axis=1)
    early_moved = to_dp[rest[0]](early)
    proj_part = rest_of(proj_part, after(proj_moved, far_all))
    own_grads, own_bias_grad = attend_back(
        own_heads,
        after(own_context_grad, rest_pieces, early, proj_part),
        own_context,
        own_log,
        ranges,
        segs,
        near_tiles[1],
        buckets,
    )

    early = rest_of(early, after(early_moved, own_grads))
    early_all = gathered(early)
    others = added(*after(rest_moves, own_grads))
    others_moved = to_dp[rest[0]](others)
    all_moved = after(all_moved, own_grads)
    more_moved = to_x(after(far_more, all_moved))
    na_kept, na_sent, attn_gain_part = enter_back(
        place_mp, tokens, after(own_grads, others, early, all_moved), far_grads, qkv_weights
    )
    early_all = after(early_all, na_sent)
    proj_moved = to_core(after(proj_part, na_sent))
    all_pieces = heads_own(
        four_index,
        normed_attn,
        own_grads,
        own_out,
        final_gain_part,
        ffn_gain_part,
        attn_gain_part,
        own_bias_grad,
        all_moved,
        after(more_moved, na_sent, early_all, proj_moved),
    )
    all_moves = scattered(all_pieces)
    others = rest_of(others, after(others_moved, all_pieces))

    both = added(*after(all_moves, others))
    both_moved = to_dp[rest[0]](both)
    others_all = gathered(after(others, both))
    na_moved = to_core(after(na_sent, both))

    stay, leaving, query_grad = inputs_back(place_mp, tokens, mid_grad, na_kept, na_moved, gain_attn)
    both = rest_of(both, after(both_moved, others_all, leaving))
    both_all = gathered(both)
    back = to_x(after(leaving, both))
    extra = both[width // 4 :]
    crossing = [(i, i ^ 3) for i in range(tensor_size)]
    extra_moves = (to_x(extra), to_core(extra), lax.ppermute(extra, "mp", crossing))
    cut = hidden_local // 2
    gate_weight_grad, up_weight_grad, down_weight_grad = widened(
        four_index,
        width,
        after((early_all, others_all), extra_moves),
        (
            (((0, 0, cut), (1, 0, cut)), False),
            (((1, cut, cut + hidden_local),), False),
            (((0, cut, cut + hidden_local),), True),
        ),
        "widen_ffn",
    )
    extra_moves, back = after((extra_moves, back), up_weight_grad)
    extra = widen(extra)
    attn_gain_grad = extra[2] + sum(widen(moved[2]) for moved in extra_moves)
    proj_weight_grad = widen(swapped(core, proj_part, proj_moved))
    position_bias_grad = jnp.transpose(extra[3 : 3 + position_bias.shape[1], :buckets])
    back = widen(back)
    doc_grad = jnp.stack([jnp.where(x == 0, stay, back), jnp.where(x == 0, back, stay)], axis=0)

    query_weight_grad, key_weight_grad, value_weight_grad, output_weight_grad = widened(
        four_index,
        width,
        (after(both_all, doc_grad, attn_gain_grad, proj_weight_grad),),
        tuple((((0, i * inner, (i + 1) * inner),), True) for i in range(4)),
        "widen_heads",
    )

    return (
        loss_value,
        found_share,
        doc_grad,
        query_grad.reshape(query_local, query_len, width),
        attn_gain_grad,
        jnp.transpose(query_weight_grad),
        jnp.transpose(key_weight_grad),
        jnp.transpose(value_weight_grad),
        output_weight_grad,
        position_bias_grad,
        extra[1],
        gate_weight_grad,
        up_weight_grad,
        down_weight_grad,
        extra[0],
        proj_weight_grad,
    )


def solution(mesh):
    placed = (
        P("dp", "mp", None),
        P(("dp", "mp"), None, None),
        P("dp", None),
        P(),
        P(None, None, "dp"),
        P(),
        P(),
        P(None, "mp"),
        P(None, "mp"),
        P(None, "mp"),
        P("mp", None),
        P(None, "mp"),
        P(),
        P(None, "mp"),
        P(None, "mp"),
        P("mp", None),
        P(),
        P(),
    )
    return jax.shard_map(
        shards,
        mesh=mesh,
        in_specs=placed,
        out_specs=(
            P(),
            P(),
            P("dp", "mp", None),
            P(("dp", "mp"), None, None),
            P(),
            P(None, "mp"),
            P(None, "mp"),
            P(None, "mp"),
            P("mp", None),
            P(None, "mp"),
            P(),
            P(None, "mp"),
            P(None, "mp"),
            P("mp", None),
            P(),
            P(),
        ),
        check_vma=False,
    )
```

```python
from functools import partial

import jax
import jax.numpy as jnp
import numpy as np
from jax import lax
from jax.experimental import pallas as pl
from jax.experimental.pallas import tpu as pltpu
from jax.sharding import PartitionSpec as P

epsilon = 1e-06
sharpness = 16.0
smoothing_divisor = 0.05
masked_score = -1e30
BLOCK = 128
PAIR = 2 * BLOCK
bf16 = jnp.bfloat16
f32 = jnp.float32


def bucket_starts(buckets):
    half = buckets // 2
    exact = half // 2
    distance = np.arange(0, 2048)
    scaled = (
        np.log(np.maximum(distance, 1) / exact) / np.log(128.0 / exact) * (half - exact)
    )
    far = np.minimum(exact + np.floor(np.maximum(scaled, 0.0)), half - 1)
    bucket = np.where(distance < exact, distance, far)
    return [int(np.argmax(bucket >= b)) for b in range(half)]


def dot_nn(a, b):
    return lax.dot_general(a, b, (((1,), (0,)), ((), ())), preferred_element_type=f32)


def dot_nt(a, b):
    return lax.dot_general(a, b, (((1,), (1,)), ((), ())), preferred_element_type=f32)


def dot_tn(a, b):
    return lax.dot_general(a, b, (((0,), (0,)), ((), ())), preferred_element_type=f32)


def dot_exact(a, b):
    return lax.dot_general(
        a, b, (((1,), (0,)), ((), ())), precision=lax.Precision.HIGHEST, preferred_element_type=f32
    )


def params(limit_mib=40):
    return pltpu.CompilerParams(vmem_limit_bytes=limit_mib << 20)


def cost(micros):
    return pl.CostEstimate(flops=int(micros * 3e9), transcendentals=0, bytes_accessed=1 << 10)


def bias_kernel(starts, heads, tab_ref, t_ref, tt_ref):
    half = len(starts)
    sub = lax.broadcasted_iota(jnp.int32, (BLOCK, BLOCK), 0)
    lane = lax.broadcasted_iota(jnp.int32, (BLOCK, BLOCK), 1)
    for ref, base in ((t_ref, lane - sub), (tt_ref, sub - lane)):
        for d in (-1, 0, 1):
            offset = base + BLOCK * d
            n = jnp.abs(offset)
            for h in range(heads):
                low = high = None
                if d <= 0:
                    low = jnp.full((BLOCK, BLOCK), tab_ref[0, h], f32)
                    for b in range(1, half):
                        low = jnp.where(n >= starts[b], tab_ref[b, h], low)
                if d >= 0:
                    high = jnp.full((BLOCK, BLOCK), tab_ref[half, h], f32)
                    for b in range(1, half):
                        high = jnp.where(n >= starts[b], tab_ref[half + b, h], high)
                if d < 0:
                    tile = low
                elif d > 0:
                    tile = high
                else:
                    tile = jnp.where(offset > 0, high, low)
                ref[h, d + 2] = tile
        for h in range(heads):
            ref[h, 0] = jnp.full((BLOCK, BLOCK), tab_ref[half - 1, h], f32)
            ref[h, 4] = jnp.full((BLOCK, BLOCK), tab_ref[2 * half - 1, h], f32)


def bias_tiles(table):
    buckets, heads = table.shape
    starts = bucket_starts(buckets)
    shape = jax.ShapeDtypeStruct((heads, 5, BLOCK, BLOCK), f32)
    return pl.pallas_call(
        partial(bias_kernel, starts, heads),
        in_specs=[pl.BlockSpec(memory_space=pltpu.SMEM)],
        out_shape=(shape, shape),
        compiler_params=params(6),
        cost_estimate=cost(2),
        name="bias_tiles",
    )(table)


def clipped(d):
    return jnp.minimum(jnp.maximum(d, -2), 2) + 2


def column(row):
    return jnp.transpose(jnp.broadcast_to(row, (8, row.shape[1])))[:, 0:1]


def attend_kernel(heads, size, most, lo_ref, cnt_ref, qkv_ref, segq_ref, segk_ref, t_ref, ctx_ref, lse_ref, k_s, v_s):
    b = pl.program_id(0)
    inner = heads * size
    last = pl.num_programs(0) - 1

    @pl.when(b == 0)
    def _():
        for h in range(heads):
            k_s[h] = qkv_ref[:, inner + h * size : inner + (h + 1) * size]
            v_s[h] = qkv_ref[:, 2 * inner + h * size : 2 * inner + (h + 1) * size]

    def window(first, count, lo, pairs):
        rows = pl.ds(pl.multiple_of(first * BLOCK, BLOCK), count * BLOCK)
        block = qkv_ref[rows, :inner]
        seg_col = column(segq_ref[:, rows])
        spans = [pl.ds(pl.multiple_of((lo + 2 * i) * BLOCK, BLOCK), PAIR) for i in range(pairs)]
        allowed = [seg_col == segk_ref[:, span] for span in spans]
        outs, logs = [], []
        for h in range(heads):
            query = block[:, h * size : (h + 1) * size]
            scores = []
            for i, span in enumerate(spans):
                s = dot_nt(query, k_s[h, span, :])
                bias = jnp.concatenate(
                    [
                        jnp.concatenate(
                            [t_ref[h, clipped(lo + 2 * i + c - first - r)] for c in range(2)], axis=1
                        )
                        for r in range(count)
                    ],
                    axis=0,
                )
                scores.append(jnp.where(allowed[i], s + bias, masked_score))
            top = scores[0]
            for s in scores[1:]:
                top = jnp.maximum(top, s)
            largest = jnp.max(top, axis=1, keepdims=True)
            total = acc = None
            for i, span in enumerate(spans):
                p = jnp.exp(scores[i] - largest)
                total = p if total is None else total + p
                more = dot_nn(p.astype(bf16), v_s[h, span, :])
                acc = more if acc is None else acc + more
            total = jnp.sum(total, axis=1, keepdims=True)
            outs.append((acc / total).astype(bf16))
            lse = jnp.broadcast_to(largest + jnp.log(total), (count * BLOCK, BLOCK))
            lse_ref[h : h + 1, rows] = jnp.transpose(lse)[0:1, :]
        ctx_ref[rows, :] = jnp.concatenate(outs, axis=1)

    for pairs in range(1, most + 1):
        pl.when((b < last) & (cnt_ref[b] == pairs))(partial(window, 2 * b, 2, lo_ref[b], pairs))
    pl.when(b == last)(partial(window, 2 * b, 1, lo_ref[b], 1))


def attend(qkv, ranges, segs, tiles):
    lo, cnt = ranges
    seg_q, seg_k = segs
    total, wide = qkv.shape
    heads = tiles.shape[0]
    inner = wide // 3
    size = inner // heads
    steps = lo.shape[0]
    whole = lambda b, *_: (0, 0)
    return pl.pallas_call(
        partial(attend_kernel, heads, size, steps - 1),
        grid_spec=pltpu.PrefetchScalarGridSpec(
            num_scalar_prefetch=2,
            grid=(steps,),
            in_specs=[
                pl.BlockSpec((total, wide), whole, pipeline_mode=pl.Buffered(1)),
                pl.BlockSpec((1, total), whole, pipeline_mode=pl.Buffered(1)),
                pl.BlockSpec((1, total), whole, pipeline_mode=pl.Buffered(1)),
                pl.BlockSpec((heads, 5, BLOCK, BLOCK), lambda b, *_: (0, 0, 0, 0), pipeline_mode=pl.Buffered(1)),
            ],
            out_specs=[
                pl.BlockSpec((total, inner), whole),
                pl.BlockSpec((8, total), whole),
            ],
            scratch_shapes=[
                pltpu.VMEM((heads, total, size), bf16),
                pltpu.VMEM((heads, total, size), bf16),
            ],
        ),
        out_shape=(
            jax.ShapeDtypeStruct((total, inner), bf16),
            jax.ShapeDtypeStruct((8, total), f32),
        ),
        compiler_params=params(12),
        cost_estimate=cost(9),
        name="attend",
    )(lo, cnt, qkv, seg_q, seg_k, tiles)


def attend_back_kernel(
    starts,
    heads,
    size,
    most,
    lo_ref,
    cnt_ref,
    qkv_ref,
    do_ref,
    ctx_ref,
    lse_ref,
    segk_ref,
    segq_ref,
    tt_ref,
    grad_ref,
    bias_ref,
    q_s,
    do_s,
    dq_s,
    delta_s,
    d_s,
):
    b = pl.program_id(0)
    last = pl.num_programs(0) - 1
    inner = heads * size
    half = len(starts)

    @pl.when(b == 0)
    def _():
        prod = do_ref[...].astype(f32) * ctx_ref[...].astype(f32)
        high = prod.astype(bf16)
        low = (prod - high.astype(f32)).astype(bf16)
        row = lax.broadcasted_iota(jnp.int32, (8, inner), 0)
        col = lax.broadcasted_iota(jnp.int32, (8, inner), 1)
        pick = ((col >= row * size) & (col < (row + 1) * size)).astype(f32).astype(bf16)
        delta_s[...] = dot_nt(pick, high) + dot_nt(pick, low)
        for h in range(heads):
            q_s[h] = qkv_ref[:, h * size : (h + 1) * size]
            do_s[h] = do_ref[:, h * size : (h + 1) * size]
        dq_s[...] = jnp.zeros(dq_s.shape, f32)
        d_s[...] = jnp.zeros(d_s.shape, f32)

    def window(first, count, lo, pairs):
        rows = pl.ds(pl.multiple_of(first * BLOCK, BLOCK), count * BLOCK)
        block = qkv_ref[rows, inner:]
        seg_col = column(segk_ref[:, rows])
        spans = [pl.ds(pl.multiple_of((lo + 2 * i) * BLOCK, BLOCK), PAIR) for i in range(pairs)]
        allowed = [seg_col == segq_ref[:, span] for span in spans]
        dks, dvs = [], []
        for h in range(heads):
            key = block[:, h * size : (h + 1) * size]
            value = block[:, inner + h * size : inner + (h + 1) * size]
            dk = dv = None
            for i, span in enumerate(spans):
                q = q_s[h, span, :]
                do = do_s[h, span, :]
                s = dot_nt(key, q)
                dp = dot_nt(value, do)
                at = [[clipped(first + r - lo - 2 * i - c) for c in range(2)] for r in range(count)]
                bias = jnp.concatenate(
                    [
                        jnp.concatenate([tt_ref[h, at[r][c]] for c in range(2)], axis=1)
                        for r in range(count)
                    ],
                    axis=0,
                )
                p = jnp.where(allowed[i], jnp.exp(s + bias - lse_ref[h : h + 1, span]), 0.0)
                ds = p * (dp - delta_s[h : h + 1, span])
                for r in range(count):
                    for c in range(2):
                        d_s[h, at[r][c]] += ds[
                            r * BLOCK : (r + 1) * BLOCK, c * BLOCK : (c + 1) * BLOCK
                        ]
                ds16 = ds.astype(bf16)
                dv_more = dot_nn(p.astype(bf16), do)
                dk_more = dot_nn(ds16, q)
                dv = dv_more if dv is None else dv + dv_more
                dk = dk_more if dk is None else dk + dk_more
                dq_s[h, :, span] += dot_tn(key, ds16)
            dks.append(dk)
            dvs.append(dv)
        grad_ref[rows, inner:] = jnp.concatenate(dks + dvs, axis=1).astype(bf16)

    for pairs in range(1, most + 1):
        pl.when((b < last) & (cnt_ref[b] == pairs))(partial(window, 2 * b, 2, lo_ref[b], pairs))
    pl.when(b == last)(partial(window, 2 * b, 1, lo_ref[b], 1))

    @pl.when(b == last)
    def _():
        grad_ref[:, :inner] = jnp.concatenate([jnp.transpose(dq_s[h]) for h in range(heads)], axis=1).astype(bf16)
        sub = lax.broadcasted_iota(jnp.int32, (BLOCK, BLOCK), 0)
        lane = lax.broadcasted_iota(jnp.int32, (BLOCK, BLOCK), 1)
        below = lane + sub > BLOCK - 1
        reverse = (lane + sub == BLOCK - 1).astype(f32)
        bucket_row = lax.broadcasted_iota(jnp.int32, (2 * half, BLOCK), 0)
        line_lane = lax.broadcasted_iota(jnp.int32, (2 * half, BLOCK), 1)
        picks = {}
        for d in (-1, 0, 1):
            for low in (False, True):
                offset = line_lane + (1 if low else 1 - BLOCK) + BLOCK * d
                n = jnp.abs(offset)
                bucket = jnp.where(offset > 0, half, 0)
                for e in range(1, half):
                    bucket = bucket + (n >= starts[e]).astype(jnp.int32)
                picks[d, low] = bucket == bucket_row
        for h in range(heads):
            whole = jnp.zeros((2 * half, BLOCK), f32)
            for d in (-1, 0, 1):
                tile = dot_exact(d_s[h, d + 2], reverse)
                for low in (False, True):
                    kept = jnp.where(below == low, tile, 0.0)
                    line = jnp.sum(
                        pltpu.roll(kept, 0, 1, stride=1, stride_axis=0), axis=0, keepdims=True
                    )
                    whole = whole + jnp.where(picks[d, low], line, 0.0)
            for e, d in ((half - 1, 0), (2 * half - 1, 4)):
                far = jnp.sum(d_s[h, d], axis=0, keepdims=True)
                whole = whole + jnp.where(bucket_row == e, far, 0.0)
            bias_ref[h] = whole


def attend_back(qkv, context_grad, context, lse, ranges, segs, tiles, buckets):
    lo, cnt = ranges
    seg_q, seg_k = segs
    total, wide = qkv.shape
    heads = tiles.shape[0]
    inner = wide // 3
    size = inner // heads
    steps = lo.shape[0]
    starts = bucket_starts(buckets)
    whole = lambda b, *_: (0, 0)
    return pl.pallas_call(
        partial(attend_back_kernel, starts, heads, size, steps - 1),
        grid_spec=pltpu.PrefetchScalarGridSpec(
            num_scalar_prefetch=2,
            grid=(steps,),
            in_specs=[
                pl.BlockSpec((total, wide), whole, pipeline_mode=pl.Buffered(1)),
                pl.BlockSpec((total, inner), whole, pipeline_mode=pl.Buffered(1)),
                pl.BlockSpec((total, inner), whole, pipeline_mode=pl.Buffered(1)),
                pl.BlockSpec((8, total), whole, pipeline_mode=pl.Buffered(1)),
                pl.BlockSpec((1, total), whole, pipeline_mode=pl.Buffered(1)),
                pl.BlockSpec((1, total), whole, pipeline_mode=pl.Buffered(1)),
                pl.BlockSpec((heads, 5, BLOCK, BLOCK), lambda b, *_: (0, 0, 0, 0), pipeline_mode=pl.Buffered(1)),
            ],
            out_specs=[
                pl.BlockSpec((total, wide), whole),
                pl.BlockSpec((heads, buckets, BLOCK), lambda b, *_: (0, 0, 0)),
            ],
            scratch_shapes=[
                pltpu.VMEM((heads, total, size), bf16),
                pltpu.VMEM((heads, total, size), bf16),
                pltpu.VMEM((heads, size, total), f32),
                pltpu.VMEM((8, total), f32),
                pltpu.VMEM((heads, 5, BLOCK, BLOCK), f32),
            ],
        ),
        out_shape=(
            jax.ShapeDtypeStruct((total, wide), bf16),
            jax.ShapeDtypeStruct((heads, buckets, BLOCK), f32),
        ),
        compiler_params=params(16),
        cost_estimate=cost(15),
        name="attend_back",
    )(lo, cnt, qkv, context_grad, context, lse, seg_k, seg_q, tiles)


def pool_matrix(shape, axis, me, query_len, query_local):
    token = lax.broadcasted_iota(jnp.int32, shape, axis)
    query = lax.broadcasted_iota(jnp.int32, shape, 1 - axis)
    span = query_len * query_local
    holder = jnp.bitwise_xor(token // span, me)
    return (holder * query_local + token % span // query_len == query).astype(f32)


def score_kernel(query_len, query_local, docs, first_ref, emb_ref, qe_ref, seg_ref, chosen_ref, pos_ref, sums_ref, logit_ref, stat_ref, acc_s):
    b = pl.program_id(0)
    count = qe_ref.shape[0]

    @pl.when(b == 0)
    def _():
        acc_s[...] = jnp.zeros(acc_s.shape, f32)

    near = jnp.exp(sharpness * (dot_nt(emb_ref[...], qe_ref[...]) - 1.0))
    seg = column(seg_ref[...])
    for d in range(docs):
        acc_s[d : d + 1, :] += jnp.sum(jnp.where(seg == d, near, 0.0), axis=0, keepdims=True)

    @pl.when(b == pl.num_programs(0) - 1)
    def _():
        sums = acc_s[:docs, :]
        sums_ref[...] = acc_s[...]
        chosen = chosen_ref[:docs, :]
        smooth = 1.0 + jnp.log(sums) / sharpness
        pool = pool_matrix((count, pos_ref.shape[1]), 0, first_ref[1], query_len, query_local)
        picked = dot_exact(chosen * smooth, pool)
        counts = dot_exact(chosen, pool)
        logits = picked / jnp.maximum(counts, 1.0) / smoothing_divisor
        top = jnp.max(logits, axis=0, keepdims=True)
        spread = jnp.sum(jnp.exp(logits - top), axis=0, keepdims=True)
        doc = lax.broadcasted_iota(jnp.int32, logits.shape, 0) + first_ref[0]
        mine = doc == pos_ref[0:1, :]
        stat_ref[0:1, :] = top
        stat_ref[1:2, :] = spread
        stat_ref[2:3, :] = jnp.sum(jnp.where(mine, logits, 0.0), axis=0, keepdims=True)
        stat_ref[3:4, :] = jnp.sum(jnp.where(mine, counts, 0.0), axis=0, keepdims=True)
        stat_ref[4:8, :] = jnp.zeros((4, pos_ref.shape[1]), f32)
        logit_ref[0:docs, :] = logits
        logit_ref[docs : 2 * docs, :] = counts


def score(first, emb, query_emb, seg_col, chosen, positives, query_len, query_local, docs):
    count, width = query_emb.shape
    lanes = positives.shape[1]
    length = emb.shape[0]
    blocks = length // PAIR
    whole = lambda b, *_: (0, 0)
    return pl.pallas_call(
        partial(score_kernel, query_len, query_local, docs),
        grid_spec=pltpu.PrefetchScalarGridSpec(
            num_scalar_prefetch=1,
            grid=(blocks,),
            in_specs=[
                pl.BlockSpec((PAIR, width), lambda b, *_: (b, 0)),
                pl.BlockSpec((count, width), whole, pipeline_mode=pl.Buffered(1)),
                pl.BlockSpec((1, PAIR), lambda b, *_: (0, b)),
                pl.BlockSpec((8, count), whole, pipeline_mode=pl.Buffered(1)),
                pl.BlockSpec((8, lanes), whole, pipeline_mode=pl.Buffered(1)),
            ],
            out_specs=[
                pl.BlockSpec((8, count), whole),
                pl.BlockSpec((8, lanes), whole),
                pl.BlockSpec((8, lanes), whole),
            ],
            scratch_shapes=[pltpu.VMEM((8, count), f32)],
        ),
        out_shape=(
            jax.ShapeDtypeStruct((8, count), f32),
            jax.ShapeDtypeStruct((8, lanes), f32),
            jax.ShapeDtypeStruct((8, lanes), f32),
        ),
        compiler_params=params(14),
        cost_estimate=cost(5),
        name="score",
    )(first, emb, query_emb, seg_col, chosen, positives)


def score_back_kernel(query_len, query_local, docs, first_ref, emb_ref, qe_ref, seg_ref, chosen_ref, pos_ref, sums_ref, logit_ref, stat_ref, demb_ref, dqe_ref, grad_s, dq_s):
    b = pl.program_id(0)
    count = qe_ref.shape[0]

    @pl.when(b == 0)
    def _():
        logits = logit_ref[0:docs, :]
        counts = logit_ref[docs : 2 * docs, :]
        doc = lax.broadcasted_iota(jnp.int32, logits.shape, 0) + first_ref[0]
        mine = (doc == pos_ref[0:1, :]).astype(f32)
        share = jnp.exp(logits - stat_ref[0:1, :]) / stat_ref[1:2, :]
        grad = (share - mine) / smoothing_divisor / jnp.maximum(counts, 1.0)
        spread = pool_matrix((logits.shape[1], count), 1, first_ref[1], query_len, query_local)
        grad_s[0:docs, :] = dot_exact(grad, spread) * chosen_ref[:docs, :] / sums_ref[:docs, :]
        dq_s[...] = jnp.zeros(dq_s.shape, f32)

    emb = emb_ref[...]
    near = jnp.exp(sharpness * (dot_nt(emb, qe_ref[...]) - 1.0))
    seg = column(seg_ref[...])
    weight = jnp.broadcast_to(grad_s[0:1, :], near.shape)
    for d in range(1, docs):
        weight = jnp.where(seg == d, grad_s[d : d + 1, :], weight)
    grad = (near * weight).astype(bf16)
    demb_ref[...] = dot_nn(grad, qe_ref[...])
    dq_s[...] += dot_tn(emb, grad)

    @pl.when(b == pl.num_programs(0) - 1)
    def _():
        dqe_ref[...] = jnp.transpose(dq_s[...]).astype(bf16)


def score_back(first, emb, query_emb, seg_col, chosen, positives, sums, logits, stats, query_len, query_local, docs):
    count, width = query_emb.shape
    lanes = positives.shape[1]
    length = emb.shape[0]
    blocks = length // PAIR
    whole = lambda b, *_: (0, 0)
    return pl.pallas_call(
        partial(score_back_kernel, query_len, query_local, docs),
        grid_spec=pltpu.PrefetchScalarGridSpec(
            num_scalar_prefetch=1,
            grid=(blocks,),
            in_specs=[
                pl.BlockSpec((PAIR, width), lambda b, *_: (b, 0)),
                pl.BlockSpec((count, width), whole, pipeline_mode=pl.Buffered(1)),
                pl.BlockSpec((1, PAIR), lambda b, *_: (0, b)),
                pl.BlockSpec((8, count), whole, pipeline_mode=pl.Buffered(1)),
                pl.BlockSpec((8, lanes), whole, pipeline_mode=pl.Buffered(1)),
                pl.BlockSpec((8, count), whole, pipeline_mode=pl.Buffered(1)),
                pl.BlockSpec((8, lanes), whole, pipeline_mode=pl.Buffered(1)),
                pl.BlockSpec((8, lanes), whole, pipeline_mode=pl.Buffered(1)),
            ],
            out_specs=[
                pl.BlockSpec((PAIR, width), lambda b, *_: (b, 0)),
                pl.BlockSpec((count, width), whole),
            ],
            scratch_shapes=[pltpu.VMEM((8, count), f32), pltpu.VMEM((width, count), f32)],
        ),
        out_shape=(
            jax.ShapeDtypeStruct((length, width), f32),
            jax.ShapeDtypeStruct((count, width), bf16),
        ),
        compiler_params=params(18),
        cost_estimate=cost(5),
        name="score_back",
    )(first, emb, query_emb, seg_col, chosen, positives, sums, logits, stats)


def full(*shape):
    return pl.BlockSpec(shape, lambda *_: (0,) * len(shape), pipeline_mode=pl.Buffered(1))


def kept(*shape):
    return pl.BlockSpec(shape, lambda *_: (0,) * len(shape))


def rows_of(count, width):
    return pl.BlockSpec((count, width), lambda b, *_: (b, 0))


SCALARS = pl.BlockSpec(memory_space=pltpu.SMEM)


def like(shape, dtype):
    return jax.ShapeDtypeStruct(shape, dtype)


def rms(values):
    return lax.rsqrt(jnp.mean(values * values, axis=-1, keepdims=True) + epsilon)


def choose_kernel(query_local, query_len, steps, place_ref, pos_ref, ret_ref, chosen_ref, rows_ref, ret_s):
    core, me = place_ref[0], place_ref[1]
    span = query_local * query_len
    blocks = ret_s.shape[0] // span

    def holder(p):
        return sum(((p >> s) & 1) << (steps - 1 - s) for s in range(steps))

    def held(p):
        return holder(jnp.bitwise_xor(me, p)) * 2 + core

    for p in range(blocks):
        start = pl.multiple_of(held(p) * span, span)
        ret_s[p * span : (p + 1) * span, :] = ret_ref[pl.ds(start, span), :].astype(f32)
    docs = ret_s.shape[1]
    row = lax.broadcasted_iota(jnp.int32, (docs, docs), 0)
    col = lax.broadcasted_iota(jnp.int32, (docs, docs), 1)
    shift = jnp.where(row < docs // 2, row + place_ref[2], -1)
    chosen_ref[...] = dot_nt((shift == col).astype(f32), ret_s[...])
    lane = lax.broadcasted_iota(jnp.int32, rows_ref.shape, 1)
    rows = jnp.full(rows_ref.shape, -1, jnp.int32)
    for p in range(blocks):
        for i in range(query_local):
            query = (holder(p) * 2 + core) * query_local + i
            rows = jnp.where(lane == p * query_local + i, pos_ref[query], rows)
    rows_ref[...] = rows


def choose(place, positives, retrieved, query_local, query_len, steps):
    total, docs = retrieved.shape
    lanes = -(-(total // 2 // query_len) // BLOCK) * BLOCK
    return pl.pallas_call(
        partial(choose_kernel, query_local, query_len, steps),
        in_specs=[SCALARS, SCALARS, pl.BlockSpec(memory_space=pltpu.VMEM)],
        out_shape=(like((8, total // 2), f32), like((8, lanes), jnp.int32)),
        scratch_shapes=[pltpu.VMEM((total // 2, docs), f32)],
        compiler_params=params(20),
        cost_estimate=cost(1),
        name="choose",
    )(place, positives, retrieved)


def pack_kernel(bit_ref, q_ref, k_ref, v_ref, o_ref, g_ref, u_ref, d_ref, b_ref, qkv_ref, half_qkv, half_o, half_g, half_u, half_d0, half_d1):
    inner = q_ref.shape[0]

    def half(ref, bit):
        rows = ref.shape[0] // 2
        return ref[pl.ds(pl.multiple_of(bit_ref[bit] * rows, rows), rows), :]

    for i, ref in enumerate((q_ref, k_ref, v_ref)):
        qkv_ref[:, i * inner : (i + 1) * inner] = jnp.transpose(ref[...])
    half_qkv[...] = half(qkv_ref, 0)
    rows = o_ref.shape[0] // 2
    half_o[:rows, :] = half(o_ref, 0)
    half_o[rows:, :] = jnp.zeros((half_o.shape[0] - rows, half_o.shape[1]), bf16)
    half_o[rows:, : b_ref.shape[1]] = b_ref[...]
    half_g[...] = half(g_ref, 0)
    half_u[...] = half(u_ref, 1)
    cut = half_d0.shape[1]
    half_d0[...] = half(d_ref, 0)[:, :cut]
    half_d1[...] = half(d_ref, 1)[:, cut:]


def pack(bits, q, k, v, o, gate, up, down, bias):
    inner, depth = q.shape
    hidden = gate.shape[1]
    shapes = (
        (depth, 3 * inner),
        (depth // 2, 3 * inner),
        (inner // 2 + bias.shape[0], depth),
        (depth // 2, hidden),
        (depth // 2, hidden),
        (hidden // 2, depth // 2),
        (hidden // 2, depth // 2),
    )
    weights = (q, k, v, o, gate, up, down, bias)
    return pl.pallas_call(
        pack_kernel,
        grid=(1,),
        in_specs=[SCALARS] + [kept(*w.shape) for w in weights],
        out_specs=[kept(*shape) for shape in shapes],
        out_shape=tuple(like(shape, bf16) for shape in shapes),
        compiler_params=params(60),
        cost_estimate=cost(3),
        name="pack",
    )(bits, *weights)


def enter_kernel(place_ref, kept_ref, near_ref, far_ref, cross_ref, gain_ref, w_ref, tok_ref, norm_ref, heads_ref):
    gain = gain_ref[...].astype(f32)
    mp = place_ref[0]
    shard = far_ref.shape[0]
    query = kept_ref.shape[0] - shard
    pieces = [(kept_ref, 0), (near_ref, 1), (far_ref, 2), (cross_ref, 3)]
    spans = [(ref, 0, shard, jnp.bitwise_xor(mp, i) * shard) for ref, i in pieces]
    spans += [
        (ref, shard, query, 4 * shard + jnp.bitwise_xor(mp % 2, i) * query) for ref, i in pieces[:2]
    ]
    for ref, first, count, start in spans:
        rows = pl.ds(pl.multiple_of(start, count), count)
        piece = ref[first : first + count, :]
        values = piece.astype(f32)
        normed = (values * rms(values) * gain).astype(bf16)
        tok_ref[rows, :] = piece
        norm_ref[rows, :] = normed
        heads_ref[rows, :] = dot_nn(normed, w_ref[...]).astype(bf16)


def enter(place, pieces, gain, weight):
    total = sum(piece.shape[0] for piece in pieces)
    depth, wide = weight.shape
    return pl.pallas_call(
        enter_kernel,
        in_specs=[SCALARS] + [pl.BlockSpec(memory_space=pltpu.VMEM)] * 6,
        out_shape=(like((total, depth), bf16), like((total, depth), bf16), like((total, wide), bf16)),
        compiler_params=params(12),
        cost_estimate=cost(3),
        name="enter",
    )(place, *pieces, gain, weight)


def gelu_parts(gate):
    inner = 0.7978845608028654 * (gate + 0.044715 * gate * gate * gate)
    return 0.5 * (1.0 + jnp.tanh(inner))


def ffn_own_kernel(tok_ref, near_ref, moved_ref, gain_ref, g_ref, u_ref, d_ref, mid_ref, norm_ref, gu_ref, part_ref):
    hidden = g_ref.shape[1]
    mid = tok_ref[...].astype(f32) + (near_ref[...].astype(f32) + moved_ref[...].astype(f32))
    mid_ref[...] = mid.astype(bf16)
    normed = (mid * rms(mid) * gain_ref[...].astype(f32)).astype(bf16)
    norm_ref[...] = normed
    gate = dot_nn(normed, g_ref[...])
    up = dot_nn(normed, u_ref[...])
    gu_ref[:, :hidden] = gate.astype(bf16)
    gu_ref[:, hidden:] = up.astype(bf16)
    part_ref[...] = dot_nn((gate * gelu_parts(gate) * up).astype(bf16), d_ref[...]).astype(bf16)


def ffn_own(tokens, near, moved, gain, gate, up, down, count):
    total, depth = tokens.shape
    hidden = gate.shape[1]
    return pl.pallas_call(
        ffn_own_kernel,
        grid=(total // count,),
        in_specs=[rows_of(count, depth)] * 3
        + [full(1, depth), full(depth, hidden), full(depth, hidden), full(hidden, depth)],
        out_specs=[
            rows_of(count, depth),
            rows_of(count, depth),
            rows_of(count, 2 * hidden),
            rows_of(count, depth),
        ],
        out_shape=(
            like((total, depth), bf16),
            like((total, depth), bf16),
            like((total, 2 * hidden), bf16),
            like((total, depth), bf16),
        ),
        compiler_params=params(16),
        cost_estimate=cost(5),
        name="ffn_own",
    )(tokens, near, moved, gain, gate, up, down)


def ffn_far_kernel(norm_ref, g_ref, u_ref, d_ref, part_ref, gu_ref, out_ref):
    hidden = d_ref.shape[0]
    normed = norm_ref[...]
    gate = dot_nn(normed, g_ref[...])
    up = dot_nn(normed, u_ref[...])
    gu_ref[:, :hidden] = gate.astype(bf16)
    gu_ref[:, hidden:] = up.astype(bf16)
    more = dot_nn((gate * gelu_parts(gate) * up).astype(bf16), d_ref[...])
    out_ref[...] = (part_ref[...].astype(f32) + more).astype(bf16)


def ffn_far(normed, gate, up, down, partial_sum, count):
    total, depth = normed.shape
    hidden = down.shape[0]
    return pl.pallas_call(
        ffn_far_kernel,
        grid=(total // count,),
        in_specs=[
            rows_of(count, depth),
            full(depth, hidden),
            full(depth, hidden),
            full(hidden, depth),
            rows_of(count, depth),
        ],
        out_specs=[rows_of(count, 2 * hidden), rows_of(count, depth)],
        out_shape=(like((total, 2 * hidden), bf16), like((total, depth), bf16)),
        compiler_params=params(14),
        cost_estimate=cost(5),
        name="ffn_far",
    )(normed, gate, up, down, partial_sum)


def leave_kernel(mid_ref, near_ref, moved_ref, gain_ref, w_ref, out_ref, proj_ref, emb_ref):
    out = mid_ref[...].astype(f32) + (near_ref[...].astype(f32) + moved_ref[...].astype(f32))
    out_ref[...] = out.astype(bf16)
    normed = (out * rms(out) * gain_ref[...].astype(f32)).astype(bf16)
    projected = dot_nn(normed, w_ref[...])
    proj_ref[...] = projected
    scale = lax.rsqrt(jnp.sum(projected * projected, axis=-1, keepdims=True) + epsilon)
    emb_ref[...] = (projected * scale).astype(bf16)


def leave(mid, near, moved, gain, weight, count):
    total, depth = mid.shape
    wide = weight.shape[1]
    return pl.pallas_call(
        leave_kernel,
        grid=(total // count,),
        in_specs=[rows_of(count, depth)] * 3 + [full(1, depth), full(depth, wide)],
        out_specs=[rows_of(count, depth), rows_of(count, wide), rows_of(count, wide)],
        out_shape=(like((total, depth), bf16), like((total, wide), f32), like((total, wide), bf16)),
        compiler_params=params(10),
        cost_estimate=cost(4),
        name="leave",
    )(mid, near, moved, gain, weight)


def norm_back(values, gain, gradient):
    scale = rms(values)
    weighted = gradient * gain
    average = jnp.mean(weighted * values, axis=-1, keepdims=True)
    back = scale * weighted - values * (scale * scale * scale) * average
    return back, gradient * values * scale


def leave_back_kernel(core_ref, out_ref, proj_ref, near_ref, moved_ref, qn_ref, qm_ref, gain_ref, w_ref, grad_ref, round_ref, gg_ref, emb_s, wg_ref):
    b = pl.program_id(0)

    @pl.when(b == 0)
    def _():
        wg_ref[...] = jnp.zeros(wg_ref.shape, f32)
        gg_ref[...] = jnp.zeros(gg_ref.shape, f32)
        length, half = near_ref.shape[0], qn_ref.shape[0]
        core = core_ref[0]
        emb_s[:length, :] = near_ref[...] + moved_ref[...].astype(f32)
        start = pl.multiple_of(length + core * half, half)
        emb_s[pl.ds(start, half), :] = qn_ref[...].astype(f32)
        start = pl.multiple_of(length + (1 - core) * half, half)
        emb_s[pl.ds(start, half), :] = qm_ref[...].astype(f32)

    count = out_ref.shape[0]
    projected = proj_ref[...]
    scale = lax.rsqrt(jnp.sum(projected * projected, axis=-1, keepdims=True) + epsilon)
    unit = projected * scale
    grad = emb_s[pl.ds(pl.multiple_of(b * count, count), count), :]
    grad = (scale * (grad - unit * jnp.sum(grad * unit, axis=-1, keepdims=True))).astype(bf16)
    out = out_ref[...].astype(f32)
    gain = gain_ref[...].astype(f32)
    normed = (out * rms(out) * gain).astype(bf16)
    wg_ref[...] += dot_tn(normed, grad)
    back, addends = norm_back(out, gain, dot_nt(grad, w_ref[...]))
    grad_ref[...] = back.astype(bf16)
    gg_ref[0:1, :] += jnp.sum(addends, axis=0, keepdims=True)

    @pl.when(b == pl.num_programs(0) - 1)
    def _():
        round_ref[...] = wg_ref[...].astype(bf16)


def leave_back(core, layer_out, projected, near, moved, query_near, query_moved, gain, weight, count):
    total, depth = layer_out.shape
    wide = weight.shape[1]
    return pl.pallas_call(
        leave_back_kernel,
        grid=(total // count,),
        in_specs=[
            SCALARS,
            rows_of(count, depth),
            rows_of(count, wide),
            full(*near.shape),
            full(*moved.shape),
            full(*query_near.shape),
            full(*query_moved.shape),
            full(1, depth),
            full(depth, wide),
        ],
        out_specs=[rows_of(count, depth), kept(depth, wide), kept(8, depth)],
        out_shape=(like((total, depth), bf16), like((depth, wide), bf16), like((8, depth), f32)),
        scratch_shapes=[pltpu.VMEM((total, wide), f32), pltpu.VMEM((depth, wide), f32)],
        compiler_params=params(14),
        cost_estimate=cost(5),
        name="leave_back",
    )(core, layer_out, projected, near, moved, query_near, query_moved, gain, weight)


def ffn_back_kernel(hidden, own, *refs):
    gate_s, up_s, down_s = refs[-3:]
    if own:
        index_ref, grad_ref, norm_ref, gu_ref, d_ref, g_ref, u_ref, more_ref, part_in, down_in = refs[:10]
        nf_ref, a_ref, b_ref, *downs = refs[10:-3]
    else:
        grad_ref, norm_ref, gu_ref, d_ref, g_ref, u_ref, more_ref, nf_ref, a_ref, b_ref, down_ref = refs[:-3]
    b = pl.program_id(0)

    @pl.when(b == 0)
    def _():
        gate_s[...] = jnp.zeros(gate_s.shape, f32)
        up_s[...] = jnp.zeros(up_s.shape, f32)
        down_s[...] = jnp.zeros(down_s.shape, f32)

    grad = grad_ref[...]
    gate = gu_ref[:, :hidden].astype(f32)
    up = gu_ref[:, hidden:].astype(f32)
    hidden_grad = dot_nt(grad, d_ref[...])
    half = gelu_parts(gate)
    curve = 0.7978845608028654 * (1.0 + 0.134145 * gate * gate)
    slope = half + 2.0 * gate * half * (1.0 - half) * curve
    act = gate * half
    gate_grad = (hidden_grad * up * slope).astype(bf16)
    up_grad = (hidden_grad * act).astype(bf16)
    normed = norm_ref[...]
    gate_s[...] += dot_tn(normed, gate_grad)
    up_s[...] += dot_tn(normed, up_grad)
    down_s[...] += dot_tn(grad, (act * up).astype(bf16))
    back = dot_nt(gate_grad, g_ref[...]) + dot_nt(up_grad, u_ref[...])
    nf_ref[...] = (part_in[...].astype(f32) + back if own else back).astype(bf16)

    @pl.when(b == pl.num_programs(0) - 1)
    def _():
        cut = hidden // 2
        a_ref[...] = gate_s[:, :cut].astype(bf16)
        b_ref[:, : hidden - cut] = gate_s[:, cut:].astype(bf16)
        b_ref[:, hidden - cut :] = up_s[...].astype(bf16)
        if not own:
            down_ref[...] = down_s[...].astype(bf16)
        else:
            for k, ref in enumerate(downs):
                size = ref.shape[0]
                rows = pl.ds(pl.multiple_of(jnp.bitwise_xor(index_ref[0], k) * size, size), size)
                wide = ref.shape[1] // 2
                ref[:, :hidden] = down_in[rows, :]
                ref[:, hidden:wide] = more_ref[rows, :]
                ref[:, wide : wide + hidden] = down_s[rows, :].astype(bf16)
                ref[:, wide + hidden :] = more_ref[rows, :]


def ffn_back(grad, normed, gate_up, down, gate, up, more, count, index=None, part_sum=None, far_down=None):
    total, depth = normed.shape
    hidden = down.shape[0]
    own = index is not None
    quarter = depth // 4
    downs = [(quarter, 2 * (hidden + more.shape[1]))] * 4 if own else [(depth, hidden)]
    shapes = [(depth, hidden // 2), (depth, hidden + hidden // 2)] + downs
    return pl.pallas_call(
        partial(ffn_back_kernel, hidden, own),
        grid=(total // count,),
        in_specs=([SCALARS] if own else [])
        + [
            rows_of(count, depth),
            rows_of(count, depth),
            rows_of(count, 2 * hidden),
            full(hidden, depth),
            full(depth, hidden),
            full(depth, hidden),
            full(*more.shape),
        ]
        + ([rows_of(count, depth), full(depth, hidden)] if own else []),
        out_specs=[rows_of(count, depth)] + [kept(*shape) for shape in shapes],
        out_shape=(like((total, depth), bf16),) + tuple(like(shape, bf16) for shape in shapes),
        scratch_shapes=[pltpu.VMEM((depth, hidden), f32)] * 3,
        compiler_params=params(28),
        cost_estimate=cost(10),
        name="ffn_back",
    )(*([index] if own else []), grad, normed, gate_up, down, gate, up, more, *([part_sum, far_down] if own else []))


def mid_back_kernel(near_ref, moved_ref, mid_ref, grad_ref, gain_ref, c0_ref, c1_ref, w0_ref, w1_ref, out_ref, dc0_ref, dc1_ref, ow0_ref, ow1_ref, gg_ref, o0_s, o1_s):
    b = pl.program_id(0)

    @pl.when(b == 0)
    def _():
        o0_s[...] = jnp.zeros(o0_s.shape, f32)
        o1_s[...] = jnp.zeros(o1_s.shape, f32)
        gg_ref[...] = jnp.zeros(gg_ref.shape, f32)

    gradient = near_ref[...].astype(f32) + moved_ref[...].astype(f32)
    back, addends = norm_back(mid_ref[...].astype(f32), gain_ref[...].astype(f32), gradient)
    rounded = (grad_ref[...].astype(f32) + back).astype(bf16)
    out_ref[...] = rounded
    gg_ref[0:1, :] += jnp.sum(addends, axis=0, keepdims=True)
    dc0_ref[...] = dot_nt(rounded, w0_ref[...]).astype(bf16)
    dc1_ref[...] = dot_nt(rounded, w1_ref[...]).astype(bf16)
    o0_s[...] += dot_tn(rounded, c0_ref[...])
    o1_s[...] += dot_tn(rounded, c1_ref[...])

    @pl.when(b == pl.num_programs(0) - 1)
    def _():
        ow0_ref[...] = o0_s[...].astype(bf16)
        ow1_ref[...] = o1_s[...].astype(bf16)


def mid_back(near, moved, mid, grad, gain, contexts, weights, count):
    total, depth = mid.shape
    inner = weights[0].shape[0]
    return pl.pallas_call(
        mid_back_kernel,
        grid=(total // count,),
        in_specs=[rows_of(count, depth)] * 4
        + [full(1, depth)]
        + [rows_of(count, inner)] * 2
        + [full(inner, depth)] * 2,
        out_specs=[
            rows_of(count, depth),
            rows_of(count, inner),
            rows_of(count, inner),
            kept(depth, inner),
            kept(depth, inner),
            kept(8, depth),
        ],
        out_shape=(
            like((total, depth), bf16),
            like((total, inner), bf16),
            like((total, inner), bf16),
            like((depth, inner), bf16),
            like((depth, inner), bf16),
            like((8, depth), f32),
        ),
        scratch_shapes=[pltpu.VMEM((depth, inner), f32)] * 2,
        compiler_params=params(16),
        cost_estimate=cost(6),
        name="mid_back",
    )(near, moved, mid, grad, gain, *contexts, *weights)


EXTRA = 16


def extra_rows(ref, start, final_ref, ffn_ref, attn_ref, bias_ref):
    rows = [final_ref[0:1, :], ffn_ref[0:1, :]]
    rows.append(jnp.zeros_like(rows[0]) if attn_ref is None else attn_ref[0:1, :])
    ones = jnp.ones((8, bias_ref.shape[2]), f32)
    ref[start : start + EXTRA, :] = jnp.zeros((EXTRA, ref.shape[1]), f32).astype(ref.dtype)
    for i, row in enumerate(rows):
        ref[start + i : start + i + 1, :] = row.astype(ref.dtype)
    for h in range(bias_ref.shape[0]):
        sums = lax.dot_general(
            ones,
            bias_ref[h],
            (((1,), (1,)), ((), ())),
            precision=lax.Precision.HIGHEST,
            preferred_element_type=f32,
        )
        ref[start + 3 + h : start + 4 + h, : sums.shape[1]] = sums[0:1, :].astype(ref.dtype)


def heads_far_kernel(norm_ref, grad_ref, ow_ref, final_ref, ffn_ref, bias_ref, a_ref, b_ref, all_s):
    wide = grad_ref.shape[1]
    depth = norm_ref.shape[1]
    all_s[:depth, :wide] = dot_tn(norm_ref[...], grad_ref[...])
    all_s[:depth, wide:] = ow_ref[...].astype(f32)
    extra_rows(all_s, depth, final_ref, ffn_ref, None, bias_ref)
    cut = a_ref.shape[1]
    a_ref[...] = all_s[:, :cut].astype(bf16)
    b_ref[...] = all_s[:, cut:].astype(bf16)


def heads_far(normed, grads, output_grad, final_gain, ffn_gain, bias_grad):
    total, depth = normed.shape
    wide = grads.shape[1] + output_grad.shape[1]
    cut = wide * 2 // 3 // BLOCK * BLOCK
    return pl.pallas_call(
        heads_far_kernel,
        in_specs=[pl.BlockSpec(memory_space=pltpu.VMEM)] * 6,
        out_shape=(like((depth + EXTRA, cut), bf16), like((depth + EXTRA, wide - cut), bf16)),
        scratch_shapes=[pltpu.VMEM((depth + EXTRA, wide), f32)],
        compiler_params=params(14),
        cost_estimate=cost(3),
        name="heads_far",
    )(normed, grads, output_grad, final_gain, ffn_gain, bias_grad)


def heads_own_kernel(index_ref, norm_ref, grad_ref, ow_ref, final_ref, ffn_ref, attn_ref, bias_ref, a_ref, b_ref, *refs):
    outs, all_s = refs[:4], refs[4]
    wide = grad_ref.shape[1]
    depth = norm_ref.shape[1]
    all_s[:depth, :wide] = dot_tn(norm_ref[...], grad_ref[...])
    all_s[:depth, wide:] = ow_ref[...].astype(f32)
    extra_rows(all_s, depth, final_ref, ffn_ref, attn_ref, bias_ref)
    cut = a_ref.shape[1]
    all_s[:, :cut] += a_ref[...].astype(f32)
    all_s[:, cut:] += b_ref[...].astype(f32)
    count = depth // 4
    for k, ref in enumerate(outs):
        start = pl.multiple_of(jnp.bitwise_xor(index_ref[0], k) * count, count)
        ref[:count, :] = all_s[pl.ds(start, count), :].astype(bf16)
        ref[count:, :] = all_s[depth:, :].astype(bf16)


def heads_own(index, normed, grads, output_grad, final_gain, ffn_gain, attn_gain, bias_grad, moved, more):
    total, depth = normed.shape
    wide = moved.shape[1] + more.shape[1]
    return pl.pallas_call(
        heads_own_kernel,
        in_specs=[SCALARS] + [pl.BlockSpec(memory_space=pltpu.VMEM)] * 9,
        out_shape=(like((depth // 4 + EXTRA, wide), bf16),) * 4,
        scratch_shapes=[pltpu.VMEM((depth + EXTRA, wide), f32)],
        compiler_params=params(16),
        cost_estimate=cost(3),
        name="heads_own",
    )(index, normed, grads, output_grad, final_gain, ffn_gain, attn_gain, bias_grad, moved, more)


def quarter_kernel(index_ref, near_ref, moved_ref, *outs):
    for k, ref in enumerate(outs):
        count = ref.shape[0]
        rows = pl.ds(pl.multiple_of(jnp.bitwise_xor(index_ref[0], k) * count, count), count)
        ref[...] = (near_ref[rows, :].astype(f32) + moved_ref[rows, :].astype(f32)).astype(bf16)


def quarter_sums(index, near, moved):
    depth, wide = near.shape
    return pl.pallas_call(
        quarter_kernel,
        in_specs=[SCALARS] + [pl.BlockSpec(memory_space=pltpu.VMEM)] * 2,
        out_shape=(like((depth // 4, wide), bf16),) * 4,
        compiler_params=params(8),
        cost_estimate=cost(1),
        name="quarter_sums",
    )(index, near, moved)


def enter_back_kernel(place_ref, tok_ref, own_ref, far_ref, w0_ref, w1_ref, kept_ref, sent_ref, gg_ref, na_s):
    core = place_ref[0] % 2
    total = tok_ref.shape[0]
    own_half = kept_ref.shape[0]
    gg_ref[...] = jnp.zeros(gg_ref.shape, f32)
    count = total // 3
    for i in range(3):
        rows = slice(i * count, (i + 1) * count)
        grad = dot_nt(own_ref[rows, :], w0_ref[...]) + dot_nt(far_ref[rows, :], w1_ref[...])
        values = tok_ref[rows, :].astype(f32)
        gg_ref[0:1, :] += jnp.sum(grad * values * rms(values), axis=0, keepdims=True)
        na_s[rows, :] = grad.astype(bf16)
    shard, query = split_of(total, own_half)
    for ref, which in ((kept_ref, core), (sent_ref, 1 - core)):
        for i in range(2):
            start = pl.multiple_of((which + 2 * i) * shard, shard)
            ref[i * shard : (i + 1) * shard, :] = na_s[pl.ds(start, shard), :]
        start = pl.multiple_of(4 * shard + which * query, query)
        ref[2 * shard :, :] = na_s[pl.ds(start, query), :]


def widen_kernel(groups, cuts, index_ref, *refs):
    outs = refs[4 * groups : 4 * groups + len(cuts)]
    scratch = list(refs[4 * groups + len(cuts) :])
    for (sources, turned), out in zip(cuts, outs):
        target = scratch.pop(0) if turned else out
        at = 0
        for group, first, last in sources:
            for k, ref in enumerate(refs[4 * group : 4 * group + 4]):
                count = target.shape[0] // 4
                rows = pl.ds(pl.multiple_of(jnp.bitwise_xor(index_ref[0], k) * count, count), count)
                target[rows, at : at + last - first] = ref[:count, first:last].astype(f32)
            at += last - first
        if turned:
            out[...] = jnp.transpose(target[...])


def widened(index, depth, groups, cuts, name):
    widths = [sum(last - first for _, first, last in sources) for sources, _ in cuts]
    return pl.pallas_call(
        partial(widen_kernel, len(groups), cuts),
        in_specs=[SCALARS] + [pl.BlockSpec(memory_space=pltpu.VMEM)] * (4 * len(groups)),
        out_shape=tuple(
            like((wide, depth) if turned else (depth, wide), f32) for wide, (_, turned) in zip(widths, cuts)
        ),
        scratch_shapes=[pltpu.VMEM((depth, wide), f32) for wide, (_, turned) in zip(widths, cuts) if turned],
        compiler_params=params(20),
        cost_estimate=cost(3),
        name=name,
    )(index, *[piece for group in groups for piece in group])


def split_of(total, half):
    query = half - (half // BLOCK) * BLOCK
    return (half - query) // 2, query


def enter_back(place, tokens, own, far, weights):
    total, depth = tokens.shape
    return pl.pallas_call(
        enter_back_kernel,
        in_specs=[SCALARS] + [pl.BlockSpec(memory_space=pltpu.VMEM)] * 5,
        out_shape=(like((total // 2, depth), bf16),) * 2 + (like((8, depth), f32),),
        scratch_shapes=[pltpu.VMEM((total, depth), bf16)],
        compiler_params=params(16),
        cost_estimate=cost(4),
        name="enter_back",
    )(place, tokens, own, far, *weights)


def inputs_back_kernel(place_ref, tok_ref, mid_ref, near_ref, moved_ref, gain_ref, stay_ref, leave_ref, query_ref):
    core, x = place_ref[0] % 2, place_ref[0] // 2
    total = tok_ref.shape[0]
    shard, query = split_of(total, near_ref.shape[0])
    gain = gain_ref[...].astype(f32)

    def piece(start, at, count):
        rows = pl.ds(pl.multiple_of(start, count), count)
        at = pl.ds(pl.multiple_of(at, count), count)
        gradient = near_ref[at, :].astype(f32) + moved_ref[at, :].astype(f32)
        back, _ = norm_back(tok_ref[rows, :].astype(f32), gain, gradient)
        return mid_ref[rows, :].astype(f32) + back

    leave_ref[...] = piece((core + 2 * (1 - x)) * shard, (1 - x) * shard, shard).astype(bf16)
    stay_ref[...] = piece((core + 2 * x) * shard, x * shard, shard)
    query_ref[...] = piece(4 * shard + core * query, 2 * shard, query)


def inputs_back(place, tokens, mid_grad, near, moved, gain):
    total, depth = tokens.shape
    shard, query = split_of(total, near.shape[0])
    return pl.pallas_call(
        inputs_back_kernel,
        in_specs=[SCALARS] + [pl.BlockSpec(memory_space=pltpu.VMEM)] * 5,
        out_shape=(like((shard, depth), f32), like((shard, depth), bf16), like((query, depth), f32)),
        compiler_params=params(12),
        cost_estimate=cost(2),
        name="inputs_back",
    )(place, tokens, mid_grad, near, moved, gain)


def swapped(bit, mine, theirs, axis=0):
    first = jnp.where(bit == 0, mine, theirs)
    second = jnp.where(bit == 0, theirs, mine)
    return jnp.concatenate([first, second], axis=axis)


def after(values, *earlier):
    return lax.optimization_barrier((values,) + earlier)[0]


def part(values, index, parts, axis=0):
    size = values.shape[axis] // parts
    return lax.dynamic_slice_in_dim(values, index * size, size, axis)


def shards(
    doc_tokens,
    query_tokens,
    doc_segments,
    query_keep,
    retrieved,
    positives,
    attn_gain,
    query_weight,
    key_weight,
    value_weight,
    output_weight,
    position_bias,
    ffn_gain,
    gate_weight,
    up_weight,
    down_weight,
    final_gain,
    proj_weight,
):
    groups = lax.axis_size("dp")
    tensor_size = lax.axis_size("mp")
    bits = groups.bit_length() - 1
    dp = lax.axis_index("dp")
    mp = lax.axis_index("mp")
    x = mp // 2
    core = mp % 2
    row_count, shard_len, width = doc_tokens.shape
    length = shard_len * tensor_size
    query_local, query_len, _ = query_tokens.shape
    chip_queries = query_local * 2
    buckets = position_bias.shape[0]
    hidden_local = gate_weight.shape[1]
    doc_local = retrieved.shape[2]
    docs_row = doc_local // row_count
    query_total = query_keep.shape[0]
    vector_width = proj_weight.shape[1]
    inner = query_weight.shape[1]

    def over(axis, size, mask):
        pairs = [(i, i ^ mask) for i in range(size)]
        return lambda values: lax.ppermute(values, axis, pairs)

    to_x = over("mp", tensor_size, 2)
    to_core = over("mp", tensor_size, 1)
    to_dp = [over("dp", groups, 1 << b) for b in range(bits)]
    dp_bit = [(dp >> b) & 1 for b in range(bits)]

    def exchange(steps):
        dp_mask = sum(1 << b for axis, b in steps if axis == "dp")
        mp_mask = 2 if any(axis == "x" for axis, b in steps) else 0
        pairs = [
            (i, ((i // tensor_size) ^ dp_mask) * tensor_size + ((i % tensor_size) ^ mp_mask))
            for i in range(groups * tensor_size)
        ]
        return lambda values: lax.ppermute(values, ("dp", "mp"), pairs)

    def rounds(order):
        out = []
        for i in range(0, len(order), 2):
            steps = order[i : i + 2]
            if len(steps) == 1:
                out.append([exchange(steps)])
            else:
                out.append([exchange(steps[:1]), exchange(steps[1:]), exchange(steps)])
        return out

    kept_rows = lax.dynamic_index_in_dim(doc_tokens, x, 0, keepdims=False)
    sent_rows = lax.dynamic_index_in_dim(doc_tokens, 1 - x, 0, keepdims=False)
    far_rows = to_x(sent_rows)
    kept_tokens = jnp.concatenate(
        [kept_rows, query_tokens.reshape(query_local * query_len, width)], axis=0
    )
    near_tokens = to_core(kept_tokens)
    cross_rows = to_core(far_rows)

    own_qkv, qkv_half, output_half, gate_half, up_half, *down_halves = pack(
        jnp.stack(dp_bit[:2]),
        jnp.transpose(after(query_weight, sent_rows)),
        jnp.transpose(key_weight),
        jnp.transpose(value_weight),
        output_weight,
        gate_weight,
        up_weight,
        down_weight,
        position_bias,
    )
    near_tiles = bias_tiles(after(position_bias.astype(f32), qkv_half))
    qkv_half = to_x(qkv_half)
    output_half = to_x(output_half)
    far_bias = output_half[inner // 2 :, : position_bias.shape[1]]
    output_half = output_half[: inner // 2]

    def other_half(got, b=0, earlier=()):
        return swapped(dp_bit[b], got, after(to_dp[b](got), earlier))


    row_segments = lax.dynamic_index_in_dim(doc_segments, x, 0, keepdims=False)
    chip_keep = lax.dynamic_slice_in_dim(
        query_keep, (dp * tensor_size + x * 2) * query_local, chip_queries, 0
    ).reshape(-1)
    query_ids = jnp.arange(chip_queries * query_len, dtype=jnp.int32) // query_len + docs_row
    seg_q = jnp.concatenate([row_segments, query_ids])
    seg_k = jnp.concatenate([row_segments, jnp.where(chip_keep > 0, query_ids, -1)])
    blocked = row_segments.reshape(-1, PAIR)
    low = jnp.sum((row_segments[None, :] < blocked[:, :1]).astype(jnp.int32), axis=1)
    high = jnp.sum((row_segments[None, :] <= blocked[:, -1:]).astype(jnp.int32), axis=1)
    low_block = low // BLOCK
    high_block = (high + BLOCK - 1) // BLOCK
    lo = jnp.concatenate([low_block, jnp.full((1,), length // BLOCK - 1, jnp.int32)])
    cnt = jnp.concatenate([(high_block - low_block + 1) // 2, jnp.ones((1,), jnp.int32)])
    ranges = (lo, cnt)

    order = [("dp", b) for b in reversed(range(bits))] + [("x", 0)]
    place = sum((x if axis == "x" else dp_bit[b]) << s for s, (axis, b) in enumerate(order))
    kept_retrieved = (query_keep[:, :, None] * retrieved).reshape(query_total * query_len, doc_local)
    seg_q, seg_k = seg_q[None, :], seg_k[None, :]
    segs = (seg_q, seg_k)
    half_queries = query_total // 2
    query_lanes = -(-half_queries // BLOCK) * BLOCK

    place_mp = mp.reshape(1)
    gain_attn, gain_ffn, gain_final = [g.reshape(1, width) for g in (attn_gain, ffn_gain, final_gain)]
    pieces = (kept_tokens, near_tokens, far_rows, cross_rows)
    tokens, normed_attn, own_heads = enter(place_mp, pieces, gain_attn, own_qkv)
    far_tiles = bias_tiles(after(far_bias.astype(f32), own_heads))
    qkv_half = after(qkv_half, far_tiles)
    gate_half = to_x(after(gate_half, own_heads))
    own_context, own_log = attend(own_heads, ranges, segs, near_tiles[0])
    far_qkv = other_half(qkv_half, 0, own_context)
    gate_half = after(gate_half, own_context)
    up_half = to_x(after(up_half, own_context))
    far_heads = dot_nn(normed_attn, after(far_qkv, gate_half)).astype(bf16)
    far_context, far_log = attend(far_heads, ranges, segs, far_tiles[0])
    far_output = other_half(after(output_half, far_qkv), 0, far_context)
    far_gate = other_half(after(gate_half, far_qkv), 0, far_context)
    up_half = after(up_half, far_context)
    down_halves = [to_x(after(half, far_context)) for half in down_halves]
    tiles = (near_tiles, far_tiles)
    heads = (own_heads, far_heads)
    contexts = (own_context, far_context)
    logs = (own_log, far_log)
    qkv_weights = (own_qkv, far_qkv)
    output_weights = (output_weight, far_output)
    attn_part = sum(
        dot_nn(c, w) for c, w in zip(after(contexts, far_gate, up_half), output_weights)
    ).astype(bf16)
    chosen, pos_rows = choose(
        jnp.stack([core, place, x * docs_row]),
        positives,
        after(kept_retrieved, attn_part),
        query_local,
        query_len,
        bits + 1,
    )
    count = tokens.shape[0] // 3
    mid, normed_ffn, own_gate_up, ffn_sum = ffn_own(
        tokens, attn_part, to_core(attn_part), gain_ffn, gate_weight, up_weight, down_weight, count
    )
    far_up = other_half(after(up_half, attn_part), 1, ffn_sum)
    down_halves = after(down_halves, ffn_sum)
    far_down = jnp.concatenate([other_half(half, b) for b, half in enumerate(down_halves)], axis=1)
    far_gate_up_out, ffn_part = ffn_far(normed_ffn, far_gate, far_up, far_down, ffn_sum, count)
    layer_out, projected, embedded = leave(
        mid, ffn_part, to_core(ffn_part), gain_final, proj_weight, count
    )

    doc_embedded = embedded[:length]
    query_emb = part(embedded[length:], core, 2)
    for moves in rounds(order):
        query_emb = jnp.concatenate([query_emb] + [move(query_emb) for move in moves], axis=0)
    first_doc = jnp.stack([dp * doc_local + x * docs_row, place])
    seg_col = seg_q[:, :length]
    sums, logits, stats = score(
        first_doc, doc_embedded, query_emb, seg_col, chosen, pos_rows, query_len, query_local, docs_row
    )
    for moves in rounds(order[::-1]):
        every = [stats] + [move(stats) for move in moves]
        top = every[0][0:1]
        for moved in every[1:]:
            top = jnp.maximum(top, moved[0:1])
        total = sum(moved[1:2] * jnp.exp(moved[0:1] - top) for moved in every)
        stats = jnp.concatenate([top, total, sum(moved[2:] for moved in every)], axis=0)
    valid = jnp.arange(query_lanes) < half_queries
    loss_sum = jnp.sum(jnp.where(valid, stats[0] + jnp.log(stats[1]) - stats[2], 0.0))
    found_sum = jnp.sum(jnp.where(valid & (stats[3] > 0.5), 1.0, 0.0))
    ends = jnp.broadcast_to(jnp.stack([loss_sum, found_sum])[:, None], (2, BLOCK))
    ends = (ends + to_core(ends)) / query_total
    loss_value = ends[0, 0]
    found_share = ends[1, 0]

    demb, dqe = score_back(
        first_doc,
        doc_embedded,
        query_emb,
        seg_col,
        chosen,
        pos_rows,
        sums,
        logits,
        stats,
        query_len,
        query_local,
        docs_row,
    )
    demb_moved = to_core(demb.astype(bf16))
    for moves in reversed(rounds(order)):
        pieces = jnp.split(dqe, len(moves) + 1, axis=0)
        moved = [move(piece).astype(f32) for move, piece in zip(moves, pieces[1:])]
        dqe = sum(moved, pieces[0].astype(f32)).astype(bf16)
    dqe_moved = to_core(dqe)

    def widen(values):
        return values.astype(f32)

    def narrow(values):
        return values.astype(bf16)

    def added(*values):
        return narrow(sum(widen(v) for v in values[1:]) + widen(values[0]))

    four = [exchange([("dp", 0)]), exchange([("dp", 1)]), exchange([("dp", 0), ("dp", 1)])]
    four_index = (dp % 4).reshape(1)
    rest = range(2, bits)

    def scattered(pieces):
        return (pieces[0],) + tuple(move(piece) for move, piece in zip(four, pieces[1:]))

    def rest_of(values, moved):
        values = added(values, moved)
        for b in rest[1:]:
            values = added(values, to_dp[b](values))
        return values

    def gathered(values):
        return (values,) + tuple(move(values) for move in four)

    def assembled(pieces):
        low = [jnp.where(dp_bit[0] == 0, pieces[0], pieces[1]), jnp.where(dp_bit[0] == 0, pieces[1], pieces[0])]
        high = [jnp.where(dp_bit[0] == 0, pieces[2], pieces[3]), jnp.where(dp_bit[0] == 0, pieces[3], pieces[2])]
        return jnp.concatenate(
            [jnp.where(dp_bit[1] == 0, u, v) for u, v in zip(low + high, high + low)], axis=0
        )

    layer_out_grad, proj_grad, final_gain_part = leave_back(
        core.reshape(1), layer_out, projected, demb, demb_moved, dqe, dqe_moved, gain_final, proj_weight, count
    )
    nf_sum, far_first, far_rest, far_down_grad = ffn_back(
        layer_out_grad, normed_ffn, far_gate_up_out, far_down, far_gate, far_up, proj_grad, count
    )
    first_moved = to_x(far_first)
    nf_part, own_first, own_rest, *down_pieces = ffn_back(
        after(layer_out_grad, far_first),
        normed_ffn,
        own_gate_up,
        down_weight,
        gate_weight,
        up_weight,
        proj_grad,
        count,
        four_index,
        nf_sum,
        far_down_grad,
    )
    first_pieces = quarter_sums(four_index, own_first, after(first_moved, nf_part))
    first_moves = scattered(first_pieces)
    rest_moved = to_x(after(far_rest, first_pieces))
    down_moves = scattered(tuple(down_pieces))
    nf_part = after(nf_part, first_pieces)
    mid_grad, own_context_grad, far_context_grad, own_out, far_out, ffn_gain_part = mid_back(
        nf_part, to_core(nf_part), mid, layer_out_grad, gain_ffn, contexts, output_weights, count
    )

    far_grads, far_bias_grad = attend_back(
        far_heads,
        far_context_grad,
        far_context,
        far_log,
        ranges,
        segs,
        far_tiles[1],
        buckets,
    )
    down = added(*after(down_moves, far_grads, rest_moved))
    down_wide = hidden_local + vector_width
    down_kept, down_moved = down[:, down_wide:], to_x(down[:, :down_wide])
    far_all, far_more = heads_far(normed_attn, after(far_grads, down), far_out, final_gain_part, ffn_gain_part, far_bias_grad)

    down = added(after(down_moved, far_all), down_kept)
    all_moved = to_x(after(far_all, down))
    first = added(*after(first_moves, far_all))
    rest_pieces = quarter_sums(four_index, own_rest, after(rest_moved, far_all))
    rest_moves = scattered(rest_pieces)
    early = jnp.concatenate([first, down], axis=1)
    early_moved = to_dp[rest[0]](early)
    own_grads, own_bias_grad = attend_back(
        own_heads,
        after(own_context_grad, rest_pieces, early),
        own_context,
        own_log,
        ranges,
        segs,
        near_tiles[1],
        buckets,
    )

    early = rest_of(early, after(early_moved, own_grads))
    early_all = gathered(early)
    others = added(*after(rest_moves, own_grads))
    others_moved = to_dp[rest[0]](others)
    all_moved = after(all_moved, own_grads)
    more_moved = to_x(after(far_more, all_moved))
    na_kept, na_sent, attn_gain_part = enter_back(
        place_mp, tokens, after(own_grads, others, early, all_moved), far_grads, qkv_weights
    )
    early_all = after(early_all, na_sent)
    all_pieces = heads_own(
        four_index,
        normed_attn,
        own_grads,
        own_out,
        final_gain_part,
        ffn_gain_part,
        attn_gain_part,
        own_bias_grad,
        all_moved,
        after(more_moved, na_sent, early_all),
    )
    all_moves = scattered(all_pieces)
    others = rest_of(others, after(others_moved, all_pieces))

    both = added(*after(all_moves, others))
    both_moved = to_dp[rest[0]](both)
    others_all = gathered(after(others, both))
    na_moved = to_core(after(na_sent, both))

    stay, leaving, query_grad = inputs_back(place_mp, tokens, mid_grad, na_kept, na_moved, gain_attn)
    both = rest_of(both, after(both_moved, others_all, leaving))
    both_all = gathered(both)
    back = to_x(after(leaving, both))
    extra = both[width // 4 :]
    crossing = [(i, i ^ 3) for i in range(tensor_size)]
    extra_moves = (to_x(extra), to_core(extra), lax.ppermute(extra, "mp", crossing))
    cut = hidden_local // 2
    gate_weight_grad, up_weight_grad, down_weight_grad, proj_weight_grad = widened(
        four_index,
        width,
        after((early_all, others_all), extra_moves),
        (
            (((0, 0, cut), (1, 0, cut)), False),
            (((1, cut, cut + hidden_local),), False),
            (((0, cut, cut + hidden_local),), True),
            (((0, cut + hidden_local, cut + down_wide),), False),
        ),
        "widen_ffn",
    )
    extra_moves, back = after((extra_moves, back), up_weight_grad)
    extra = widen(extra)
    attn_gain_grad = extra[2] + sum(widen(moved[2]) for moved in extra_moves)
    position_bias_grad = jnp.transpose(extra[3 : 3 + position_bias.shape[1], :buckets])
    back = widen(back)
    doc_grad = jnp.stack([jnp.where(x == 0, stay, back), jnp.where(x == 0, back, stay)], axis=0)

    query_weight_grad, key_weight_grad, value_weight_grad, output_weight_grad = widened(
        four_index,
        width,
        (after(both_all, doc_grad, attn_gain_grad),),
        tuple((((0, i * inner, (i + 1) * inner),), True) for i in range(4)),
        "widen_heads",
    )

    return (
        loss_value,
        found_share,
        doc_grad,
        query_grad.reshape(query_local, query_len, width),
        attn_gain_grad,
        jnp.transpose(query_weight_grad),
        jnp.transpose(key_weight_grad),
        jnp.transpose(value_weight_grad),
        output_weight_grad,
        position_bias_grad,
        extra[1],
        gate_weight_grad,
        up_weight_grad,
        down_weight_grad,
        extra[0],
        proj_weight_grad,
    )


def solution(mesh):
    placed = (
        P("dp", "mp", None),
        P(("dp", "mp"), None, None),
        P("dp", None),
        P(),
        P(None, None, "dp"),
        P(),
        P(),
        P(None, "mp"),
        P(None, "mp"),
        P(None, "mp"),
        P("mp", None),
        P(None, "mp"),
        P(),
        P(None, "mp"),
        P(None, "mp"),
        P("mp", None),
        P(),
        P(),
    )
    return jax.shard_map(
        shards,
        mesh=mesh,
        in_specs=placed,
        out_specs=(
            P(),
            P(),
            P("dp", "mp", None),
            P(("dp", "mp"), None, None),
            P(),
            P(None, "mp"),
            P(None, "mp"),
            P(None, "mp"),
            P("mp", None),
            P(None, "mp"),
            P(),
            P(None, "mp"),
            P(None, "mp"),
            P("mp", None),
            P(),
            P(),
        ),
        check_vma=False,
    )
```
